32 devices in a mesh: dp: 8 (over z, y), tensor: 4 (over x, core).
Axes of the slice: x: 2, y: 2, z: 4, core: 2. Of those that a mesh axis runs over, the one named last changes fastest.
Arguments:
- tokens: bfloat16 [16384, 768], P(('dp', 'tensor')), may hold values from -6 to 6
- cotangent: bfloat16 [16384, 768], P(('dp', 'tensor')), may hold values from -6 to 6
- segment_ids: int32 [8, 2048], P('dp'), may hold values from 0 to 7, never falling along the last dimension, each value on 1 to 512 neighbouring positions
- ln1_gain: bfloat16 [768], P('dp'), may hold values from 0.5 to 1.5
- ln1_bias: bfloat16 [768], P('dp'), may hold values from -3 to 3
- w_query: bfloat16 [768, 768], P('dp', 'tensor'), may hold values from -0.3125 to 0.3125
- query_bias: bfloat16 [768], P('dp'), may hold values from -3 to 3
- w_key: bfloat16 [768, 768], P('dp', 'tensor'), may hold values from -0.3125 to 0.3125
- w_value: bfloat16 [768, 768], P('dp', 'tensor'), may hold values from -0.21875 to 0.21875
- value_bias: bfloat16 [768], P('dp'), may hold values from -3 to 3
- w_out: bfloat16 [768, 768], P('tensor', 'dp'), may hold values from -0.625 to 0.625
- out_bias: bfloat16 [768], P('dp'), may hold values from -3 to 3
- ln2_gain: bfloat16 [768], P('dp'), may hold values from 0.5 to 1.5
- ln2_bias: bfloat16 [768], P('dp'), may hold values from -3 to 3
- w_in: bfloat16 [768, 3072], P('dp', 'tensor'), may hold values from -0.21875 to 0.21875
- in_bias: bfloat16 [3072], P('dp'), may hold values from -3 to 3
- w_back: bfloat16 [3072, 768], P('tensor', 'dp'), may hold values from -0.15625 to 0.15625
- back_bias: bfloat16 [768], P('dp'), may hold values from -3 to 3
Outputs:
- output: bfloat16 [16384, 768], P(('dp', 'tensor'))
- grad_tokens: float32 [16384, 768], P(('dp', 'tensor'))
- grad_ln1_gain: float32 [768], P('dp')
- grad_ln1_bias: float32 [768], P('dp')
- grad_w_query: float32 [768, 768], P('dp', 'tensor')
- grad_query_bias: float32 [768], P('dp')
- grad_w_key: float32 [768, 768], P('dp', 'tensor')
- grad_w_value: float32 [768, 768], P('dp', 'tensor')
- grad_value_bias: float32 [768], P('dp')
- grad_w_out: float32 [768, 768], P('tensor', 'dp')
- grad_out_bias: float32 [768], P('dp')
- grad_ln2_gain: float32 [768], P('dp')
- grad_ln2_bias: float32 [768], P('dp')
- grad_w_in: float32 [768, 3072], P('dp', 'tensor')
- grad_in_bias: float32 [3072], P('dp')
- grad_w_back: float32 [3072, 768], P('tensor', 'dp')
- grad_back_bias: float32 [768], P('dp')
The draws below stay inside these ranges and needn't reach their ends.
Inputs may be any that keep to these rules, and one draw needn't show every extreme that they name: `segment_ids`: in each sequence the document numbers never fall; every number 0 to 7 appears, on 1 to 512 consecutive patches, and some document has exactly 512.
All inputs are finite; a program needn't handle non-finite values.
Results may differ from the reference program's by a relative error of at most 0.02.
Values may be sent and summed in bfloat16 or wider, within the bound.
A program may use at most 128 MiB of HBM per device.

```python
import math
from functools import partial
import jax
import jax.numpy as jnp
import numpy as np
from jax import lax

D = 768
HEADS = 12
HEAD_DIM = 64
FF = 3072
SEQ_LEN = 2048
SEG_COUNT = 8
DOC_MOST = 512
SEQS = 8
TOKENS = 16384
N_TENSOR = 4


def level_of(own_key, extent, pieces, least, high):
    def one(dim, blocks):
        draws = jax.random.uniform(jax.random.fold_in(jax.random.fold_in(own_key, 6), dim), (blocks,), jnp.float32, least / len(pieces), high / len(pieces))
        return jnp.repeat(jnp.exp(draws), extent[dim] // blocks).reshape((-1,) + (1,) * (len(extent) - dim - 1))

    loudness = one(*pieces[0])
    for cut in pieces[1:]:
        loudness = loudness * one(*cut)
    return loudness


def length_profile(count, total, bound, skew):
    weights = [(1 << 20) // math.isqrt(grade ** skew) + 1 for grade in range(2, count + 1)]
    spare, holding = total - bound - (count - 1), [1] * (count - 1)
    while spare > 0:
        candidates = [i for i in range(count - 1) if holding[i] < bound]
        whole, budget = sum([weights[i] for i in candidates]), spare
        for i in candidates:
            addition = min(bound - holding[i], max(1, budget * weights[i] // whole), spare)
            holding[i] = holding[i] + addition
            spare = spare - addition
    return np.array([bound] + holding)


def uneven(rng, amount, total, limit, skew):
    if amount == 2:
        one = jax.random.randint(rng, (), max(1, total - limit), min(limit, total - 1) + 1)
        return jnp.stack([one, total - one])
    lengths = jnp.asarray(length_profile(amount, total, limit, skew), jnp.int32)
    twos = (amount - 1) // 2
    giver, taker = lengths[1:1 + 2 * twos:2], lengths[2:2 + 2 * twos:2]
    room = jnp.minimum(giver - 1, limit - taker)
    shifted = jax.random.randint(jax.random.fold_in(rng, 1), (twos,), 0, 1 << 20) % (room + 1)
    lengths = lengths.at[1:1 + 2 * twos:2].set(giver - shifted).at[2:2 + 2 * twos:2].set(taker + shifted)
    return lengths[jax.random.permutation(jax.random.fold_in(rng, 2), amount)]


def gaussian(key, shape, scale, limit, cuts=(), kind=jnp.bfloat16):
    drawn = jax.random.normal(key, shape, jnp.float32) * scale
    if len(cuts) > 0:
        drawn = level_of(key, shape, cuts, -0.22, 0.18) * drawn
    return jnp.clip(drawn, min=-limit, max=limit).astype(kind)


def setup_inputs(seed: int = 0) -> dict:
    seeds = jax.random.split(jax.random.key(seed), 19)
    tokens = gaussian(seeds[0], (TOKENS, D), 1.0, 6.0, ((0, 32),))
    cotangent = gaussian(seeds[1], (TOKENS, D), 1.0, 6.0, ((0, 32),))
    segment_ids = jax.vmap(lambda own: jnp.searchsorted(jnp.cumsum(uneven(own, SEG_COUNT, SEQ_LEN, DOC_MOST, 2)), jnp.arange(SEQ_LEN), side="right"))(jax.random.split(seeds[2], SEQS)).reshape((SEQS, SEQ_LEN)).astype(jnp.int32)
    ln1_gain = jnp.clip(1.0 + 0.1 * jax.random.normal(seeds[3], (D,), jnp.float32), 0.5, 1.5).astype(jnp.bfloat16)
    ln1_bias = gaussian(seeds[4], (D,), 0.5, 3.0, ((0, 8),))
    w_query = gaussian(seeds[5], (D, D), (D // 2) ** -0.5, 0.3125, ((0, 8), (1, 4)))
    query_bias = gaussian(seeds[6], (D,), 0.5, 3.0, ((0, 8),))
    w_key = gaussian(seeds[7], (D, D), (D // 2) ** -0.5, 0.3125, ((0, 8), (1, 4)))
    w_value = gaussian(seeds[8], (D, D), D ** -0.5, 0.21875, ((0, 8), (1, 4)))
    value_bias = gaussian(seeds[9], (D,), 0.5, 3.0, ((0, 8),))
    w_out = gaussian(seeds[10], (D, D), (D // 8) ** -0.5, 0.625, ((0, 4), (1, 8)))
    out_bias = gaussian(seeds[11], (D,), 0.5, 3.0, ((0, 8),))
    ln2_gain = jnp.clip(1.0 + 0.1 * jax.random.normal(seeds[12], (D,), jnp.float32), 0.5, 1.5).astype(jnp.bfloat16)
    ln2_bias = gaussian(seeds[13], (D,), 0.5, 3.0, ((0, 8),))
    w_in = gaussian(seeds[14], (D, FF), D ** -0.5, 0.21875, ((0, 8), (1, 4)))
    in_bias = gaussian(seeds[15], (FF,), 0.5, 3.0, ((0, 8),))
    w_back = gaussian(seeds[16], (FF, D), (FF // 2) ** -0.5, 0.15625, ((0, 4), (1, 8)))
    back_bias = gaussian(seeds[17], (D,), 0.5, 3.0, ((0, 8),))
    return dict(tokens=tokens, cotangent=cotangent, segment_ids=segment_ids, ln1_gain=ln1_gain, ln1_bias=ln1_bias, w_query=w_query, query_bias=query_bias, w_key=w_key, w_value=w_value, value_bias=value_bias, w_out=w_out, out_bias=out_bias, ln2_gain=ln2_gain, ln2_bias=ln2_bias, w_in=w_in, in_bias=in_bias, w_back=w_back, back_bias=back_bias)


@jax.custom_vjp
def low(v):
    return lax.optimization_barrier(v.astype(jnp.bfloat16)).astype(jnp.float32)

@jax.custom_vjp
def low_back(v):
    return v

def low_keep(v):
    return (low(v), None)

def low_pass(kept, grad):
    return (grad,)

def back_keep(v):
    return (v, None)

def back_low(kept, grad):
    return (low(grad),)
low.defvjp(low_keep, low_pass)
low_back.defvjp(back_keep, back_low)
EPSILON = 1e-12
HIGHEST = lax.Precision.HIGHEST

def layer_norm(values, gain, shift):
    center = values - lax.optimization_barrier(jnp.mean(values, axis=-1, keepdims=True))
    spread = lax.optimization_barrier(jnp.mean(center * center, axis=-1, keepdims=True))
    return center * lax.rsqrt(spread + EPSILON) * gain + shift

def grouped_product(left, right):
    group_width = left.shape[1] // N_TENSOR
    total = low(jnp.dot(left[:, :group_width], right[:group_width], precision=HIGHEST))
    for member in range(1, N_TENSOR):
        begin = member * group_width
        total = total + low(jnp.dot(left[:, begin:begin + group_width], right[begin:begin + group_width], precision=HIGHEST))
    return total

def head_attend(triple, same):
    query, keys, values = triple
    raw = jnp.einsum('qd,kd->qk', query, keys, precision=HIGHEST)
    scores = jnp.where(same, low_back(raw) * HEAD_DIM ** (-0.5), -1000000000.0)
    top = lax.optimization_barrier(jnp.max(scores, axis=-1, keepdims=True))
    expo = jnp.exp(scores - top)
    probs = expo / lax.optimization_barrier(jnp.sum(expo, axis=-1, keepdims=True))
    weights = low(probs)
    return jnp.einsum('qk,kd->qd', weights, values, precision=HIGHEST)

def split_heads(matrix):
    return matrix.reshape(matrix.shape[0], HEADS, HEAD_DIM).transpose(1, 0, 2)

def layer(inputs, segments, params):
    ln1_gain, ln1_bias, w_query, query_bias, w_key, w_value, value_bias, w_out, out_bias, ln2_gain, ln2_bias, w_in, in_bias, w_back, back_bias = params
    act_one = low(layer_norm(inputs, ln1_gain, ln1_bias))
    query = low(low_back(jnp.dot(act_one, w_query, precision=HIGHEST)) + query_bias)
    keys = low(low_back(jnp.dot(act_one, w_key, precision=HIGHEST)))
    values = low(low_back(jnp.dot(act_one, w_value, precision=HIGHEST)) + value_bias)
    same = segments[:, None] == segments[None, :]
    attend = jax.checkpoint(partial(head_attend, same=same))
    heads = lax.map(attend, (split_heads(query), split_heads(keys), split_heads(values)))
    context = heads.transpose(1, 0, 2).reshape(inputs.shape[0], D)
    context = low(low_back(context))
    middle = inputs + low_back(grouped_product(context, w_out)) + out_bias
    act_two = low(layer_norm(middle, ln2_gain, ln2_bias))
    pre = low_back(jnp.dot(act_two, w_in, precision=HIGHEST)) + in_bias
    hidden = low(jax.nn.gelu(pre, approximate=False))
    return middle + low_back(grouped_product(hidden, w_back)) + back_bias

def reference(tokens, cotangent, segment_ids, ln1_gain, ln1_bias, w_query, query_bias, w_key, w_value, value_bias, w_out, out_bias, ln2_gain, ln2_bias, w_in, in_bias, w_back, back_bias):
    params = tuple((item.astype(jnp.float32) for item in (ln1_gain, ln1_bias, w_query, query_bias, w_key, w_value, value_bias, w_out, out_bias, ln2_gain, ln2_bias, w_in, in_bias, w_back, back_bias)))
    inputs = tokens.astype(jnp.float32).reshape(SEQS, SEQ_LEN, D)
    upstream = cotangent.astype(jnp.float32).reshape(SEQS, SEQ_LEN, D)

    def one_sequence(total, item):
        rows, grad_rows, segments = item
        result, pullback = jax.vjp(lambda first, second: layer(first, segments, second), rows, params)
        grad_input, grad_params = pullback(grad_rows)
        total = jax.tree.map(lambda left, right: left + right, total, grad_params)
        return (total, (result, grad_input))
    zeros = jax.tree.map(jnp.zeros_like, params)
    total, (results, grad_inputs) = lax.scan(one_sequence, zeros, (inputs, upstream, segment_ids))
    return (results.reshape(TOKENS, D).astype(jnp.bfloat16), grad_inputs.reshape(TOKENS, D), total[0], total[1], total[2], total[3], total[4], total[5], total[6], total[7], total[8], total[9], total[10], total[11], total[12], total[13], total[14])
```

```python
import functools

import jax
import jax.numpy as jnp
from jax import lax
from jax.experimental import pallas as pl
from jax.experimental.pallas import tpu as pltpu
from jax.sharding import PartitionSpec as P

HEAD_DIM = 64
EPSILON = 1e-12
MASKED = -1000000000.0
MESH_ID = pl.DeviceIdType.MESH
F32 = jnp.float32
BF16 = jnp.bfloat16

NN = (((1,), (0,)), ((), ()))
NT = (((1,), (1,)), ((), ()))
TN = (((0,), (0,)), ((), ()))


def mxu(left, right, dims):
    return lax.dot_general(left, right, dims, preferred_element_type=F32)


def position():
    dp = lax.axis_index("dp")
    tensor = lax.axis_index("tensor")
    return dp // 2, dp % 2, tensor // 2, tensor % 2


def device(z, y, x, core):
    return (z * 2 + y, x * 2 + core)


def offsets(depth):
    found = [(dz, dy, dx) for dz in range(1 - depth, depth) for dy in range(2) for dx in range(2)]
    return sorted(found, key=lambda item: abs(item[0]) + item[1] + item[2])


def level(route, offset):
    dims = dict(zip("zyx", offset))
    last = -1
    for place, name in enumerate(route):
        if dims[name] != 0:
            last = place
    return last


def when(condition, action):
    if condition is True:
        action()
    else:
        pl.when(condition)(action)


def meet_neighbours(depth):
    z, y, x, core = position()
    dp, tensor = lax.axis_index("dp"), lax.axis_index("tensor")
    barrier = pltpu.get_barrier_semaphore()

    def signal(target):
        pl.semaphore_signal(barrier, inc=1, device_id=target, device_id_type=MESH_ID)

    signal(device(z, y, x, 1 - core))
    signal(device(z, y, 1 - x, core))
    signal(device(z, 1 - y, x, core))
    pl.when(z > 0)(lambda: signal(device(z - 1, y, x, core)))
    pl.when(z < depth - 1)(lambda: signal(device(z + 1, y, x, core)))
    middle = (tensor == 1) | (tensor == 2)
    pl.when(middle)(lambda: signal((dp, 3 - tensor)))
    as_int = lambda flag: flag.astype(jnp.int32)
    pl.semaphore_wait(barrier, 3 + as_int(z > 0) + as_int(z < depth - 1) + as_int(middle))


def tree_sends(route, offset, depth):
    z, y, x, core = position()
    dz = offset[0]
    lev = level(route, offset)
    sends = []
    for place, name in enumerate(route):
        if name == "z":
            if place < lev:
                continue
            if place > lev or dz < 0:
                sends.append((0, device(jnp.minimum(z + 1, depth - 1), y, x, core), z < depth - 1, 0))
            if place > lev or dz > 0:
                sends.append((1, device(jnp.maximum(z - 1, 0), y, x, core), z > 0, 0))
        elif place > lev:
            if name == "y":
                sends.append((2, device(z, 1 - y, x, core), True, 2))
            else:
                sends.append((3, device(z, y, 1 - x, core), True, 1))
    return sends


def tree_parent(route, offset):
    z, y, x, core = position()
    dz, dy, dx = offset
    name = route[level(route, offset)]
    if name == "z":
        if dz < 0:
            return 0, device(z - 1, y, x, core)
        return 1, device(z + 1, y, x, core)
    if name == "y":
        return 2, device(z, 1 - y, x, core)
    return 3, device(z, y, 1 - x, core)


def exchange_halo(rows_left, rows_right, halo, halo_send, halo_recv, own_left, own_right):
    dp, tensor = lax.axis_index("dp"), lax.axis_index("tensor")
    has_left, has_right = tensor > 0, tensor < 3
    to_right = pltpu.make_async_remote_copy(
        rows_right, halo.at[0], halo_send.at[0], halo_recv.at[0], device_id=(dp, jnp.minimum(tensor + 1, 3)), device_id_type=MESH_ID
    )
    to_left = pltpu.make_async_remote_copy(
        rows_left, halo.at[1], halo_send.at[1], halo_recv.at[1], device_id=(dp, jnp.maximum(tensor - 1, 0)), device_id_type=MESH_ID
    )
    fill_left = pltpu.make_async_copy(own_left, halo.at[0], halo_send.at[2])
    fill_right = pltpu.make_async_copy(own_right, halo.at[1], halo_send.at[3])
    pl.when(has_right)(lambda: to_right.start())
    pl.when(has_left)(lambda: to_left.start())
    pl.when(~has_left)(lambda: fill_left.start())
    pl.when(~has_right)(lambda: fill_right.start())

    def finish():
        pl.when(has_right)(lambda: to_right.wait_send())
        pl.when(has_left)(lambda: to_left.wait_send())
        pl.when(has_left)(lambda: to_right.wait_recv())
        pl.when(has_right)(lambda: to_left.wait_recv())
        pl.when(~has_left)(lambda: fill_left.wait())
        pl.when(~has_right)(lambda: fill_right.wait())

    return finish


def gather_kernel(parts, depth, count, *refs):
    srcs, tok = refs[:count], refs[count]
    outs, halo = refs[count + 1 : 2 * count + 1], refs[2 * count + 1]
    send_sem, recv_sem, core_send, core_recv, own_sem, halo_send, halo_recv = refs[2 * count + 2 :]
    z, y, x, core = position()
    dp, tensor = lax.axis_index("dp"), lax.axis_index("tensor")
    sibling = device(z, y, x, 1 - core)
    meet_neighbours(depth)
    own = [pltpu.make_async_copy(srcs[i], outs[i].at[tensor, dp], own_sem.at[i]) for i in range(count)]
    for copy in own:
        copy.start()
    finish_halo = exchange_halo(tok, tok, halo, halo_send, halo_recv, tok, tok)

    def piece(part, offset, owner_core):
        dz, dy, dx = offset
        _, which, begin, size = parts[part]
        oy = 1 - y if dy else y
        ox = 1 - x if dx else x
        return outs[which].at[ox * 2 + owner_core, (z + dz) * 2 + oy, pl.ds(begin, size)]

    waits = []
    for offset in offsets(depth):
        for part, (route, which, begin, size) in enumerate(parts):
            dz, dy, dx = offset
            mine = offset == (0, 0, 0)
            target = piece(part, offset, core)
            block = srcs[which].at[pl.ds(begin, size)] if mine else target
            zi, bi = z + dz, dy * 2 + dx
            valid = True if dz == 0 else ((z + dz >= 0) & (z + dz <= depth - 1))
            sends = []
            for way, to, ok, shift in tree_sends(route, offset, depth):
                copy = pltpu.make_async_remote_copy(
                    block, target, send_sem.at[part, way, zi, bi], recv_sem.at[part, zi, bi + shift], device_id=to, device_id_type=MESH_ID
                )
                sends.append((copy, ok))
            arrival = pltpu.make_async_remote_copy(
                block, target, send_sem.at[part, 0, 0, 0], recv_sem.at[part, zi, bi], device_id=sibling, device_id_type=MESH_ID
            )
            over = pltpu.make_async_remote_copy(
                block, target, core_send.at[part, zi, bi], core_recv.at[part, zi, bi], device_id=sibling, device_id_type=MESH_ID
            )
            other = piece(part, offset, 1 - core)
            back = pltpu.make_async_remote_copy(
                other, other, core_send.at[part, zi, bi], core_recv.at[part, zi, bi], device_id=sibling, device_id_type=MESH_ID
            )

            def arrive(sends=sends, arrival=arrival, over=over, mine=mine):
                if not mine:
                    arrival.wait_recv()
                for copy, ok in sends:
                    when(ok, lambda copy=copy: copy.start())
                over.start()

            def finish(sends=sends, over=over, back=back):
                for copy, ok in sends:
                    when(ok, lambda copy=copy: copy.wait_send())
                over.wait_send()
                back.wait_recv()

            when(valid, arrive)
            waits.append((valid, finish))
    for valid, finish in waits:
        when(valid, finish)
    for copy in own:
        copy.wait()
    finish_halo()


GATHER_PARTS = (
    ("zyx", 1, 0, 48),
    ("zxy", 1, 48, 48),
    ("zxy", 2, 0, 16),
    ("zyx", 0, 0, 32),
    ("zxy", 0, 32, 32),
    ("yzx", 0, 64, 16),
    ("xzy", 0, 80, 16),
)


def gather_by_kernel(shards, tokens):
    hbm = pl.BlockSpec(memory_space=pl.ANY)
    n, count = len(GATHER_PARTS), len(shards)
    depth = 4
    return pl.pallas_call(
        functools.partial(gather_kernel, GATHER_PARTS, depth, count),
        out_shape=tuple(jax.ShapeDtypeStruct((4, 8) + s.shape, s.dtype) for s in shards)
        + (jax.ShapeDtypeStruct((2,) + tokens.shape, tokens.dtype),),
        in_specs=[hbm] * (count + 1),
        out_specs=(hbm,) * (count + 1),
        scratch_shapes=[
            pltpu.SemaphoreType.DMA((n, 4, 4, 4)),
            pltpu.SemaphoreType.DMA((n, 4, 4)),
            pltpu.SemaphoreType.DMA((n, 4, 4)),
            pltpu.SemaphoreType.DMA((n, 4, 4)),
            pltpu.SemaphoreType.DMA((count,)),
            pltpu.SemaphoreType.DMA((4,)),
            pltpu.SemaphoreType.DMA((2,)),
        ],
        compiler_params=pltpu.CompilerParams(collective_id=0, has_side_effects=True),
        name="gather_weights",
    )(*shards, tokens)


REDUCE_PARTS = (
    ("zyx", 0, 0, 32),
    ("zxy", 0, 32, 32),
    ("yzx", 0, 64, 16),
    ("xzy", 0, 80, 16),
    ("zyx", 1, 0, 48),
    ("zxy", 1, 48, 48),
    ("zxy", 2, 0, 16),
)


def reduce_kernel(parts, depth, count, *refs):
    grads, halo_in = refs[:count], refs[count]
    outs, halo = refs[count + 1 : 2 * count + 1], refs[2 * count + 1]
    accs = refs[2 * count + 2 : 3 * count + 2]
    cores = refs[3 * count + 2 : 4 * count + 2]
    lands = refs[4 * count + 2 : 5 * count + 2]
    load_sem, core_send, core_recv, send_sem, recv_sem, halo_send, halo_recv = refs[5 * count + 2 :]
    z, y, x, core = position()
    tensor = lax.axis_index("tensor")
    sibling = device(z, y, x, 1 - core)
    meet_neighbours(depth)
    finish_halo = exchange_halo(halo_in.at[0], halo_in.at[1], halo, halo_send, halo_recv, halo_in.at[0], halo_in.at[1])
    order = list(reversed(offsets(depth)))
    loads, overs = {}, {}
    for part, (route, which, begin, size) in enumerate(parts):
        for side in range(2):
            owner = 2 * side + core
            rows = pl.ds(begin, size)
            loads[part, side] = pltpu.make_async_copy(
                grads[which].at[owner, :, rows], accs[which].at[side, :, rows], load_sem.at[part, side]
            )
            overs[part, side] = pltpu.make_async_remote_copy(
                grads[which].at[2 * side + 1 - core, :, rows],
                cores[which].at[side, :, rows],
                core_send.at[part, side],
                core_recv.at[part, side],
                device_id=sibling,
                device_id_type=MESH_ID,
            )
            overs[part, side].start()
            loads[part, side].start()
    for part in range(len(parts)):
        for side in range(2):
            loads[part, side].wait()
            overs[part, side].wait_recv()
    waits = []
    for offset in order:
        for part, (route, which, begin, size) in enumerate(parts):
            dz, dy, dx = offset
            mine = offset == (0, 0, 0)
            zi, bi = z + dz, dy * 2 + dx
            valid = True if dz == 0 else ((z + dz >= 0) & (z + dz <= depth - 1))
            oy = 1 - y if dy else y
            ox = 1 - x if dx else x
            rows = pl.ds(begin, size)
            spot = zi * 2 + oy
            mine_acc = accs[which].at[ox, spot, rows]
            mine_core = cores[which].at[ox, spot, rows]
            children = []
            for way, to, ok, shift in tree_sends(route, offset, depth):
                land = lands[which].at[way, zi, bi, rows]
                wait = pltpu.make_async_remote_copy(
                    land, land, send_sem.at[part, 0, 0], recv_sem.at[part, way, zi, bi], device_id=sibling, device_id_type=MESH_ID
                )
                children.append((land, wait, ok))
            send = None
            if not mine:
                way, to = tree_parent(route, offset)
                shift = {0: 0, 1: 0, 2: 2, 3: 1}[way]
                send = pltpu.make_async_remote_copy(
                    mine_acc,
                    lands[which].at[way, zi, bi - shift, rows],
                    send_sem.at[part, zi, bi],
                    recv_sem.at[part, way, zi, bi - shift],
                    device_id=to,
                    device_id_type=MESH_ID,
                )

            def work(mine_acc=mine_acc, mine_core=mine_core, children=children, send=send, which=which, rows=rows):
                for land, wait, ok in children:
                    when(ok, lambda wait=wait: wait.wait_recv())
                total = mine_acc[...].astype(F32) + mine_core[...].astype(F32)
                for land, wait, ok in children:
                    term = land[...].astype(F32)
                    total = total + (term if ok is True else jnp.where(ok, term, 0.0))
                if send is None:
                    outs[which][rows] = total
                else:
                    mine_acc[...] = total.astype(BF16)
                    send.start()

            when(valid, work)
            if send is not None:
                waits.append((valid, send))
    for valid, send in waits:
        when(valid, lambda send=send: send.wait_send())
    for part in range(len(parts)):
        for side in range(2):
            overs[part, side].wait_send()
    finish_halo()


def reduce_by_kernel(grads, halo_rows):
    hbm = pl.BlockSpec(memory_space=pl.ANY)
    vmem = pl.BlockSpec(memory_space=pltpu.VMEM)
    n, count = len(REDUCE_PARTS), len(grads)
    depth = 4
    shapes = [g.shape[2:] for g in grads]
    return pl.pallas_call(
        functools.partial(reduce_kernel, REDUCE_PARTS, depth, count),
        out_shape=tuple(jax.ShapeDtypeStruct(s, F32) for s in shapes) + (jax.ShapeDtypeStruct(halo_rows.shape, halo_rows.dtype),),
        in_specs=[hbm] * (count + 1),
        out_specs=(vmem,) * count + (hbm,),
        scratch_shapes=[pltpu.VMEM((2, 8) + s, BF16) for s in shapes]
        + [pltpu.VMEM((2, 8) + s, BF16) for s in shapes]
        + [pltpu.VMEM((4, 4, 4) + s, BF16) for s in shapes]
        + [
            pltpu.SemaphoreType.DMA((n, 2)),
            pltpu.SemaphoreType.DMA((n, 2)),
            pltpu.SemaphoreType.DMA((n, 2)),
            pltpu.SemaphoreType.DMA((n, 4, 4)),
            pltpu.SemaphoreType.DMA((n, 4, 4, 4)),
            pltpu.SemaphoreType.DMA((4,)),
            pltpu.SemaphoreType.DMA((2,)),
        ],
        compiler_params=pltpu.CompilerParams(collective_id=1, has_side_effects=True, vmem_limit_bytes=60 * 1024 * 1024),
        name="reduce_gradients",
    )(*grads, halo_rows)


def gather_by_ops(shards, tokens):
    full = []
    for shard in shards:
        over_dp = lax.all_gather(shard, "dp", axis=0, tiled=False)
        full.append(lax.all_gather(over_dp, "tensor", axis=0, tiled=False))
    return tuple(full) + (halo_by_ops(tokens, tokens),)


def halo_by_ops(rows_left, rows_right):
    count = lax.axis_size("tensor")
    from_left = lax.ppermute(rows_right, "tensor", [(i, i + 1) for i in range(count - 1)])
    from_right = lax.ppermute(rows_left, "tensor", [(i, i - 1) for i in range(1, count)])
    return jnp.stack([from_left, from_right])


def reduce_by_ops(grads, halo_rows):
    sums = []
    for grad in grads:
        over_tensor = lax.psum_scatter(grad, "tensor", scatter_dimension=0, tiled=False)
        sums.append(lax.psum_scatter(over_tensor, "dp", scatter_dimension=0, tiled=False).astype(F32))
    return tuple(sums) + (halo_by_ops(halo_rows[0], halo_rows[1]),)


def norm_parts(values):
    center = values - jnp.mean(values, axis=-1, keepdims=True)
    rate = lax.rsqrt(jnp.mean(center * center, axis=-1, keepdims=True) + EPSILON)
    return center * rate, rate


def norm_pull(grad, normed, rate, gain):
    scaled = grad * gain
    return rate * (
        scaled
        - jnp.mean(scaled, axis=-1, keepdims=True)
        - normed * jnp.mean(scaled * normed, axis=-1, keepdims=True)
    )


def head_mask(head):
    lane = lax.broadcasted_iota(jnp.int32, (1, 3 * HEAD_DIM), 1)
    return (lane >= head * HEAD_DIM) & (lane < (head + 1) * HEAD_DIM)


QB = 256


def attend_kernel(q_ref, k_ref, v_ref, segq_ref, segk_ref, ctx_ref, lse_ref):
    rows, width = q_ref.shape[1], q_ref.shape[2]
    band = QB + 2 * rows
    for block in range(rows // QB):
        here = pl.ds(block * QB, QB)
        keys = pl.ds(block * QB, band)
        same = segq_ref[here, :] == segk_ref[:, keys]
        q = q_ref[0, here, :]
        k = k_ref[0, keys, :]
        v = v_ref[0, keys, :]
        total = jnp.zeros((QB, width), F32)
        for head in range(width // HEAD_DIM):
            mask = head_mask(head)
            raw = mxu(jnp.where(mask, q, jnp.zeros_like(q)), k, NT)
            scores = jnp.where(same, raw, MASKED)
            top = jnp.max(scores, axis=1, keepdims=True)
            expo = jnp.exp(scores - top)
            denom = jnp.sum(expo, axis=1, keepdims=True)
            part = mxu(expo.astype(BF16), v, NN)
            total = jnp.where(mask, part / denom, total)
            lse_ref[0, here, head : head + 1] = top + jnp.log(denom)
        ctx_ref[0, here, :] = total.astype(BF16)


def attend(query, keys, values, segq, segk):
    groups, rows, width = query.shape
    span = keys.shape[1]
    per_group = lambda n, w: pl.BlockSpec((1, n, w), lambda t: (t, 0, 0))
    return pl.pallas_call(
        attend_kernel,
        out_shape=(jax.ShapeDtypeStruct(query.shape, BF16), jax.ShapeDtypeStruct((groups, rows, width // HEAD_DIM), F32)),
        grid=(groups,),
        in_specs=[
            per_group(rows, width),
            per_group(span, width),
            per_group(span, width),
            pl.BlockSpec((rows, 1), lambda t: (0, 0)),
            pl.BlockSpec((1, span), lambda t: (0, 0)),
        ],
        out_specs=(per_group(rows, width), per_group(rows, width // HEAD_DIM)),
        compiler_params=pltpu.CompilerParams(vmem_limit_bytes=40 * 1024 * 1024),
        cost_estimate=pl.CostEstimate(flops=4 * 10**9, bytes_accessed=8 * 10**6, transcendentals=8 * 10**6),
        name="attend_forward",
    )(query, keys, values, segq, segk)


def pull_kernel(q_ref, k_ref, v_ref, kt_ref, do_ref, lse_ref, delta_ref, segq_ref, segk_ref, dq_ref, dk_ref, dv_ref, dk_acc, dv_acc, dq_acc):
    rows, width = q_ref.shape[1], q_ref.shape[2]
    heads = width // HEAD_DIM
    dk_acc[...] = jnp.zeros_like(dk_acc)
    dv_acc[...] = jnp.zeros_like(dv_acc)
    dq_acc[...] = jnp.zeros_like(dq_acc)
    tiles = (QB + 2 * rows) // QB
    for block in range(rows // QB):
        here = pl.ds(block * QB, QB)
        segq = segq_ref[:, here]
        q_heads, do_heads, lse, delta = [], [], [], []
        for head in range(heads):
            mask = head_mask(head)
            q_heads.append(jnp.where(mask, q_ref[0, here, :], jnp.zeros((), BF16)))
            do_heads.append(jnp.where(mask, do_ref[0, here, :], jnp.zeros((), BF16)))
            lse.append(lse_ref[0, head : head + 1, here])
            delta.append(delta_ref[0, head : head + 1, here])
        for tile in range(tiles):
            keys = pl.ds(block * QB + tile * QB, QB)
            same = segk_ref[keys, :] == segq
            k = k_ref[0, keys, :]
            v = v_ref[0, keys, :]
            dv_part = jnp.zeros((QB, width), F32)
            dk_part = jnp.zeros((QB, width), F32)
            for head in range(heads):
                raw = mxu(k, q_heads[head], NT)
                probs = jnp.exp(jnp.where(same, raw, MASKED) - lse[head])
                grad_weights = mxu(v, do_heads[head], NT)
                grad_raw = (probs * (grad_weights - delta[head])).astype(BF16)
                dv_part = dv_part + mxu(probs.astype(BF16), do_heads[head], NN)
                dk_part = dk_part + mxu(grad_raw, q_heads[head], NN)
                lanes = pl.ds(head * HEAD_DIM, HEAD_DIM)
                dq_acc[lanes, here] += mxu(kt_ref[0, lanes, keys], grad_raw, NN)
            dv_acc[keys, :] += dv_part
            dk_acc[keys, :] += dk_part
    dq_ref[0] = (dq_acc[...] * HEAD_DIM**-0.5).T.astype(BF16)
    dk_ref[0] = dk_acc[...].astype(BF16)
    dv_ref[0] = dv_acc[...].astype(BF16)


def attend_pull(query, keys, values, keys_t, grad_context, lse, delta, segq, segk):
    groups, rows, width = query.shape
    span = keys.shape[1]
    per_group = lambda n, w: pl.BlockSpec((1, n, w), lambda t: (t, 0, 0))
    heads = width // HEAD_DIM
    return pl.pallas_call(
        pull_kernel,
        out_shape=(
            jax.ShapeDtypeStruct(query.shape, BF16),
            jax.ShapeDtypeStruct(keys.shape, BF16),
            jax.ShapeDtypeStruct(keys.shape, BF16),
        ),
        grid=(groups,),
        in_specs=[
            per_group(rows, width),
            per_group(span, width),
            per_group(span, width),
            per_group(width, span),
            per_group(rows, width),
            per_group(heads, rows),
            per_group(heads, rows),
            pl.BlockSpec((1, rows), lambda t: (0, 0)),
            pl.BlockSpec((span, 1), lambda t: (0, 0)),
        ],
        out_specs=(per_group(rows, width), per_group(span, width), per_group(span, width)),
        scratch_shapes=[pltpu.VMEM((span, width), F32), pltpu.VMEM((span, width), F32), pltpu.VMEM((width, rows), F32)],
        compiler_params=pltpu.CompilerParams(vmem_limit_bytes=40 * 1024 * 1024),
        cost_estimate=pl.CostEstimate(flops=10 * 10**9, bytes_accessed=16 * 10**6, transcendentals=8 * 10**6),
        name="attend_backward",
    )(query, keys, values, keys_t, grad_context, lse, delta, segq, segk)


UNITS = 256


def mlp_kernel(act_ref, cot_ref, win_ref, wback_ref, bias_ref, out_ref, gact_ref, gin_ref, gback_ref, gbias_ref):
    @pl.when((pl.program_id(0) == 0) & (pl.program_id(1) == 0))
    def _():
        out_ref[...] = jnp.zeros_like(out_ref)
        gact_ref[...] = jnp.zeros_like(gact_ref)

    act, cot = act_ref[...], cot_ref[...]
    win, wback = win_ref[0], wback_ref[0]
    pre = mxu(act, win, NN) + bias_ref[0]
    phi = 0.5 + 0.5 * lax.erf(pre * (0.5**0.5))
    hidden = (pre * phi).astype(BF16)
    slope = phi + pre * (jnp.exp(-0.5 * pre * pre) * 0.3989422804014327)
    grad_pre = mxu(cot, wback, NN) * slope
    low = grad_pre.astype(BF16)
    gbias_ref[0] = jnp.sum(grad_pre, axis=0, keepdims=True)
    out_ref[...] += mxu(hidden, wback, NT)
    gact_ref[...] += mxu(low, win, NT)
    gin_ref[0] = mxu(act, low, TN).astype(BF16)
    gback_ref[0] = mxu(cot, hidden, TN).astype(BF16)


def mlp(act, cot, win, wback, bias):
    rows, width = act.shape
    groups, _, units = win.shape
    whole = pl.BlockSpec((rows, width), lambda t, u: (0, 0))
    tile = pl.BlockSpec((1, width, UNITS), lambda t, u: (t, 0, u))
    line = pl.BlockSpec((1, 1, UNITS), lambda t, u: (t, 0, u))
    return pl.pallas_call(
        mlp_kernel,
        out_shape=(
            jax.ShapeDtypeStruct((rows, width), F32),
            jax.ShapeDtypeStruct((rows, width), F32),
            jax.ShapeDtypeStruct(win.shape, BF16),
            jax.ShapeDtypeStruct(wback.shape, BF16),
            jax.ShapeDtypeStruct((groups, 1, units), F32),
        ),
        grid=(groups, units // UNITS),
        in_specs=[whole, whole, tile, tile, line],
        out_specs=(whole, whole, tile, tile, line),
        compiler_params=pltpu.CompilerParams(vmem_limit_bytes=40 * 1024 * 1024),
        cost_estimate=pl.CostEstimate(flops=15 * 10**9, bytes_accessed=40 * 10**6, transcendentals=3 * 10**6),
        name="mlp_both_ways",
    )(act, cot, win, wback, bias)


def per_device(by_kernel, *args):
    (
        tokens,
        cotangent,
        segment_ids,
        ln1_gain,
        ln1_bias,
        w_query,
        query_bias,
        w_key,
        w_value,
        value_bias,
        w_out,
        out_bias,
        ln2_gain,
        ln2_bias,
        w_in,
        in_bias,
        w_back,
        back_bias,
    ) = args
    rows, width = tokens.shape
    n_dp, n_tensor = lax.axis_size("dp"), lax.axis_size("tensor")
    index = lax.axis_index("tensor")
    head_width = w_query.shape[1]
    units = w_in.shape[1]
    seq_len = segment_ids.shape[1]
    slots = 16 * 128

    shard_mlp = jnp.concatenate([w_in, w_back.T], axis=1)
    shard_att = jnp.concatenate([w_query, w_key, w_value, w_out.T], axis=1)
    vectors = (ln1_gain, ln1_bias, query_bias, value_bias, out_bias, ln2_gain, ln2_bias, back_bias, in_bias)
    lengths = [v.shape[0] for v in vectors]
    flat = jnp.concatenate(vectors)
    shard_vec = jnp.pad(flat, (0, slots - flat.shape[0])).reshape(16, 128)

    gather = gather_by_kernel if by_kernel else gather_by_ops
    full_mlp, full_att, full_vec, halo = gather((shard_mlp, shard_att, shard_vec), tokens)
    full_mlp = full_mlp.reshape(n_tensor, width, 2 * units)
    full_att = full_att.reshape(n_tensor, width, 4 * head_width)
    flat_vec = full_vec[0].reshape(n_dp, slots)
    whole, begin = [], 0
    for length in lengths:
        whole.append(flat_vec[:, begin : begin + length].reshape(-1).astype(F32))
        begin += length
    gain_one, shift_one, q_shift, v_shift, o_shift, gain_two, shift_two, b_shift, i_shift = whole

    segs = segment_ids[0]
    edge = jnp.full((rows,), -1, jnp.int32)
    segs_all = jnp.concatenate([edge, segs, edge])
    segk = lax.dynamic_slice_in_dim(segs_all, index * rows, 3 * rows)
    segq = segk[rows : 2 * rows]

    inputs = jnp.concatenate([halo[0], tokens, halo[1]], axis=0).astype(F32)
    norm_one, rate_one = norm_parts(inputs)
    act_one = (norm_one * gain_one + shift_one).astype(BF16)
    own = act_one[rows : 2 * rows]
    wq = full_att[:, :, :head_width]
    wk = full_att[:, :, head_width : 2 * head_width]
    wv = full_att[:, :, 2 * head_width : 3 * head_width]
    wo_t = full_att[:, :, 3 * head_width :]
    project = lambda act, weight: jnp.einsum("rd,tdc->trc", act, weight, preferred_element_type=F32)
    query = (project(own, wq) + q_shift.reshape(n_tensor, 1, head_width)).astype(BF16)
    query = query * jnp.asarray(HEAD_DIM**-0.5, BF16)
    keys = project(act_one, wk).astype(BF16)
    values = (project(act_one, wv) + v_shift.reshape(n_tensor, 1, head_width)).astype(BF16)

    context, lse = attend(query, keys, values, segq[:, None], segk[None, :])

    attn = jnp.einsum("trc,toc->ro", context, wo_t, preferred_element_type=F32)
    middle = tokens.astype(F32) + attn + o_shift
    norm_two, rate_two = norm_parts(middle)
    act_two = (norm_two * gain_two + shift_two).astype(BF16)
    mlp_out, grad_two, grad_in, grad_back, grad_in_bias = mlp(
        act_two, cotangent, full_mlp[:, :, :units], full_mlp[:, :, units:], i_shift.reshape(n_tensor, 1, units)
    )
    output = (middle + mlp_out + b_shift).astype(BF16)

    upstream = cotangent.astype(F32)
    grad_middle = upstream + norm_pull(grad_two, norm_two, rate_two, gain_two)
    middle_low = grad_middle.astype(BF16)
    grad_out_t = jnp.einsum("ro,trc->toc", middle_low, context, preferred_element_type=F32).astype(BF16)
    grad_context = jnp.einsum("ro,toc->trc", middle_low, wo_t, preferred_element_type=F32).astype(BF16)
    heads = head_width // HEAD_DIM
    delta = jnp.sum(
        (grad_context.astype(F32) * context.astype(F32)).reshape(n_tensor, rows, heads, HEAD_DIM), axis=-1
    )
    dq, dk, dv = attend_pull(
        query,
        keys,
        values,
        jnp.swapaxes(keys, 1, 2),
        grad_context,
        jnp.swapaxes(lse, 1, 2),
        jnp.swapaxes(delta, 1, 2),
        segq[None, :],
        segk[:, None],
    )

    weight_grad = lambda act, grad: jnp.einsum("rd,trc->tdc", act, grad, preferred_element_type=F32).astype(BF16)
    back = lambda grad, weight: jnp.einsum("trc,tdc->rd", grad, weight, preferred_element_type=F32)
    grad_att = jnp.concatenate([weight_grad(own, dq), weight_grad(act_one, dk), weight_grad(act_one, dv), grad_out_t], axis=2)
    grad_one = back(dk, wk) + back(dv, wv)
    grad_one = jnp.concatenate(
        [grad_one[:rows], grad_one[rows : 2 * rows] + back(dq, wq), grad_one[2 * rows :]], axis=0
    )

    total = lambda values: jnp.sum(values.astype(F32), axis=0)
    pieces = (
        total(grad_one * norm_one),
        total(grad_one),
        jnp.sum(dq.astype(F32), axis=1).reshape(-1),
        jnp.sum(dv.astype(F32), axis=1).reshape(-1),
        total(grad_middle),
        total(grad_two * norm_two),
        total(grad_two),
        total(upstream),
        grad_in_bias.reshape(-1),
    )
    grad_vec = jnp.concatenate([p.reshape(n_dp, -1) for p in pieces], axis=1)
    grad_vec = jnp.pad(grad_vec, ((0, 0), (0, slots - grad_vec.shape[1]))).reshape(n_dp, 16, 128).astype(BF16)
    grad_vec = jnp.broadcast_to(grad_vec[None], (n_tensor,) + grad_vec.shape)
    grad_mlp = jnp.concatenate([grad_in, grad_back], axis=2)
    halo_rows = jnp.stack([grad_one[:rows], grad_one[2 * rows :]]).astype(BF16)

    reduce = reduce_by_kernel if by_kernel else reduce_by_ops
    split = lambda array: array.reshape(n_tensor, n_dp, width // n_dp, array.shape[-1])
    sum_mlp, sum_att, sum_vec, halo_back = reduce((split(grad_mlp), split(grad_att), grad_vec), halo_rows)

    from_left = jnp.where(index > 0, halo_back[0].astype(F32), 0.0)
    from_right = jnp.where(index < n_tensor - 1, halo_back[1].astype(F32), 0.0)
    own_grad = grad_one[rows : 2 * rows] + from_left + from_right
    grad_tokens = grad_middle + norm_pull(own_grad, norm_one[rows : 2 * rows], rate_one[rows : 2 * rows], gain_one)

    flat_sums = sum_vec.reshape(-1)
    vec, begin = [], 0
    for length in lengths:
        vec.append(flat_sums[begin : begin + length])
        begin += length
    g_ln1_gain, g_ln1_bias, g_q, g_v, g_o, g_ln2_gain, g_ln2_bias, g_b, g_i = vec
    return (
        output,
        grad_tokens,
        g_ln1_gain,
        g_ln1_bias,
        sum_att[:, :head_width],
        g_q,
        sum_att[:, head_width : 2 * head_width],
        sum_att[:, 2 * head_width : 3 * head_width],
        g_v,
        sum_att[:, 3 * head_width :].T,
        g_o,
        g_ln2_gain,
        g_ln2_bias,
        sum_mlp[:, :units],
        g_i,
        sum_mlp[:, units:].T,
        g_b,
    )


def solution(mesh):
    by_kernel = mesh.shape["dp"] == 8 and mesh.shape["tensor"] == 4
    rows = P(("dp", "tensor"), None)
    line, first, second = P("dp"), P("dp", "tensor"), P("tensor", "dp")
    return jax.shard_map(
        functools.partial(per_device, by_kernel),
        mesh=mesh,
        in_specs=(rows, rows, P("dp", None), line, line, first, line, first, first, line, second, line, line, line, first, line, second, line),
        out_specs=(rows, rows, line, line, first, line, first, first, line, second, line, line, line, first, line, second, line),
        check_vma=False,
    )
```

```python
import functools

import jax
import jax.numpy as jnp
from jax import lax
from jax.experimental import pallas as pl
from jax.experimental.pallas import tpu as pltpu
from jax.sharding import PartitionSpec as P

HEAD_DIM = 64
EPSILON = 1e-12
MASKED = -1000000000.0
MESH_ID = pl.DeviceIdType.MESH
F32 = jnp.float32
BF16 = jnp.bfloat16

NN = (((1,), (0,)), ((), ()))
NT = (((1,), (1,)), ((), ()))
TN = (((0,), (0,)), ((), ()))


def mxu(left, right, dims):
    return lax.dot_general(left, right, dims, preferred_element_type=F32)


def position():
    dp = lax.axis_index("dp")
    tensor = lax.axis_index("tensor")
    return dp // 2, dp % 2, tensor // 2, tensor % 2


def device(z, y, x, core):
    return (z * 2 + y, x * 2 + core)


def offsets(depth):
    found = [(dz, dy, dx) for dz in range(1 - depth, depth) for dy in range(2) for dx in range(2)]
    return sorted(found, key=lambda item: abs(item[0]) + item[1] + item[2])


def level(route, offset):
    dims = dict(zip("zyx", offset))
    last = -1
    for place, name in enumerate(route):
        if dims[name] != 0:
            last = place
    return last


def when(condition, action):
    if condition is True:
        action()
    else:
        pl.when(condition)(action)


def meet_neighbours(depth):
    z, y, x, core = position()
    dp, tensor = lax.axis_index("dp"), lax.axis_index("tensor")
    barrier = pltpu.get_barrier_semaphore()

    def signal(target):
        pl.semaphore_signal(barrier, inc=1, device_id=target, device_id_type=MESH_ID)

    signal(device(z, y, x, 1 - core))
    signal(device(z, y, 1 - x, core))
    signal(device(z, 1 - y, x, core))
    pl.when(z > 0)(lambda: signal(device(z - 1, y, x, core)))
    pl.when(z < depth - 1)(lambda: signal(device(z + 1, y, x, core)))
    middle = (tensor == 1) | (tensor == 2)
    pl.when(middle)(lambda: signal((dp, 3 - tensor)))
    as_int = lambda flag: flag.astype(jnp.int32)
    pl.semaphore_wait(barrier, 3 + as_int(z > 0) + as_int(z < depth - 1) + as_int(middle))


def tree_sends(route, offset, depth):
    z, y, x, core = position()
    dz = offset[0]
    lev = level(route, offset)
    sends = []
    for place, name in enumerate(route):
        if name == "z":
            if place < lev:
                continue
            if place > lev or dz < 0:
                sends.append((0, device(jnp.minimum(z + 1, depth - 1), y, x, core), z < depth - 1, 0))
            if place > lev or dz > 0:
                sends.append((1, device(jnp.maximum(z - 1, 0), y, x, core), z > 0, 0))
        elif place > lev:
            if name == "y":
                sends.append((2, device(z, 1 - y, x, core), True, 2))
            else:
                sends.append((3, device(z, y, 1 - x, core), True, 1))
    return sends


def tree_parent(route, offset):
    z, y, x, core = position()
    dz, dy, dx = offset
    name = route[level(route, offset)]
    if name == "z":
        if dz < 0:
            return 0, device(z - 1, y, x, core)
        return 1, device(z + 1, y, x, core)
    if name == "y":
        return 2, device(z, 1 - y, x, core)
    return 3, device(z, y, 1 - x, core)


def exchange_halo(rows_left, rows_right, halo, halo_send, halo_recv, own_left, own_right):
    dp, tensor = lax.axis_index("dp"), lax.axis_index("tensor")
    has_left, has_right = tensor > 0, tensor < 3
    to_right = pltpu.make_async_remote_copy(
        rows_right, halo.at[0], halo_send.at[0], halo_recv.at[0], device_id=(dp, jnp.minimum(tensor + 1, 3)), device_id_type=MESH_ID
    )
    to_left = pltpu.make_async_remote_copy(
        rows_left, halo.at[1], halo_send.at[1], halo_recv.at[1], device_id=(dp, jnp.maximum(tensor - 1, 0)), device_id_type=MESH_ID
    )
    fill_left = pltpu.make_async_copy(own_left, halo.at[0], halo_send.at[2])
    fill_right = pltpu.make_async_copy(own_right, halo.at[1], halo_send.at[3])
    pl.when(has_right)(lambda: to_right.start())
    pl.when(has_left)(lambda: to_left.start())
    pl.when(~has_left)(lambda: fill_left.start())
    pl.when(~has_right)(lambda: fill_right.start())

    def finish():
        pl.when(has_right)(lambda: to_right.wait_send())
        pl.when(has_left)(lambda: to_left.wait_send())
        pl.when(has_left)(lambda: to_right.wait_recv())
        pl.when(has_right)(lambda: to_left.wait_recv())
        pl.when(~has_left)(lambda: fill_left.wait())
        pl.when(~has_right)(lambda: fill_right.wait())

    return finish


def gather_kernel(parts, depth, count, *refs):
    srcs, tok = refs[:count], refs[count]
    outs, halo = refs[count + 1 : 2 * count + 1], refs[2 * count + 1]
    send_sem, recv_sem, core_send, core_recv, own_sem, halo_send, halo_recv = refs[2 * count + 2 :]
    z, y, x, core = position()
    dp, tensor = lax.axis_index("dp"), lax.axis_index("tensor")
    sibling = device(z, y, x, 1 - core)
    meet_neighbours(depth)
    own = [pltpu.make_async_copy(srcs[i], outs[i].at[tensor, dp], own_sem.at[i]) for i in range(count)]
    for copy in own:
        copy.start()
    finish_halo = exchange_halo(tok, tok, halo, halo_send, halo_recv, tok, tok)

    def piece(part, offset, owner_core):
        dz, dy, dx = offset
        _, which, begin, size = parts[part]
        oy = 1 - y if dy else y
        ox = 1 - x if dx else x
        return outs[which].at[ox * 2 + owner_core, (z + dz) * 2 + oy, pl.ds(begin, size)]

    waits = []
    for offset in offsets(depth):
        for part, (route, which, begin, size) in enumerate(parts):
            dz, dy, dx = offset
            mine = offset == (0, 0, 0)
            target = piece(part, offset, core)
            block = srcs[which].at[pl.ds(begin, size)] if mine else target
            zi, bi = z + dz, dy * 2 + dx
            valid = True if dz == 0 else ((z + dz >= 0) & (z + dz <= depth - 1))
            sends = []
            for way, to, ok, shift in tree_sends(route, offset, depth):
                copy = pltpu.make_async_remote_copy(
                    block, target, send_sem.at[part, way, zi, bi], recv_sem.at[part, zi, bi + shift], device_id=to, device_id_type=MESH_ID
                )
                sends.append((copy, ok))
            arrival = pltpu.make_async_remote_copy(
                block, target, send_sem.at[part, 0, 0, 0], recv_sem.at[part, zi, bi], device_id=sibling, device_id_type=MESH_ID
            )
            over = pltpu.make_async_remote_copy(
                block, target, core_send.at[part, zi, bi], core_recv.at[part, zi, bi], device_id=sibling, device_id_type=MESH_ID
            )
            other = piece(part, offset, 1 - core)
            back = pltpu.make_async_remote_copy(
                other, other, core_send.at[part, zi, bi], core_recv.at[part, zi, bi], device_id=sibling, device_id_type=MESH_ID
            )

            def arrive(sends=sends, arrival=arrival, over=over, mine=mine):
                if not mine:
                    arrival.wait_recv()
                for copy, ok in sends:
                    when(ok, lambda copy=copy: copy.start())
                over.start()

            def finish(sends=sends, over=over, back=back):
                for copy, ok in sends:
                    when(ok, lambda copy=copy: copy.wait_send())
                over.wait_send()
                back.wait_recv()

            when(valid, arrive)
            waits.append((valid, finish))
    for valid, finish in waits:
        when(valid, finish)
    for copy in own:
        copy.wait()
    finish_halo()


GATHER_PARTS = (
    ("zyx", 1, 0, 48),
    ("zxy", 1, 48, 48),
    ("zxy", 2, 0, 16),
    ("zyx", 0, 0, 32),
    ("zxy", 0, 32, 32),
    ("yzx", 0, 64, 16),
    ("xzy", 0, 80, 16),
)


def gather_by_kernel(shards, tokens):
    hbm = pl.BlockSpec(memory_space=pl.ANY)
    n, count = len(GATHER_PARTS), len(shards)
    depth = 4
    return pl.pallas_call(
        functools.partial(gather_kernel, GATHER_PARTS, depth, count),
        out_shape=tuple(jax.ShapeDtypeStruct((4, 8) + s.shape, s.dtype) for s in shards)
        + (jax.ShapeDtypeStruct((2,) + tokens.shape, tokens.dtype),),
        in_specs=[hbm] * (count + 1),
        out_specs=(hbm,) * (count + 1),
        scratch_shapes=[
            pltpu.SemaphoreType.DMA((n, 4, 4, 4)),
            pltpu.SemaphoreType.DMA((n, 4, 4)),
            pltpu.SemaphoreType.DMA((n, 4, 4)),
            pltpu.SemaphoreType.DMA((n, 4, 4)),
            pltpu.SemaphoreType.DMA((count,)),
            pltpu.SemaphoreType.DMA((4,)),
            pltpu.SemaphoreType.DMA((2,)),
        ],
        compiler_params=pltpu.CompilerParams(collective_id=0, has_side_effects=True),
        name="gather_weights",
    )(*shards, tokens)


def gather_by_ops(shards, tokens):
    full = []
    for shard in shards:
        over_dp = lax.all_gather(shard, "dp", axis=0, tiled=False)
        full.append(lax.all_gather(over_dp, "tensor", axis=0, tiled=False))
    return tuple(full) + (halo_by_ops(tokens, tokens),)


def halo_by_ops(rows_left, rows_right):
    count = lax.axis_size("tensor")
    from_left = lax.ppermute(rows_right, "tensor", [(i, i + 1) for i in range(count - 1)])
    from_right = lax.ppermute(rows_left, "tensor", [(i, i - 1) for i in range(1, count)])
    return jnp.stack([from_left, from_right])


def reduce_by_ops(grads, halo_rows):
    sums = []
    for grad in grads:
        over_tensor = lax.psum_scatter(grad, "tensor", scatter_dimension=0, tiled=False)
        sums.append(lax.psum_scatter(over_tensor, "dp", scatter_dimension=0, tiled=False).astype(F32))
    return tuple(sums) + (halo_by_ops(halo_rows[0], halo_rows[1]),)


def norm_parts(values):
    center = values - jnp.mean(values, axis=-1, keepdims=True)
    rate = lax.rsqrt(jnp.mean(center * center, axis=-1, keepdims=True) + EPSILON)
    return center * rate, rate


def norm_pull(grad, normed, rate, gain):
    scaled = grad * gain
    return rate * (
        scaled
        - jnp.mean(scaled, axis=-1, keepdims=True)
        - normed * jnp.mean(scaled * normed, axis=-1, keepdims=True)
    )


def head_mask(head):
    lane = lax.broadcasted_iota(jnp.int32, (1, 3 * HEAD_DIM), 1)
    return (lane >= head * HEAD_DIM) & (lane < (head + 1) * HEAD_DIM)


QB = 256
UNITS = 256
VMEM_LIMIT = 63 * 1024 * 1024
VEC_ROWS = 16
SHIFTS = 8
VMEM_SPEC = pl.BlockSpec(memory_space=pltpu.VMEM)
HBM_SPEC = pl.BlockSpec(memory_space=pl.ANY)


def unpack_vectors(vec_ref, rows_ref, units_ref, n_dp):
    width, groups = rows_ref.shape[1], units_ref.shape[0]
    piece, unit_rows = width // n_dp, units_ref.shape[2] * groups // n_dp // 128
    for dp in range(n_dp):
        rows_ref[0:SHIFTS, dp * piece : (dp + 1) * piece] = vec_ref[dp, 0:SHIFTS, 0:piece].astype(F32)
        for row in range(unit_rows):
            begin = (dp * unit_rows + row) * 128
            group, lane = begin // units_ref.shape[2], begin % units_ref.shape[2]
            units_ref[group, :, lane : lane + 128] = vec_ref[dp, SHIFTS + row : SHIFTS + row + 1, :].astype(F32)


def pack_vectors(rows_ref, units_ref, vec_ref, n_dp):
    width, groups = rows_ref.shape[1], units_ref.shape[0]
    piece, unit_rows = width // n_dp, units_ref.shape[2] * groups // n_dp // 128
    vec_ref[...] = jnp.zeros_like(vec_ref)
    for dp in range(n_dp):
        vec_ref[dp, 0:SHIFTS, 0:piece] = rows_ref[0:SHIFTS, dp * piece : (dp + 1) * piece].astype(BF16)
        for row in range(unit_rows):
            begin = (dp * unit_rows + row) * 128
            group, lane = begin // units_ref.shape[2], begin % units_ref.shape[2]
            vec_ref[dp, SHIFTS + row : SHIFTS + row + 1, :] = units_ref[group, :, lane : lane + 128].astype(BF16)


def attend_block(q, k, v, same):
    total = jnp.zeros(q.shape, F32)
    logs = []
    for head in range(q.shape[1] // HEAD_DIM):
        mask = head_mask(head)
        raw = mxu(jnp.where(mask, q, jnp.zeros_like(q)), k, NT)
        scores = jnp.where(same, raw, MASKED)
        top = jnp.max(scores, axis=1, keepdims=True)
        expo = jnp.exp(scores - top)
        denom = jnp.sum(expo, axis=1, keepdims=True)
        part = mxu(expo.astype(BF16), v, NN)
        total = jnp.where(mask, part / denom, total)
        logs.append(top + jnp.log(denom))
    return total.astype(BF16), logs


def forward_stages(tok, halo, wa, rows_ref, segq, segk, act, q, k, v, ctx, lse, middle, act_two, attn, logs_ref, tick):
    rows, width = tok.shape
    groups = wa.shape[0]
    head_width = q.shape[2]
    gain, shift = rows_ref[0:1, :], rows_ref[1:2, :]
    for part, source in enumerate((halo.at[0], tok, halo.at[1])):
        normed, _ = norm_parts(source[...].astype(F32))
        act[part * rows : (part + 1) * rows, :] = (normed * gain + shift).astype(BF16)
        tick()
    for group in range(groups):
        lanes = slice(group * head_width, (group + 1) * head_width)
        weights = wa[group]
        own = act[rows : 2 * rows, :]
        query = (mxu(own, weights[:, :head_width], NN) + rows_ref[2:3, lanes]).astype(BF16)
        q[group] = query * jnp.asarray(HEAD_DIM**-0.5, BF16)
        k[group] = mxu(act[...], weights[:, head_width : 2 * head_width], NN).astype(BF16)
        tick()
        v[group] = (mxu(act[...], weights[:, 2 * head_width : 3 * head_width], NN) + rows_ref[3:4, lanes]).astype(BF16)
        tick()
        band = QB + 2 * rows
        for block in range(rows // QB):
            here, keys = pl.ds(block * QB, QB), pl.ds(block * QB, band)
            same = segq[here, :] == segk[:, keys]
            result, logs = attend_block(q[group, here, :], k[group, keys, :], v[group, keys, :], same)
            ctx[group, here, :] = result
            for head, value in enumerate(logs):
                logs_ref[here, head : head + 1] = value
            tick()
        lse[group] = logs_ref[...].T[0 : lse.shape[1], :]
        part = mxu(ctx[group], weights[:, 3 * head_width :], NT)
        if group == 0:
            attn[...] = part
        else:
            attn[...] += part
        tick()
    total = tok[...].astype(F32) + attn[...] + rows_ref[4:5, :]
    middle[...] = total
    normed, _ = norm_parts(total)
    act_two[...] = (normed * rows_ref[5:6, :] + rows_ref[6:7, :]).astype(BF16)
    tick()


def forward_kernel(n_dp, tok, halo, wa, vec, segq, segk, rows_ref, units_ref, act_t, q, k, v, ctx, lse, middle, act_two, act, attn, logs_ref):
    unpack_vectors(vec, rows_ref, units_ref, n_dp)
    logs_ref[...] = jnp.zeros_like(logs_ref)
    forward_stages(tok, halo, wa, rows_ref, segq, segk, act, q, k, v, ctx, lse, middle, act_two, attn, logs_ref, lambda: None)
    act_t[...] = act[...].T


def forward_local(tok, halo, wa, vec, segq, segk, units):
    rows, width = tok.shape
    groups = wa.shape[0]
    head_width = wa.shape[2] // 4
    shape = jax.ShapeDtypeStruct
    return pl.pallas_call(
        functools.partial(forward_kernel, SPLIT),
        out_shape=(
            shape((VEC_ROWS, width), F32),
            shape((groups, 1, units), F32),
            shape((width, 3 * rows), BF16),
            shape((groups, rows, head_width), BF16),
            shape((groups, 3 * rows, head_width), BF16),
            shape((groups, 3 * rows, head_width), BF16),
            shape((groups, rows, head_width), BF16),
            shape((groups, 8, rows), F32),
            shape((rows, width), F32),
            shape((rows, width), BF16),
        ),
        in_specs=[VMEM_SPEC] * 6,
        out_specs=(VMEM_SPEC,) * 10,
        scratch_shapes=[pltpu.VMEM((3 * rows, width), BF16), pltpu.VMEM((rows, width), F32), pltpu.VMEM((rows, 128), F32)],
        compiler_params=pltpu.CompilerParams(vmem_limit_bytes=VMEM_LIMIT),
        name="forward_rows",
    )(tok, halo, wa, vec, segq, segk)


SPLIT = 8


def mlp_block(act, cot, act_t, cot_t, win, wback, bias, out, gact, gbias):
    pre = mxu(act[...], win, NN) + bias
    phi = 0.5 + 0.5 * lax.erf(pre * (0.5**0.5))
    hidden = (pre * phi).astype(BF16)
    slope = phi + pre * (jnp.exp(-0.5 * pre * pre) * 0.3989422804014327)
    grad_pre = mxu(cot[...], wback, NN) * slope
    low = grad_pre.astype(BF16)
    gbias[...] = jnp.sum(grad_pre, axis=0, keepdims=True)
    out[...] += mxu(hidden, wback, NT)
    gact[...] += mxu(low, win, NT)
    return mxu(act_t[...], low, NN).astype(BF16), mxu(cot_t[...], hidden, NN).astype(BF16)


def pull_group(q, k, v, do, ctx, lse, segq_row, segk_col, kt, dk_acc, dv_acc, dq_acc, tick):
    rows, width = q.shape
    heads = width // HEAD_DIM
    kt[...] = k[...].T
    dk_acc[...] = jnp.zeros_like(dk_acc)
    dv_acc[...] = jnp.zeros_like(dv_acc)
    dq_acc[...] = jnp.zeros_like(dq_acc)
    grad = do[...]
    product = grad.astype(F32) * ctx[...].astype(F32)
    row = lax.broadcasted_iota(jnp.int32, (8, width), 0)
    lane = lax.broadcasted_iota(jnp.int32, (8, width), 1)
    pick = jnp.where((lane >= row * HEAD_DIM) & (lane < (row + 1) * HEAD_DIM), 1.0, 0.0)
    delta_all = lax.dot_general(pick, product, NT, precision=lax.Precision.HIGHEST, preferred_element_type=F32)
    for block in range(rows // QB):
        here = pl.ds(block * QB, QB)
        span = slice(block * QB, (block + 1) * QB)
        segq = segq_row[:, here]
        query = q[here, :]
        q_stack = jnp.concatenate([jnp.where(head_mask(h), query, jnp.zeros_like(query)) for h in range(heads)], axis=0)
        do_stack = jnp.concatenate([jnp.where(head_mask(h), grad[span], jnp.zeros_like(query)) for h in range(heads)], axis=0)

        def body(tile, carry):
            keys = pl.ds(pl.multiple_of(block * QB + tile * QB, QB), QB)
            same = segk_col[keys, :] == segq
            raw = mxu(k[keys, :], q_stack, NT)
            grad_weights = mxu(v[keys, :], do_stack, NT)
            lows, grads = [], []
            for head in range(heads):
                part = slice(head * QB, (head + 1) * QB)
                probs = jnp.exp(jnp.where(same, raw[:, part], MASKED) - lse[head : head + 1, here])
                grad_raw = (probs * (grad_weights[:, part] - delta_all[head : head + 1, span])).astype(BF16)
                lows.append(probs.astype(BF16))
                grads.append(grad_raw)
                lanes = pl.ds(head * HEAD_DIM, HEAD_DIM)
                dq_acc[lanes, here] += mxu(kt[lanes, keys], grad_raw, NN)
            dv_acc[keys, :] += mxu(jnp.concatenate(lows, axis=1), do_stack, NN)
            dk_acc[keys, :] += mxu(jnp.concatenate(grads, axis=1), q_stack, NN)
            return carry

        lax.fori_loop(0, (QB + 2 * rows) // QB, body, 0)
        tick()


def land_slots(route, depth):
    ways = []
    for offset in offsets(depth):
        lev = level(route, offset)
        dz, dy, dx = offset
        for place, name in enumerate(route):
            if name == "z":
                if place < lev:
                    continue
                if place > lev or dz < 0:
                    ways.append((0, dy * 2 + dx))
                if place > lev or dz > 0:
                    ways.append((1, dy * 2 + dx))
            elif place > lev:
                ways.append((2 if name == "y" else 3, dy * 2 + dx))
    ways = sorted(set(ways))
    return {way: number * depth for number, way in enumerate(ways)}


def reduce_events(parts, depth, accs, cores, lands, outs, send_sem, recv_sem):
    z, y, x, core = position()
    sibling = device(z, y, x, 1 - core)
    events, ends = {}, []
    for offset in reversed(offsets(depth)):
        for part, (route, which, begin, size) in enumerate(parts):
            slots = land_slots(route, depth)
            dz, dy, dx = offset
            mine = offset == (0, 0, 0)
            zi, bi = z + dz, dy * 2 + dx
            valid = True if dz == 0 else ((z + dz >= 0) & (z + dz <= depth - 1))
            oy = 1 - y if dy else y
            ox = 1 - x if dx else x
            rows = pl.ds(begin, size)
            spot = zi * 2 + oy
            own = accs[which].at[ox, spot, rows]
            other = cores[which].at[ox, spot, rows]
            children = []
            for way, to, ok, shift in tree_sends(route, offset, depth):
                slot = slots[way, bi] + zi
                land = lands[part].at[slot]
                wait = pltpu.make_async_remote_copy(
                    land, land, send_sem.at[part, 0, 0], recv_sem.at[part, slot], device_id=sibling, device_id_type=MESH_ID
                )
                children.append((land, wait, ok))
            send = None
            if not mine:
                way, to = tree_parent(route, offset)
                slot = slots[way, bi - {0: 0, 1: 0, 2: 2, 3: 1}[way]] + zi
                send = pltpu.make_async_remote_copy(
                    own, lands[part].at[slot], send_sem.at[part, zi, bi], recv_sem.at[part, slot], device_id=to, device_id_type=MESH_ID
                )

            def work(own=own, other=other, children=children, send=send, which=which, rows=rows):
                for land, wait, ok in children:
                    when(ok, lambda wait=wait: wait.wait_recv())
                total = own[...].astype(F32) + other[...].astype(F32)
                for land, wait, ok in children:
                    term = land[...].astype(F32)
                    total = total + (term if ok is True else jnp.where(ok, term, 0.0))
                if send is None:
                    outs[which][rows] = total
                else:
                    own[...] = total.astype(BF16)
                    send.start()

            events[part * 100 + offsets(depth).index(offset)] = lambda valid=valid, work=work: when(valid, work)
            if send is not None:
                ends.append(lambda valid=valid, send=send: when(valid, lambda: send.wait_send()))
    return events, ends


REDUCE_PARTS = (
    ("zyx", 0, 0, 48),
    ("zxy", 0, 48, 48),
    ("zyx", 1, 0, 96),
    ("zyx", 2, 0, 16),
)

REDUCE_STEPS = (
    (),
    (27, 127, 26, 126, 24, 23, 123, 22),
    (124, 122, 20, 120, 17, 16, 116, 15),
    (117, 115, 13, 113, 9, 8, 108, 6),
    (109, 106, 2, 25, 125, 21, 121, 18),
    (102, 118, 14, 114, 10, 110, 7, 107),
    (19, 12, 103),
    (119, 112),
    (11, 5, 3),
    (111, 105),
    (),
    (4, 1),
    (104, 101),
    (227, 226, 224, 223, 222, 220, 217, 216),
    (0, 100, 215, 213, 209, 208, 206, 202),
    (),
    (),
    (),
    (),
    (),
    (),
    (),
    (),
    (225, 221, 218, 214, 210, 207, 203),
    (),
    (219, 212, 327, 326, 324, 323, 322, 320, 317, 316, 315, 313, 309, 308, 306, 302),
    (325, 321, 318, 314, 310, 307, 303, 211, 205, 319, 312, 204, 305, 201, 311, 301, 304, 200, 300),
)


class Ticker:
    def __init__(self, steps, table):
        self.steps, self.table, self.point = steps, table, 0

    def __call__(self):
        if self.steps:
            for number in self.table[self.point]:
                self.steps[number]()
        self.point += 1


def backward_kernel(remote, *refs):
    (tok, halo, cot_hbm, mid_hbm, two_hbm, act_t_hbm, wm_hbm, wa_hbm, rows_ref, units_ref) = refs[:10]
    (q_hbm, k_hbm, v_hbm, ctx_hbm, lse, segq_row, segk_col) = refs[10:17]
    output_hbm, sum_m, sum_a, sum_v, result_hbm, rest_hbm, back_hbm = refs[17:24]
    (cot, two, cot_t, two_t, mid, out_acc, gact, low_ref, wm, wa, q, k, v, ctx, stage_m) = refs[24:39]
    (grad_one, dk_acc, dv_acc, dq_acc, kt, do_ref, sums, gunits, qsum, vsum, gvec) = refs[39:50]
    (in_sem, wm_sem, wa_sem, group_sem, out_sem) = refs[50:55]
    rows, width = tok.shape
    groups = wm_hbm.shape[0]
    head_width = q.shape[1]
    units = units_ref.shape[2]
    narrow = wa.shape[2]
    stage_a = wm.at[1, :, :, pl.ds(0, narrow)]
    depth = 4
    tick = Ticker(None, None)
    if remote:
        count = len(REDUCE_PARTS)
        (acc_m, acc_a, acc_v, core_m, core_a, core_v, halo_land) = refs[55:62]
        lands = refs[62 : 62 + count]
        core_send, core_recv, send_sem, recv_sem, halo_send, halo_recv = refs[62 + count :]
        z, y, x, core = position()
        dp, tensor = lax.axis_index("dp"), lax.axis_index("tensor")
        sibling = device(z, y, x, 1 - core)
        order = [((1 - x) * 2 + 1 - core, 1 - x, False), ((1 - x) * 2 + core, 1 - x, True), (x * 2 + 1 - core, x, False), (x * 2 + core, x, True)]
        events, ends = reduce_events(
            REDUCE_PARTS, depth, (acc_m, acc_a, acc_v), (core_m, core_a, core_v), lands, (sum_m, sum_a, sum_v), send_sem, recv_sem
        )
        over = {}
        for which, (stage, cores) in enumerate(((stage_m, core_m), (stage_a, core_a))):
            for step, side in ((0, 1 - x), (2, x)):
                over[which, step] = pltpu.make_async_remote_copy(
                    stage, cores.at[side], core_send.at[which, step // 2], core_recv.at[which, step // 2], device_id=sibling, device_id_type=MESH_ID
                )
        meet_neighbours(depth)
        tick = Ticker(events, REDUCE_STEPS)
    else:
        order = [(t, 0, False) for t in range(groups)]
    t_of = [item[0] for item in order]

    load = lambda source, target, number: pltpu.make_async_copy(source, target, in_sem.at[number])
    inputs = [load(cot_hbm, cot, 0), load(two_hbm, two, 1), load(mid_hbm, mid, 2)]
    for copy in inputs:
        copy.start()
    wm_loads = [pltpu.make_async_copy(wm_hbm.at[t_of[s]], wm.at[s % 2], wm_sem.at[s % 2]) for s in range(groups)]
    wa_loads = [pltpu.make_async_copy(wa_hbm.at[t_of[s]], wa.at[s % 2], wa_sem.at[s % 2]) for s in range(groups)]
    group_loads = [
        [
            pltpu.make_async_copy(source.at[t_of[s]], target, group_sem.at[i])
            for i, (source, target) in enumerate(((q_hbm, q), (k_hbm, k), (v_hbm, v), (ctx_hbm, ctx)))
        ]
        for s in range(groups)
    ]
    wm_loads[0].start()
    wm_loads[1].start()
    wa_loads[0].start()
    for copy in group_loads[0]:
        copy.start()
    for copy in inputs:
        copy.wait()
    two_t[...] = two[...].T
    cot_t[...] = cot[...].T
    out_acc[...] = jnp.zeros_like(out_acc)
    gact[...] = jnp.zeros_like(gact)
    sums[...] = jnp.zeros_like(sums)

    def block_rows(value):
        return value.reshape(SPLIT, width // SPLIT, value.shape[1])

    for s in range(groups):
        t, side, mine = order[s]
        slot = s % 2
        wm_loads[s].wait()
        target = acc_m.at[side] if mine else stage_m
        if remote and s == 2:
            over[0, 0].wait_send()

        def body(block, carry):
            here = pl.ds(pl.multiple_of(block * UNITS, UNITS), UNITS)
            there = pl.ds(pl.multiple_of(units + block * UNITS, UNITS), UNITS)
            gin, gback = mlp_block(
                two, cot, two_t, cot_t, wm[slot, :, :, here].reshape(width, UNITS), wm[slot, :, :, there].reshape(width, UNITS), units_ref[t, :, here], out_acc, gact, gunits.at[t, :, here]
            )
            target[:, :, here] = block_rows(gin)
            target[:, :, there] = block_rows(gback)
            return carry

        lax.fori_loop(0, units // UNITS, body, 0)
        if remote:
            if not mine:
                over[0, s].start()
            else:
                over[0, s - 1].wait_recv()
        else:
            copy = pltpu.make_async_copy(stage_m, rest_hbm[0].at[t], out_sem.at[0])
            copy.start()
            copy.wait()
        if s + 2 < groups:
            wm_loads[s + 2].start()
        tick()
    act_t = wm.at[0]
    act_load = pltpu.make_async_copy(act_t_hbm, act_t, in_sem.at[2])
    act_load.start()
    upstream = cot[...].astype(F32)
    normed, rate = norm_parts(mid[...])
    two[...] = (mid[...] + out_acc[...] + rows_ref[7:8, :]).astype(BF16)
    output_store = pltpu.make_async_copy(two, output_hbm, out_sem.at[1])
    output_store.start()
    grad_two = gact[...]
    gmid = upstream + norm_pull(grad_two, normed, rate, rows_ref[5:6, :])
    mid[...] = gmid
    low_ref[...] = gmid.astype(BF16)
    sums[4:5, :] = jnp.sum(gmid, axis=0, keepdims=True)
    sums[5:6, :] = jnp.sum(grad_two * normed, axis=0, keepdims=True)
    sums[6:7, :] = jnp.sum(grad_two, axis=0, keepdims=True)
    sums[7:8, :] = jnp.sum(upstream, axis=0, keepdims=True)
    low_t = two_t
    low_t[...] = low_ref[...].T
    halo_loads = [
        pltpu.make_async_copy(halo.at[0], cot, in_sem.at[0]),
        pltpu.make_async_copy(halo.at[1], wa.at[groups % 2, pl.ds(0, rows)], in_sem.at[1]),
    ]
    halo_loads[0].start()
    tick()
    act_load.wait()
    for s in range(groups):
        t, side, mine = order[s]
        wa_loads[s].wait()
        for copy in group_loads[s]:
            copy.wait()
        if s + 1 < groups:
            wa_loads[s + 1].start()
        else:
            halo_loads[1].start()
        weights = wa[s % 2]
        target = acc_a.at[side] if mine else stage_a
        if remote and s == 2:
            over[1, 0].wait_send()
        first, second, third = head_width, 2 * head_width, 3 * head_width
        do_ref[...] = mxu(low_ref[...], weights[:, third:], NN).astype(BF16)
        target[:, :, third:] = block_rows(mxu(low_t[...], ctx[...], NN).astype(BF16))
        tick()
        pull_group(q, k, v, do_ref, ctx, lse.at[t], segq_row, segk_col, kt, dk_acc, dv_acc, dq_acc, lambda: tick())
        if s + 1 < groups:
            for copy in group_loads[s + 1]:
                copy.start()
        dq = (dq_acc[...] * HEAD_DIM**-0.5).T.astype(BF16)
        dk = dk_acc[...].astype(BF16)
        dv = dv_acc[...].astype(BF16)
        qsum[t] = jnp.sum(dq.astype(F32), axis=0, keepdims=True)
        vsum[t] = jnp.sum(dv_acc[...], axis=0, keepdims=True)
        target[:, :, :first] = block_rows(mxu(act_t[:, :, rows : 2 * rows].reshape(width, rows), dq, NN).astype(BF16))
        target[:, :, first:second] = block_rows(mxu(act_t[...].reshape(width, 3 * rows), dk, NN).astype(BF16))
        target[:, :, second:third] = block_rows(mxu(act_t[...].reshape(width, 3 * rows), dv, NN).astype(BF16))
        if remote:
            if not mine:
                over[1, s].start()
            else:
                over[1, s - 1].wait_recv()
        tick()
        part = mxu(dk, weights[:, first:second], NT) + mxu(dv, weights[:, second:third], NT)
        if s == 0:
            grad_one[...] = part
        else:
            grad_one[...] += part
        grad_one[rows : 2 * rows, :] += mxu(dq, weights[:, :first], NT)
        if not remote:
            copy = pltpu.make_async_copy(stage_a, rest_hbm[1].at[t], out_sem.at[0])
            copy.start()
            copy.wait()
        tick()
    output_store.wait()
    low_ref[...] = grad_one[:rows, :].astype(BF16)
    two[...] = grad_one[2 * rows :, :].astype(BF16)
    if remote:
        finish_halo = exchange_halo(low_ref, two, halo_land, halo_send, halo_recv, low_ref, two)
    gain_sum = jnp.zeros((1, width), F32)
    for copy in halo_loads:
        copy.wait()
    for part, source in enumerate((cot, tok, wa.at[groups % 2, pl.ds(0, rows)])):
        normed, rate = norm_parts(source[...].astype(F32))
        gain_sum = gain_sum + jnp.sum(grad_one[part * rows : (part + 1) * rows, :] * normed, axis=0, keepdims=True)
    sums[0:1, :] = gain_sum
    sums[1:2, :] = jnp.sum(grad_one[...], axis=0, keepdims=True)
    for t in range(groups):
        sums[2:3, t * head_width : (t + 1) * head_width] = qsum[t]
        sums[3:4, t * head_width : (t + 1) * head_width] = vsum[t]
    pack_vectors(sums, gunits, gvec, SPLIT)
    if not remote:
        copies = [
            pltpu.make_async_copy(low_ref, rest_hbm[2].at[0], out_sem.at[0]),
            pltpu.make_async_copy(two, rest_hbm[2].at[1], out_sem.at[1]),
            pltpu.make_async_copy(grad_one.at[pl.ds(rows, rows)], result_hbm, out_sem.at[2]),
            pltpu.make_async_copy(mid, back_hbm, out_sem.at[3]),
            pltpu.make_async_copy(gvec, rest_hbm[3], out_sem.at[4]),
        ]
        for copy in copies:
            copy.start()
        for copy in copies:
            copy.wait()
        return
    acc_v[0] = gvec[...]
    acc_v[1] = gvec[...]
    over_v = [
        pltpu.make_async_remote_copy(
            gvec, core_v.at[side], core_send.at[2, side], core_recv.at[2, side], device_id=sibling, device_id_type=MESH_ID
        )
        for side in range(2)
    ]
    for copy in over_v:
        copy.start()
    for copy in over_v:
        copy.wait_recv()
    tick()
    finish_halo()
    from_left = jnp.where(tensor > 0, halo_land[0].astype(F32), 0.0)
    from_right = jnp.where(tensor < 3, halo_land[1].astype(F32), 0.0)
    normed, rate = norm_parts(tok[...].astype(F32))
    total = grad_one[rows : 2 * rows, :] + from_left + from_right
    out_acc[...] = mid[...] + norm_pull(total, normed, rate, rows_ref[0:1, :])
    result_store = pltpu.make_async_copy(out_acc, result_hbm, out_sem.at[2])
    result_store.start()
    tick()
    for end in ends:
        end()
    over[0, 2].wait_send()
    over[1, 2].wait_send()
    for copy in over_v:
        copy.wait_send()
    result_store.wait()


def backward_rows(remote, tok, halo, cot, middle, act_two, act_t, wm, wa, rows_ref, units_ref, q, k, v, ctx, lse, segq_row, segk_col):
    rows, width = tok.shape
    groups, wide = wm.shape[0], wm.shape[-1]
    narrow = wa.shape[2]
    head_width = narrow // 4
    shape = jax.ShapeDtypeStruct
    vmem = pltpu.VMEM
    dma = lambda *dims: pltpu.SemaphoreType.DMA(dims)
    in_specs = [VMEM_SPEC, HBM_SPEC] + [HBM_SPEC] * 6 + [VMEM_SPEC] * 2 + [HBM_SPEC] * 4 + [VMEM_SPEC] * 3
    piece = width // SPLIT
    if remote:
        out_shape = (
            shape((rows, width), BF16),
            shape((piece, wide), F32),
            shape((piece, narrow), F32),
            shape((16, 128), F32),
            shape((rows, width), F32),
        )
        out_specs = (HBM_SPEC, VMEM_SPEC, VMEM_SPEC, VMEM_SPEC, HBM_SPEC)
    else:
        out_shape = (
            shape((rows, width), BF16),
            shape((groups, SPLIT, piece, wide), BF16),
            shape((groups, SPLIT, piece, narrow), BF16),
            shape((SPLIT, 16, 128), BF16),
            shape((2, rows, width), BF16),
            shape((rows, width), F32),
            shape((rows, width), F32),
        )
        out_specs = (HBM_SPEC,) * 7
    scratch = [
        vmem((rows, width), BF16),
        vmem((rows, width), BF16),
        vmem((width, rows), BF16),
        vmem((width, rows), BF16),
        vmem((rows, width), F32),
        vmem((rows, width), F32),
        vmem((rows, width), F32),
        vmem((rows, width), BF16),
        vmem((2, SPLIT, piece, wide), BF16),
        vmem((2, width, narrow), BF16),
        vmem((rows, head_width), BF16),
        vmem((3 * rows, head_width), BF16),
        vmem((3 * rows, head_width), BF16),
        vmem((rows, head_width), BF16),
        vmem((SPLIT, piece, wide), BF16),
        vmem((3 * rows, width), F32),
        vmem((3 * rows, head_width), F32),
        vmem((3 * rows, head_width), F32),
        vmem((head_width, rows), F32),
        vmem((head_width, 3 * rows), BF16),
        vmem((rows, head_width), BF16),
        vmem((VEC_ROWS, width), F32),
        vmem(units_ref.shape, F32),
        vmem((groups, 1, head_width), F32),
        vmem((groups, 1, head_width), F32),
        vmem((SPLIT, 16, 128), BF16),
        dma(3),
        dma(2),
        dma(2),
        dma(4),
        dma(5),
    ]
    params = dict(vmem_limit_bytes=VMEM_LIMIT)
    if remote:
        n = len(REDUCE_PARTS)
        sizes = ((piece, wide), (piece, narrow), (16, 128))
        slots = [4 * len(land_slots(p[0], 4)) for p in REDUCE_PARTS]
        scratch += [vmem((2, SPLIT) + size, BF16) for size in sizes]
        scratch += [vmem((2, SPLIT) + size, BF16) for size in sizes]
        scratch += [vmem((2, rows, width), BF16)]
        scratch += [vmem((slots[i], p[3], sizes[p[1]][1]), BF16) for i, p in enumerate(REDUCE_PARTS)]
        scratch += [dma(3, 2), dma(3, 2), dma(n, 4, 4), dma(n, max(slots)), dma(4), dma(2)]
        params.update(collective_id=1, has_side_effects=True)

    def kernel(*refs):
        ins, outs, rest = refs[:17], refs[17 : 17 + len(out_shape)], refs[17 + len(out_shape) :]
        if remote:
            outs = (outs[0], outs[1], outs[2], outs[3], outs[4], None, None)
        else:
            outs = (outs[0], None, None, None, outs[5], (outs[1], outs[2], outs[4], outs[3]), outs[6])
        backward_kernel(remote, *ins, *outs, *rest)

    return pl.pallas_call(
        kernel,
        out_shape=out_shape,
        in_specs=in_specs,
        out_specs=out_specs,
        scratch_shapes=scratch,
        compiler_params=pltpu.CompilerParams(**params),
        name="backward_rows",
    )(tok, halo, cot, middle, act_two, act_t.reshape(SPLIT, piece, 3 * rows), wm, wa, rows_ref, units_ref, q, k, v, ctx, lse, segq_row, segk_col)


def per_device(by_kernel, *args):
    (
        tokens,
        cotangent,
        segment_ids,
        ln1_gain,
        ln1_bias,
        w_query,
        query_bias,
        w_key,
        w_value,
        value_bias,
        w_out,
        out_bias,
        ln2_gain,
        ln2_bias,
        w_in,
        in_bias,
        w_back,
        back_bias,
    ) = args
    rows, width = tokens.shape
    n_dp, n_tensor = lax.axis_size("dp"), lax.axis_size("tensor")
    index = lax.axis_index("tensor")
    head_width = w_query.shape[1]
    units = w_in.shape[1]
    piece = ln1_gain.shape[0]
    unit_piece = in_bias.shape[0]

    shard_mlp = jnp.concatenate([w_in, w_back.T], axis=1)
    shard_att = jnp.concatenate([w_query, w_key, w_value, w_out.T], axis=1)
    vectors = jnp.stack([ln1_gain, ln1_bias, query_bias, value_bias, out_bias, ln2_gain, ln2_bias, back_bias])
    gather = gather_by_kernel if by_kernel else gather_by_ops
    if by_kernel:
        shard_vec = jnp.concatenate([jnp.pad(vectors, ((0, 0), (0, 128 - piece))), in_bias.reshape(-1, 128)], axis=0)
        shard_vec = jnp.pad(shard_vec, ((0, 16 - shard_vec.shape[0]), (0, 0)))
        full_mlp, full_att, full_vec, halo = gather((shard_mlp, shard_att, shard_vec), tokens)
        full_vec, n_pieces = full_vec[0], n_dp
    else:
        shard_vec = jnp.concatenate([vectors.reshape(-1), in_bias])
        full_mlp, full_att, full_vec, halo = gather((shard_mlp, shard_att, shard_vec), tokens)
        flat = full_vec[0]
        rows8 = jnp.swapaxes(flat[:, : 8 * piece].reshape(n_dp, 8, piece), 0, 1).reshape(8, 8, width // 8)
        rows8 = jnp.pad(jnp.swapaxes(rows8, 0, 1), ((0, 0), (0, 0), (0, 128 - width // 8)))
        n_pieces = SPLIT
        unit_rows = flat[:, 8 * piece :].reshape(n_pieces, -1, 128)
        full_vec = jnp.concatenate([rows8, unit_rows], axis=1)
        full_vec = jnp.pad(full_vec, ((0, 0), (0, 16 - full_vec.shape[1]), (0, 0)))
    full_mlp = full_mlp.reshape(n_tensor, SPLIT, width // SPLIT, 2 * units)
    full_att = full_att.reshape(n_tensor, width, 4 * head_width)

    segs = segment_ids[0]
    edge = jnp.full((rows,), -1, jnp.int32)
    segs_all = jnp.concatenate([edge, segs, edge])
    segk = lax.dynamic_slice_in_dim(segs_all, index * rows, 3 * rows)
    segq = segk[rows : 2 * rows]

    rows_vec, units_vec, act_t, query, keys, values, context, lse, middle, act_two = forward_local(
        tokens, halo, full_att, full_vec, segq[:, None], segk[None, :], units
    )
    results = backward_rows(
        by_kernel, tokens, halo, cotangent, middle, act_two, act_t, full_mlp, full_att, rows_vec, units_vec, query, keys, values,
        context, lse, segq[None, :], segk[:, None],
    )
    if by_kernel:
        output, sum_mlp, sum_att, sum_vec, grad_tokens = results
        vec = [sum_vec[i, :piece] for i in range(8)] + [sum_vec[8 : 8 + unit_piece // 128].reshape(-1)]
    else:
        output, grad_mlp, grad_att, grad_vec, halo_rows, grad_own, grad_middle = results
        split = lambda array: array.reshape(n_tensor, n_dp, width // n_dp, array.shape[-1])
        rows8 = jnp.swapaxes(grad_vec[:, :8, : width // 8], 0, 1).reshape(8, n_dp, piece)
        unit_flat = grad_vec[:, 8 : 8 + unit_piece * n_dp // SPLIT // 128].reshape(n_dp, unit_piece)
        flat = jnp.concatenate([jnp.swapaxes(rows8, 0, 1).reshape(n_dp, 8 * piece), unit_flat], axis=1)
        flat = jnp.broadcast_to(flat[None], (n_tensor,) + flat.shape)
        sum_mlp, sum_att, sum_vec, halo_back = reduce_by_ops((split(grad_mlp), split(grad_att), flat), halo_rows)
        vec = [sum_vec[i * piece : (i + 1) * piece] for i in range(8)] + [sum_vec[8 * piece :]]
        from_left = jnp.where(index > 0, halo_back[0].astype(F32), 0.0)
        from_right = jnp.where(index < n_tensor - 1, halo_back[1].astype(F32), 0.0)
        norm_one, rate_one = norm_parts(tokens.astype(F32))
        grad_tokens = grad_middle + norm_pull(grad_own + from_left + from_right, norm_one, rate_one, rows_vec[0:1])
    g_ln1_gain, g_ln1_bias, g_q, g_v, g_o, g_ln2_gain, g_ln2_bias, g_b, g_i = vec
    return (
        output,
        grad_tokens,
        g_ln1_gain,
        g_ln1_bias,
        sum_att[:, :head_width],
        g_q,
        sum_att[:, head_width : 2 * head_width],
        sum_att[:, 2 * head_width : 3 * head_width],
        g_v,
        sum_att[:, 3 * head_width :].T,
        g_o,
        g_ln2_gain,
        g_ln2_bias,
        sum_mlp[:, :units],
        g_i,
        sum_mlp[:, units:].T,
        g_b,
    )


def solution(mesh):
    by_kernel = mesh.shape["dp"] == 8 and mesh.shape["tensor"] == 4
    rows = P(("dp", "tensor"), None)
    line, first, second = P("dp"), P("dp", "tensor"), P("tensor", "dp")
    return jax.shard_map(
        functools.partial(per_device, by_kernel),
        mesh=mesh,
        in_specs=(rows, rows, P("dp", None), line, line, first, line, first, first, line, second, line, line, line, first, line, second, line),
        out_specs=(rows, rows, line, line, first, line, first, first, line, second, line, line, line, first, line, second, line),
        check_vma=False,
    )
```

```python
import functools

import jax
import jax.numpy as jnp
from jax import lax
from jax.experimental import pallas as pl
from jax.experimental.pallas import tpu as pltpu
from jax.sharding import PartitionSpec as P

HEAD_DIM = 64
EPSILON = 1e-12
MASKED = -1000000000.0
MESH_ID = pl.DeviceIdType.MESH
F32 = jnp.float32
BF16 = jnp.bfloat16

NN = (((1,), (0,)), ((), ()))
NT = (((1,), (1,)), ((), ()))
TN = (((0,), (0,)), ((), ()))


def mxu(left, right, dims):
    return lax.dot_general(left, right, dims, preferred_element_type=F32)


def position():
    dp = lax.axis_index("dp")
    tensor = lax.axis_index("tensor")
    return dp // 2, dp % 2, tensor // 2, tensor % 2


def device(z, y, x, core):
    return (z * 2 + y, x * 2 + core)


def offsets(depth):
    found = [(dz, dy, dx) for dz in range(1 - depth, depth) for dy in range(2) for dx in range(2)]
    return sorted(found, key=lambda item: abs(item[0]) + item[1] + item[2])


def level(route, offset):
    dims = dict(zip("zyx", offset))
    last = -1
    for place, name in enumerate(route):
        if dims[name] != 0:
            last = place
    return last


def when(condition, action):
    if condition is True:
        action()
    else:
        pl.when(condition)(action)


def meet_neighbours(depth):
    z, y, x, core = position()
    dp, tensor = lax.axis_index("dp"), lax.axis_index("tensor")
    barrier = pltpu.get_barrier_semaphore()

    def signal(target):
        pl.semaphore_signal(barrier, inc=1, device_id=target, device_id_type=MESH_ID)

    signal(device(z, y, x, 1 - core))
    signal(device(z, y, 1 - x, core))
    signal(device(z, 1 - y, x, core))
    pl.when(z > 0)(lambda: signal(device(z - 1, y, x, core)))
    pl.when(z < depth - 1)(lambda: signal(device(z + 1, y, x, core)))
    middle = (tensor == 1) | (tensor == 2)
    pl.when(middle)(lambda: signal((dp, 3 - tensor)))
    as_int = lambda flag: flag.astype(jnp.int32)
    pl.semaphore_wait(barrier, 3 + as_int(z > 0) + as_int(z < depth - 1) + as_int(middle))


def tree_sends(route, offset, depth):
    z, y, x, core = position()
    dz = offset[0]
    lev = level(route, offset)
    sends = []
    for place, name in enumerate(route):
        if name == "z":
            if place < lev:
                continue
            if place > lev or dz < 0:
                sends.append((0, device(jnp.minimum(z + 1, depth - 1), y, x, core), z < depth - 1, 0))
            if place > lev or dz > 0:
                sends.append((1, device(jnp.maximum(z - 1, 0), y, x, core), z > 0, 0))
        elif place > lev:
            if name == "y":
                sends.append((2, device(z, 1 - y, x, core), True, 2))
            else:
                sends.append((3, device(z, y, 1 - x, core), True, 1))
    return sends


def tree_parent(route, offset):
    z, y, x, core = position()
    dz, dy, dx = offset
    name = route[level(route, offset)]
    if name == "z":
        if dz < 0:
            return 0, device(z - 1, y, x, core)
        return 1, device(z + 1, y, x, core)
    if name == "y":
        return 2, device(z, 1 - y, x, core)
    return 3, device(z, y, 1 - x, core)


def exchange_halo(rows_left, rows_right, halo, halo_send, halo_recv, own_left, own_right):
    dp, tensor = lax.axis_index("dp"), lax.axis_index("tensor")
    has_left, has_right = tensor > 0, tensor < 3
    to_right = pltpu.make_async_remote_copy(
        rows_right, halo.at[0], halo_send.at[0], halo_recv.at[0], device_id=(dp, jnp.minimum(tensor + 1, 3)), device_id_type=MESH_ID
    )
    to_left = pltpu.make_async_remote_copy(
        rows_left, halo.at[1], halo_send.at[1], halo_recv.at[1], device_id=(dp, jnp.maximum(tensor - 1, 0)), device_id_type=MESH_ID
    )
    fill_left = pltpu.make_async_copy(own_left, halo.at[0], halo_send.at[2])
    fill_right = pltpu.make_async_copy(own_right, halo.at[1], halo_send.at[3])
    pl.when(has_right)(lambda: to_right.start())
    pl.when(has_left)(lambda: to_left.start())
    pl.when(~has_left)(lambda: fill_left.start())
    pl.when(~has_right)(lambda: fill_right.start())

    def finish():
        pl.when(has_right)(lambda: to_right.wait_send())
        pl.when(has_left)(lambda: to_left.wait_send())
        pl.when(has_left)(lambda: to_right.wait_recv())
        pl.when(has_right)(lambda: to_left.wait_recv())
        pl.when(~has_left)(lambda: fill_left.wait())
        pl.when(~has_right)(lambda: fill_right.wait())

    return finish


def gather_events(parts, depth, srcs, outs, send_sem, recv_sem, core_send, core_recv):
    z, y, x, core = position()
    sibling = device(z, y, x, 1 - core)
    events, backs, ends = {}, {}, []

    def piece(part, offset, owner_core):
        dz, dy, dx = offset
        _, which, begin, size = parts[part]
        oy = 1 - y if dy else y
        ox = 1 - x if dx else x
        return outs[which].at[ox * 2 + owner_core, (z + dz) * 2 + oy, pl.ds(begin, size)]

    for number, offset in enumerate(offsets(depth)):
        for part, (route, which, begin, size) in enumerate(parts):
            dz, dy, dx = offset
            mine = offset == (0, 0, 0)
            target = piece(part, offset, core)
            block = srcs[which].at[pl.ds(begin, size)] if mine else target
            zi, bi = z + dz, dy * 2 + dx
            valid = True if dz == 0 else ((z + dz >= 0) & (z + dz <= depth - 1))
            sends = []
            for way, to, ok, shift in tree_sends(route, offset, depth):
                copy = pltpu.make_async_remote_copy(
                    block, target, send_sem.at[part, way, zi, bi], recv_sem.at[part, zi, bi + shift], device_id=to, device_id_type=MESH_ID
                )
                sends.append((copy, ok))
            arrival = pltpu.make_async_remote_copy(
                block, target, send_sem.at[part, 0, 0, 0], recv_sem.at[part, zi, bi], device_id=sibling, device_id_type=MESH_ID
            )
            over = pltpu.make_async_remote_copy(
                block, target, core_send.at[part, zi, bi], core_recv.at[part, zi, bi], device_id=sibling, device_id_type=MESH_ID
            )
            other = piece(part, offset, 1 - core)
            back = pltpu.make_async_remote_copy(
                other, other, core_send.at[part, zi, bi], core_recv.at[part, zi, bi], device_id=sibling, device_id_type=MESH_ID
            )

            def arrive(sends=sends, arrival=arrival, over=over, mine=mine):
                if not mine:
                    arrival.wait_recv()
                for copy, ok in sends:
                    when(ok, lambda copy=copy: copy.start())
                over.start()

            def finish(sends=sends, over=over):
                for copy, ok in sends:
                    when(ok, lambda copy=copy: copy.wait_send())
                over.wait_send()

            events[part * 100 + number] = lambda valid=valid, arrive=arrive: when(valid, arrive)
            backs[part * 100 + number] = lambda valid=valid, back=back: when(valid, lambda: back.wait_recv())
            ends.append(lambda valid=valid, finish=finish: when(valid, finish))
    return events, backs, ends


GATHER_PARTS = (
    ("yzx", 1, 0, 48),
    ("xzy", 1, 48, 48),
    ("zyx", 0, 0, 48),
    ("zxy", 0, 48, 48),
)

GATHER_STEPS = (
    (0, 100),
    (1, 101, 3, 103, 4, 104),
    (),
    (),
    (5, 107, 10, 110, 105, 11, 2, 7, 111, 102, 12, 114, 18, 6, 112, 118, 19, 119, 8, 14, 108, 9, 109, 121, 106, 13, 200, 300, 21, 20, 125, 25),
    (113, 16, 24),
    (116, 17, 117),
    (15, 115, 22, 201, 23, 204),
    (203,),
    (301, 202, 304),
    (120, 124, 26, 27, 303, 122),
    (123, 302, 205),
    (211,),
    (305, 206, 207, 311),
    (126, 127),
    (209, 210, 212, 219),
    (),
    (307, 208, 312, 319),
    (),
    (306, 310),
    (),
    (308, 309),
    (213, 214, 221, 225),
    (217, 218, 220, 224),
    (313, 314, 321, 325),
    (318, 320, 324, 215, 317, 315, 227, 327, 216, 316, 222, 322, 226, 326, 223, 323),
)


def gather_by_ops(shards, tokens):
    full = []
    for shard in shards:
        over_dp = lax.all_gather(shard, "dp", axis=0, tiled=False)
        full.append(lax.all_gather(over_dp, "tensor", axis=0, tiled=False))
    return tuple(full) + (halo_by_ops(tokens, tokens),)


def halo_by_ops(rows_left, rows_right):
    count = lax.axis_size("tensor")
    from_left = lax.ppermute(rows_right, "tensor", [(i, i + 1) for i in range(count - 1)])
    from_right = lax.ppermute(rows_left, "tensor", [(i, i - 1) for i in range(1, count)])
    return jnp.stack([from_left, from_right])


def reduce_by_ops(grads, halo_rows):
    sums = []
    for grad in grads:
        over_tensor = lax.psum_scatter(grad, "tensor", scatter_dimension=0, tiled=False)
        sums.append(lax.psum_scatter(over_tensor, "dp", scatter_dimension=0, tiled=False).astype(F32))
    return tuple(sums) + (halo_by_ops(halo_rows[0], halo_rows[1]),)


def norm_parts(values):
    center = values - jnp.mean(values, axis=-1, keepdims=True)
    rate = lax.rsqrt(jnp.mean(center * center, axis=-1, keepdims=True) + EPSILON)
    return center * rate, rate


def norm_pull(grad, normed, rate, gain):
    scaled = grad * gain
    return rate * (
        scaled
        - jnp.mean(scaled, axis=-1, keepdims=True)
        - normed * jnp.mean(scaled * normed, axis=-1, keepdims=True)
    )


def head_mask(head):
    lane = lax.broadcasted_iota(jnp.int32, (1, 3 * HEAD_DIM), 1)
    return (lane >= head * HEAD_DIM) & (lane < (head + 1) * HEAD_DIM)


QB = 256
UNITS = 256
VMEM_LIMIT = 63 * 1024 * 1024
VEC_ROWS = 16
SPLIT = 8
SHIFTS = 8
VMEM_SPEC = pl.BlockSpec(memory_space=pltpu.VMEM)
HBM_SPEC = pl.BlockSpec(memory_space=pl.ANY)


class Ticker:
    def __init__(self, steps, table):
        self.steps, self.table, self.point = steps, table, 0

    def __call__(self):
        if self.steps:
            for number in self.table[self.point]:
                self.steps[number]()
        self.point += 1


def unpack_vectors(vec_ref, rows_ref, units_ref, n_dp):
    width, groups = rows_ref.shape[1], units_ref.shape[0]
    piece, unit_rows = width // n_dp, units_ref.shape[2] * groups // n_dp // 128
    pieces = [vec_ref[dp].astype(F32) for dp in range(n_dp)]
    rows_ref[...] = jnp.concatenate([item[:, :piece] for item in pieces], axis=1)
    lines = [item[SHIFTS + row : SHIFTS + row + 1, :] for item in pieces for row in range(unit_rows)]
    per_group = len(lines) // groups
    for group in range(groups):
        units_ref[group] = jnp.concatenate(lines[group * per_group : (group + 1) * per_group], axis=1)


def pack_vectors(rows_ref, units_ref, vec_ref, n_dp):
    width, groups = rows_ref.shape[1], units_ref.shape[0]
    piece, unit_rows = width // n_dp, units_ref.shape[2] * groups // n_dp // 128
    vec_ref[...] = jnp.zeros_like(vec_ref)
    for dp in range(n_dp):
        vec_ref[dp, 0:SHIFTS, 0:piece] = rows_ref[0:SHIFTS, dp * piece : (dp + 1) * piece].astype(BF16)
        for row in range(unit_rows):
            begin = (dp * unit_rows + row) * 128
            group, lane = begin // units_ref.shape[2], begin % units_ref.shape[2]
            vec_ref[dp, SHIFTS + row : SHIFTS + row + 1, :] = units_ref[group, :, lane : lane + 128].astype(BF16)


def attend_block(q, k, v, same):
    total = jnp.zeros(q.shape, F32)
    logs = []
    for head in range(q.shape[1] // HEAD_DIM):
        mask = head_mask(head)
        raw = mxu(jnp.where(mask, q, jnp.zeros_like(q)), k, NT)
        scores = jnp.where(same, raw, MASKED)
        top = jnp.max(scores, axis=1, keepdims=True)
        expo = jnp.exp(scores - top)
        denom = jnp.sum(expo, axis=1, keepdims=True)
        part = mxu(expo.astype(BF16), v, NN)
        total = jnp.where(mask, part / denom, total)
        logs.append(top + jnp.log(denom))
    return total.astype(BF16), logs


def forward_kernel(remote, *refs):
    if remote:
        tok, segs, w_in, w_back, w_query, w_key, w_value, w_out = refs[:8]
        lines, unit_line = refs[8:16], refs[16]
        full_m, full_a, halo_hbm = refs[17:20]
        refs = refs[20:]
    else:
        tok, segs, halo, wa, vec = refs[:5]
        refs = refs[5:]
    rows_ref, units_ref, segk, segcol, lse, *stores_hbm = refs[:12]
    act, attn, logs_ref, qshift, act_t, q, k, v, ctx, middle, act_two, store_sem = refs[12:24]
    if remote:
        halo, wa, vec, shard_m, shard_a, shard_v, segs_all = refs[24:31]
        send_sem, recv_sem, core_send, core_recv, own_sem, vec_send, vec_recv, halo_send, halo_recv = refs[31:]
    rows, width = tok.shape
    groups = wa.shape[0]
    head_width = q.shape[2]
    depth = 4
    tick = Ticker(None, None)
    order = list(range(groups))
    logs_ref[...] = jnp.zeros_like(logs_ref)
    if remote:
        z, y, x, core = position()
        dp, tensor = lax.axis_index("dp"), lax.axis_index("tensor")
        order = [x * 2 + core, x * 2 + 1 - core, (1 - x) * 2 + core, (1 - x) * 2 + 1 - core]
        peers = [lax.rem(dp + shift, SPLIT) for shift in range(1, SPLIT)]
        stacked = jnp.concatenate([line[...].astype(F32) for line in lines], axis=0)
        padding = jnp.zeros((SHIFTS, 128 - stacked.shape[1]), F32)
        tail = jnp.zeros((16 - SHIFTS - unit_line.shape[0], 128), F32)
        shard_v[...] = jnp.concatenate(
            [jnp.concatenate([stacked, padding], axis=1), unit_line[...].astype(F32), tail], axis=0
        ).astype(BF16)
        shard_a[...] = jnp.concatenate([w_query[...], w_key[...], w_value[...], w_out[...].T], axis=1)
        shard_m[:, : w_in.shape[1]] = w_in[...]
        shard_m[:, w_in.shape[1] :] = w_back[...]
        edge = jnp.full((1, rows), -1, jnp.int32)
        segs_all[...] = jnp.concatenate([edge, segs[...], edge], axis=1)
        barrier = pltpu.get_barrier_semaphore()
        middle_pair = (tensor == 1) | (tensor == 2)

        def signal(target):
            pl.semaphore_signal(barrier, inc=1, device_id=target, device_id_type=MESH_ID)

        for peer in peers:
            signal((peer, tensor))
        signal(device(z, y, x, 1 - core))
        signal(device(z, y, 1 - x, core))
        pl.when(middle_pair)(lambda: signal((dp, 3 - tensor)))
        pl.semaphore_wait(barrier, SPLIT + 1 + middle_pair.astype(jnp.int32))
        own = [
            pltpu.make_async_copy(shard_v, vec.at[dp], own_sem.at[0]),
            pltpu.make_async_copy(shard_a, wa.at[tensor, dp], own_sem.at[1]),
            pltpu.make_async_copy(shard_m, full_m.at[tensor, dp], own_sem.at[2]),
        ]
        vec_copies = [
            pltpu.make_async_remote_copy(
                shard_v, vec.at[dp], vec_send.at[i], vec_recv.at[i], device_id=(peer, tensor), device_id_type=MESH_ID
            )
            for i, peer in enumerate(peers)
        ]
        for copy in vec_copies:
            copy.start()
        for copy in own:
            copy.start()
        finish_halo = exchange_halo(tok, tok, halo, halo_send, halo_recv, tok, tok)
        events, backs, ends = gather_events(GATHER_PARTS, depth, (shard_m, shard_a), (full_m, wa), send_sem, recv_sem, core_send, core_recv)
        tick = Ticker(events, GATHER_STEPS)
        tick()
        for i in range(SPLIT - 1):
            source = lax.rem(dp + SPLIT - 1 - i, SPLIT)
            pltpu.make_async_remote_copy(
                vec.at[source], vec.at[source], vec_send.at[i], vec_recv.at[i], device_id=(dp, 3 - tensor), device_id_type=MESH_ID
            ).wait_recv()
        own[0].wait()

    def wait_backs(array, dx):
        if remote:
            for key, step in backs.items():
                part, number = key // 100, key % 100
                if GATHER_PARTS[part][1] == array and (dx is None or offsets(depth)[number][2] == dx):
                    step()

    if remote:
        segk[...] = segs_all[:, pl.ds(pl.multiple_of(tensor * rows, rows), 3 * rows)]
    else:
        segk[...] = segs[...]
    segcol[...] = jnp.broadcast_to(segk[...], (8, 3 * rows)).T
    unpack_vectors(vec, rows_ref, units_ref, SPLIT)
    shifts = rows_ref[0:SHIFTS, :]
    for group in range(groups):
        lanes = slice(group * head_width, (group + 1) * head_width)
        qshift[group] = shifts[:, lanes]
    tick()
    gain, shift = rows_ref[0:1, :], rows_ref[1:2, :]
    for part in (1, 0, 2):
        if remote and part == 0:
            finish_halo()
        source = tok if part == 1 else halo.at[part // 2]
        normed, _ = norm_parts(source[...].astype(F32))
        act[part * rows : (part + 1) * rows, :] = (normed * gain + shift).astype(BF16)
        tick()
    act_t[...] = act[...].T
    stores = [pltpu.make_async_copy(act_t, stores_hbm[0], store_sem.at[0])]
    stores[0].start()
    if remote:
        halo_copy = pltpu.make_async_copy(halo, halo_hbm, own_sem.at[0])
        halo_copy.start()
        own[1].wait()
    for s in range(groups):
        t = order[s]
        if s % 2 == 1:
            wait_backs(1, s // 2)
        if remote and s == groups - 1:
            att_copy = pltpu.make_async_copy(wa, full_a, own_sem.at[1])
            att_copy.start()
        cut = lambda i: wa[t, :, :, i * head_width : (i + 1) * head_width].reshape(width, head_width)
        own_rows = act[rows : 2 * rows, :]
        query = (mxu(own_rows, cut(0), NN) + qshift[t, 2:3, :]).astype(BF16)
        q[t] = query * jnp.asarray(HEAD_DIM**-0.5, BF16)
        k[t] = mxu(act[...], cut(1), NN).astype(BF16)
        tick()
        v[t] = (mxu(act[...], cut(2), NN) + qshift[t, 3:4, :]).astype(BF16)
        tick()
        band = QB + 2 * rows
        for block in range(rows // QB):
            here, keys = pl.ds(block * QB, QB), pl.ds(block * QB, band)
            same = segcol[pl.ds(rows + block * QB, QB), 0:1] == segk[:, keys]
            result, logs = attend_block(q[t, here, :], k[t, keys, :], v[t, keys, :], same)
            ctx[t, here, :] = result
            for head, value in enumerate(logs):
                logs_ref[here, head : head + 1] = value
            tick()
        lse[t] = logs_ref[...].T[0 : lse.shape[1], :]
        part = mxu(ctx[t], cut(3), NT)
        if s == 0:
            attn[...] = part
        else:
            attn[...] += part
        for i, source in enumerate((q, k, v, ctx)):
            stores.append(pltpu.make_async_copy(source.at[t], stores_hbm[1 + i].at[t], store_sem.at[1 + 4 * s + i]))
            stores[-1].start()
        tick()
    total = tok[...].astype(F32) + attn[...] + rows_ref[4:5, :]
    middle[...] = total
    normed, _ = norm_parts(total)
    act_two[...] = (normed * rows_ref[5:6, :] + rows_ref[6:7, :]).astype(BF16)
    for i, source in enumerate((middle, act_two)):
        stores.append(pltpu.make_async_copy(source, stores_hbm[5 + i], store_sem.at[1 + 4 * groups + i]))
        stores[-1].start()
    tick()
    for copy in stores:
        copy.wait()
    if remote:
        wait_backs(0, None)
        own[2].wait()
        for end in ends:
            end()
        for copy in vec_copies:
            copy.wait_send()
        halo_copy.wait()
        att_copy.wait()


def forward_rows(remote, tok, segs, units, *sources):
    rows, width = tok.shape
    groups, head_width = 4, width // 4
    piece = width // SPLIT
    shape = jax.ShapeDtypeStruct
    vmem = pltpu.VMEM
    dma = lambda *dims: pltpu.SemaphoreType.DMA(dims)
    saved = (
        ((width, 3 * rows), BF16),
        ((groups, rows, head_width), BF16),
        ((groups, 3 * rows, head_width), BF16),
        ((groups, 3 * rows, head_width), BF16),
        ((groups, rows, head_width), BF16),
        ((rows, width), F32),
        ((rows, width), BF16),
    )
    out_shape = (
        shape((VEC_ROWS, width), F32),
        shape((groups, 1, units), F32),
        shape((1, 3 * rows), jnp.int32),
        shape((3 * rows, 8), jnp.int32),
        shape((groups, 8, rows), F32),
    ) + tuple(shape(*item) for item in saved)
    out_specs = (VMEM_SPEC,) * 5 + (HBM_SPEC,) * 7
    scratch = [
        vmem((3 * rows, width), BF16),
        vmem((rows, width), F32),
        vmem((rows, 128), F32),
        vmem((groups, SHIFTS, head_width), F32),
    ]
    scratch += [vmem(*item) for item in saved] + [dma(3 + 4 * groups)]
    params = dict(vmem_limit_bytes=VMEM_LIMIT)
    if remote:
        n = len(GATHER_PARTS)
        wide, narrow = (piece, 2 * units), (piece, 4 * head_width)
        out_shape = (
            shape((groups, SPLIT) + wide, BF16),
            shape((groups, SPLIT) + narrow, BF16),
            shape((2, rows, width), BF16),
        ) + out_shape
        out_specs = (HBM_SPEC,) * 3 + out_specs
        scratch += [
            vmem((2, rows, width), BF16),
            vmem((groups, SPLIT) + narrow, BF16),
            vmem((SPLIT, 16, 128), BF16),
            vmem(wide, BF16),
            vmem(narrow, BF16),
            vmem((16, 128), BF16),
            vmem((1, segs.shape[1] + 2 * rows), jnp.int32),
        ]
        scratch += [dma(n, 4, 4, 4), dma(n, 4, 4), dma(n, 4, 4), dma(n, 4, 4), dma(3), dma(SPLIT - 1), dma(SPLIT - 1), dma(4), dma(2)]
        params.update(collective_id=0, has_side_effects=True)
    return pl.pallas_call(
        functools.partial(forward_kernel, remote),
        out_shape=out_shape,
        in_specs=[VMEM_SPEC] * (2 + len(sources)),
        out_specs=out_specs,
        scratch_shapes=scratch,
        compiler_params=pltpu.CompilerParams(**params),
        name="forward_rows",
    )(tok, segs, *sources)


def mlp_block(act, cot, act_t, cot_t, win, wback, bias, out, gact, gbias):
    pre = mxu(act[...], win, NN) + bias
    phi = 0.5 + 0.5 * lax.erf(pre * (0.5**0.5))
    hidden = (pre * phi).astype(BF16)
    slope = phi + pre * (jnp.exp(-0.5 * pre * pre) * 0.3989422804014327)
    grad_pre = mxu(cot[...], wback, NN) * slope
    low = grad_pre.astype(BF16)
    gbias[...] = jnp.sum(grad_pre, axis=0, keepdims=True)
    out[...] += mxu(hidden, wback, NT)
    gact[...] += mxu(low, win, NT)
    return mxu(act_t[...], low, NN).astype(BF16), mxu(cot_t[...], hidden, NN).astype(BF16)


def pull_group(q, k, v, do, ctx, lse, segq_row, segk_col, kt, dk_acc, dv_acc, dq_acc, tick):
    rows, width = q.shape
    heads = width // HEAD_DIM
    kt[...] = k[...].T
    dk_acc[...] = jnp.zeros_like(dk_acc)
    dv_acc[...] = jnp.zeros_like(dv_acc)
    dq_acc[...] = jnp.zeros_like(dq_acc)
    grad = do[...]
    product = grad.astype(F32) * ctx[...].astype(F32)
    row = lax.broadcasted_iota(jnp.int32, (8, width), 0)
    lane = lax.broadcasted_iota(jnp.int32, (8, width), 1)
    pick = jnp.where((lane >= row * HEAD_DIM) & (lane < (row + 1) * HEAD_DIM), 1.0, 0.0)
    delta_all = lax.dot_general(pick, product, NT, precision=lax.Precision.HIGHEST, preferred_element_type=F32)
    for block in range(rows // QB):
        here = pl.ds(block * QB, QB)
        span = slice(block * QB, (block + 1) * QB)
        segq = segq_row[:, here]
        query = q[here, :]
        q_stack = jnp.concatenate([jnp.where(head_mask(h), query, jnp.zeros_like(query)) for h in range(heads)], axis=0)
        do_stack = jnp.concatenate([jnp.where(head_mask(h), grad[span], jnp.zeros_like(query)) for h in range(heads)], axis=0)

        def body(tile, carry):
            keys = pl.ds(pl.multiple_of(block * QB + tile * QB, QB), QB)
            same = segk_col[keys, 0:1] == segq
            raw = mxu(k[keys, :], q_stack, NT)
            grad_weights = mxu(v[keys, :], do_stack, NT)
            lows, grads = [], []
            for head in range(heads):
                part = slice(head * QB, (head + 1) * QB)
                probs = jnp.exp(jnp.where(same, raw[:, part], MASKED) - lse[head : head + 1, here])
                grad_raw = (probs * (grad_weights[:, part] - delta_all[head : head + 1, span])).astype(BF16)
                lows.append(probs.astype(BF16))
                grads.append(grad_raw)
                lanes = pl.ds(head * HEAD_DIM, HEAD_DIM)
                dq_acc[lanes, here] += mxu(kt[lanes, keys], grad_raw, NN)
            dv_acc[keys, :] += mxu(jnp.concatenate(lows, axis=1), do_stack, NN)
            dk_acc[keys, :] += mxu(jnp.concatenate(grads, axis=1), q_stack, NN)
            return carry

        lax.fori_loop(0, (QB + 2 * rows) // QB, body, 0)
        tick()


def land_slots(route, depth):
    ways = []
    for offset in offsets(depth):
        lev = level(route, offset)
        dz, dy, dx = offset
        for place, name in enumerate(route):
            if name == "z":
                if place < lev:
                    continue
                if place > lev or dz < 0:
                    ways.append((0, dy * 2 + dx))
                if place > lev or dz > 0:
                    ways.append((1, dy * 2 + dx))
            elif place > lev:
                ways.append((2 if name == "y" else 3, dy * 2 + dx))
    ways = sorted(set(ways))
    return {way: number * depth for number, way in enumerate(ways)}


def reduce_events(parts, depth, accs, cores, lands, outs, send_sem, recv_sem):
    z, y, x, core = position()
    sibling = device(z, y, x, 1 - core)
    events, ends = {}, []
    for offset in reversed(offsets(depth)):
        for part, (route, which, begin, size) in enumerate(parts):
            slots = land_slots(route, depth)
            dz, dy, dx = offset
            mine = offset == (0, 0, 0)
            zi, bi = z + dz, dy * 2 + dx
            valid = True if dz == 0 else ((z + dz >= 0) & (z + dz <= depth - 1))
            oy = 1 - y if dy else y
            ox = 1 - x if dx else x
            rows = pl.ds(begin, size)
            spot = zi * 2 + oy
            own = accs[which].at[ox, spot, rows]
            other = cores[which].at[ox, spot, rows]
            children = []
            for way, to, ok, shift in tree_sends(route, offset, depth):
                slot = slots[way, bi] + zi
                land = lands[part].at[slot]
                wait = pltpu.make_async_remote_copy(
                    land, land, send_sem.at[part, 0, 0], recv_sem.at[part, slot], device_id=sibling, device_id_type=MESH_ID
                )
                children.append((land, wait, ok))
            send = None
            if not mine:
                way, to = tree_parent(route, offset)
                slot = slots[way, bi - {0: 0, 1: 0, 2: 2, 3: 1}[way]] + zi
                send = pltpu.make_async_remote_copy(
                    own, lands[part].at[slot], send_sem.at[part, zi, bi], recv_sem.at[part, slot], device_id=to, device_id_type=MESH_ID
                )

            def work(own=own, other=other, children=children, send=send, which=which, rows=rows):
                for land, wait, ok in children:
                    when(ok, lambda wait=wait: wait.wait_recv())
                total = own[...].astype(F32) + other[...].astype(F32)
                for land, wait, ok in children:
                    term = land[...].astype(F32)
                    total = total + (term if ok is True else jnp.where(ok, term, 0.0))
                if send is None:
                    outs[which][rows] = total
                else:
                    own[...] = total.astype(BF16)
                    send.start()

            events[part * 100 + offsets(depth).index(offset)] = lambda valid=valid, work=work: when(valid, work)
            if send is not None:
                ends.append(lambda valid=valid, send=send: when(valid, lambda: send.wait_send()))
    return events, ends


REDUCE_PARTS = (
    ("zyx", 0, 0, 48),
    ("zxy", 0, 48, 48),
    ("zyx", 1, 0, 96),
    ("zyx", 2, 0, 16),
)

REDUCE_STEPS = (
    (),
    (27, 127, 26, 126, 24, 23, 123, 22),
    (124, 122, 20, 120, 17, 16, 116, 15),
    (117, 115, 13, 113, 9, 8, 108, 6),
    (109, 106, 2, 25, 125, 21, 121, 18),
    (102, 118, 14, 114, 10, 110, 7, 107),
    (19, 12, 103),
    (119, 112),
    (11, 5, 3),
    (111, 105),
    (),
    (4, 1),
    (104, 101),
    (227, 226, 224, 223, 222, 220, 217, 216),
    (0, 100, 215, 213, 209, 208, 206, 202),
    (),
    (),
    (),
    (),
    (),
    (),
    (),
    (),
    (225, 221, 218, 214, 210, 207, 203),
    (),
    (219, 212, 327, 326, 324, 323, 322, 320, 317, 316, 315, 313, 309, 308, 306, 302),
    (325, 321, 318, 314, 310, 307, 303, 211, 205, 319, 312, 204, 305, 201, 311, 301, 304, 200, 300),
)


def backward_kernel(remote, *refs):
    (tok, halo, cot_hbm, mid_hbm, two_hbm, act_t_hbm, wm_hbm, wa_hbm, rows_ref, units_ref) = refs[:10]
    (q_hbm, k_hbm, v_hbm, ctx_hbm, lse, segk_row, segk_col) = refs[10:17]
    output_hbm, sum_m, sum_a, sum_v, result_hbm, rest_hbm, back_hbm = refs[17:24]
    (cot, two, cot_t, two_t, mid, out_acc, gact, low_ref, wm, wa, q, k, v, ctx, stage_m) = refs[24:39]
    (grad_one, dk_acc, dv_acc, dq_acc, kt, do_ref, sums, gunits, qsum, vsum, gvec) = refs[39:50]
    (in_sem, wm_sem, wa_sem, group_sem, out_sem) = refs[50:55]
    rows, width = tok.shape
    groups = wm_hbm.shape[0]
    head_width = q.shape[1]
    units = units_ref.shape[2]
    segq_row = segk_row.at[:, pl.ds(rows, rows)]
    narrow = wa.shape[2]
    stage_a = wm.at[1, :, :, pl.ds(0, narrow)]
    depth = 4
    tick = Ticker(None, None)
    if remote:
        count = len(REDUCE_PARTS)
        (acc_m, acc_a, acc_v, core_m, core_a, core_v, halo_land) = refs[55:62]
        lands = refs[62 : 62 + count]
        core_send, core_recv, send_sem, recv_sem, halo_send, halo_recv = refs[62 + count :]
        z, y, x, core = position()
        dp, tensor = lax.axis_index("dp"), lax.axis_index("tensor")
        sibling = device(z, y, x, 1 - core)
        order = [((1 - x) * 2 + 1 - core, 1 - x, False), ((1 - x) * 2 + core, 1 - x, True), (x * 2 + 1 - core, x, False), (x * 2 + core, x, True)]
        events, ends = reduce_events(
            REDUCE_PARTS, depth, (acc_m, acc_a, acc_v), (core_m, core_a, core_v), lands, (sum_m, sum_a, sum_v), send_sem, recv_sem
        )
        over = {}
        for which, (stage, cores) in enumerate(((stage_m, core_m), (stage_a, core_a))):
            for step, side in ((0, 1 - x), (2, x)):
                over[which, step] = pltpu.make_async_remote_copy(
                    stage, cores.at[side], core_send.at[which, step // 2], core_recv.at[which, step // 2], device_id=sibling, device_id_type=MESH_ID
                )
        meet_neighbours(depth)
        tick = Ticker(events, REDUCE_STEPS)
    else:
        order = [(t, 0, False) for t in range(groups)]
    t_of = [item[0] for item in order]

    load = lambda source, target, number: pltpu.make_async_copy(source, target, in_sem.at[number])
    inputs = [load(cot_hbm, cot, 0), load(two_hbm, two, 1), load(mid_hbm, mid, 2)]
    for copy in inputs:
        copy.start()
    wm_loads = [pltpu.make_async_copy(wm_hbm.at[t_of[s]], wm.at[s % 2], wm_sem.at[s % 2]) for s in range(groups)]
    wa_loads = [pltpu.make_async_copy(wa_hbm.at[t_of[s]], wa.at[s % 2], wa_sem.at[s % 2]) for s in range(groups)]
    group_loads = [
        [
            pltpu.make_async_copy(source.at[t_of[s]], target, group_sem.at[i])
            for i, (source, target) in enumerate(((q_hbm, q), (k_hbm, k), (v_hbm, v), (ctx_hbm, ctx)))
        ]
        for s in range(groups)
    ]
    wm_loads[0].start()
    wm_loads[1].start()
    wa_loads[0].start()
    for copy in group_loads[0]:
        copy.start()
    for copy in inputs:
        copy.wait()
    two_t[...] = two[...].T
    cot_t[...] = cot[...].T
    out_acc[...] = jnp.zeros_like(out_acc)
    gact[...] = jnp.zeros_like(gact)
    sums[...] = jnp.zeros_like(sums)

    def block_rows(value):
        return value.reshape(SPLIT, width // SPLIT, value.shape[1])

    for s in range(groups):
        t, side, mine = order[s]
        slot = s % 2
        wm_loads[s].wait()
        target = acc_m.at[side] if mine else stage_m
        if remote and s == 2:
            over[0, 0].wait_send()

        def body(block, carry):
            here = pl.ds(pl.multiple_of(block * UNITS, UNITS), UNITS)
            there = pl.ds(pl.multiple_of(units + block * UNITS, UNITS), UNITS)
            gin, gback = mlp_block(
                two, cot, two_t, cot_t, wm[slot, :, :, here].reshape(width, UNITS), wm[slot, :, :, there].reshape(width, UNITS), units_ref[t, :, here], out_acc, gact, gunits.at[t, :, here]
            )
            target[:, :, here] = block_rows(gin)
            target[:, :, there] = block_rows(gback)
            return carry

        lax.fori_loop(0, units // UNITS, body, 0)
        if remote:
            if not mine:
                over[0, s].start()
            else:
                over[0, s - 1].wait_recv()
        else:
            copy = pltpu.make_async_copy(stage_m, rest_hbm[0].at[t], out_sem.at[0])
            copy.start()
            copy.wait()
        if s + 2 < groups:
            wm_loads[s + 2].start()
        tick()
    act_t = wm.at[0]
    act_load = pltpu.make_async_copy(act_t_hbm, act_t, in_sem.at[2])
    act_load.start()
    upstream = cot[...].astype(F32)
    normed, rate = norm_parts(mid[...])
    two[...] = (mid[...] + out_acc[...] + rows_ref[7:8, :]).astype(BF16)
    output_store = pltpu.make_async_copy(two, output_hbm, out_sem.at[1])
    output_store.start()
    grad_two = gact[...]
    gmid = upstream + norm_pull(grad_two, normed, rate, rows_ref[5:6, :])
    mid[...] = gmid
    low_ref[...] = gmid.astype(BF16)
    sums[4:5, :] = jnp.sum(gmid, axis=0, keepdims=True)
    sums[5:6, :] = jnp.sum(grad_two * normed, axis=0, keepdims=True)
    sums[6:7, :] = jnp.sum(grad_two, axis=0, keepdims=True)
    sums[7:8, :] = jnp.sum(upstream, axis=0, keepdims=True)
    low_t = two_t
    low_t[...] = low_ref[...].T
    halo_loads = [
        pltpu.make_async_copy(halo.at[0], cot, in_sem.at[0]),
        pltpu.make_async_copy(halo.at[1], wa.at[groups % 2, pl.ds(0, rows)], in_sem.at[1]),
    ]
    halo_loads[0].start()
    tick()
    act_load.wait()
    for s in range(groups):
        t, side, mine = order[s]
        wa_loads[s].wait()
        for copy in group_loads[s]:
            copy.wait()
        if s + 1 < groups:
            wa_loads[s + 1].start()
        else:
            halo_loads[1].start()
        weights = wa[s % 2]
        target = acc_a.at[side] if mine else stage_a
        if remote and s == 2:
            over[1, 0].wait_send()
        first, second, third = head_width, 2 * head_width, 3 * head_width
        do_ref[...] = mxu(low_ref[...], weights[:, third:], NN).astype(BF16)
        target[:, :, third:] = block_rows(mxu(low_t[...], ctx[...], NN).astype(BF16))
        tick()
        pull_group(q, k, v, do_ref, ctx, lse.at[t], segq_row, segk_col, kt, dk_acc, dv_acc, dq_acc, lambda: tick())
        if s + 1 < groups:
            for copy in group_loads[s + 1]:
                copy.start()
        dq = (dq_acc[...] * HEAD_DIM**-0.5).T.astype(BF16)
        dk = dk_acc[...].astype(BF16)
        dv = dv_acc[...].astype(BF16)
        qsum[t] = jnp.sum(dq.astype(F32), axis=0, keepdims=True)
        vsum[t] = jnp.sum(dv_acc[...], axis=0, keepdims=True)
        target[:, :, :first] = block_rows(mxu(act_t[:, :, rows : 2 * rows].reshape(width, rows), dq, NN).astype(BF16))
        target[:, :, first:second] = block_rows(mxu(act_t[...].reshape(width, 3 * rows), dk, NN).astype(BF16))
        target[:, :, second:third] = block_rows(mxu(act_t[...].reshape(width, 3 * rows), dv, NN).astype(BF16))
        if remote:
            if not mine:
                over[1, s].start()
            else:
                over[1, s - 1].wait_recv()
        tick()
        part = mxu(dk, weights[:, first:second], NT) + mxu(dv, weights[:, second:third], NT)
        if s == 0:
            grad_one[...] = part
        else:
            grad_one[...] += part
        grad_one[rows : 2 * rows, :] += mxu(dq, weights[:, :first], NT)
        if not remote:
            copy = pltpu.make_async_copy(stage_a, rest_hbm[1].at[t], out_sem.at[0])
            copy.start()
            copy.wait()
        tick()
    output_store.wait()
    low_ref[...] = grad_one[:rows, :].astype(BF16)
    two[...] = grad_one[2 * rows :, :].astype(BF16)
    if remote:
        finish_halo = exchange_halo(low_ref, two, halo_land, halo_send, halo_recv, low_ref, two)
    gain_sum = jnp.zeros((1, width), F32)
    for copy in halo_loads:
        copy.wait()
    for part, source in enumerate((cot, tok, wa.at[groups % 2, pl.ds(0, rows)])):
        normed, rate = norm_parts(source[...].astype(F32))
        gain_sum = gain_sum + jnp.sum(grad_one[part * rows : (part + 1) * rows, :] * normed, axis=0, keepdims=True)
    sums[0:1, :] = gain_sum
    sums[1:2, :] = jnp.sum(grad_one[...], axis=0, keepdims=True)
    for t in range(groups):
        sums[2:3, t * head_width : (t + 1) * head_width] = qsum[t]
        sums[3:4, t * head_width : (t + 1) * head_width] = vsum[t]
    pack_vectors(sums, gunits, gvec, SPLIT)
    if not remote:
        copies = [
            pltpu.make_async_copy(low_ref, rest_hbm[2].at[0], out_sem.at[0]),
            pltpu.make_async_copy(two, rest_hbm[2].at[1], out_sem.at[1]),
            pltpu.make_async_copy(grad_one.at[pl.ds(rows, rows)], result_hbm, out_sem.at[2]),
            pltpu.make_async_copy(mid, back_hbm, out_sem.at[3]),
            pltpu.make_async_copy(gvec, rest_hbm[3], out_sem.at[4]),
        ]
        for copy in copies:
            copy.start()
        for copy in copies:
            copy.wait()
        return
    acc_v[0] = gvec[...]
    acc_v[1] = gvec[...]
    over_v = [
        pltpu.make_async_remote_copy(
            gvec, core_v.at[side], core_send.at[2, side], core_recv.at[2, side], device_id=sibling, device_id_type=MESH_ID
        )
        for side in range(2)
    ]
    for copy in over_v:
        copy.start()
    for copy in over_v:
        copy.wait_recv()
    tick()
    finish_halo()
    from_left = jnp.where(tensor > 0, halo_land[0].astype(F32), 0.0)
    from_right = jnp.where(tensor < 3, halo_land[1].astype(F32), 0.0)
    normed, rate = norm_parts(tok[...].astype(F32))
    total = grad_one[rows : 2 * rows, :] + from_left + from_right
    out_acc[...] = mid[...] + norm_pull(total, normed, rate, rows_ref[0:1, :])
    result_store = pltpu.make_async_copy(out_acc, result_hbm, out_sem.at[2])
    result_store.start()
    tick()
    for end in ends:
        end()
    over[0, 2].wait_send()
    over[1, 2].wait_send()
    for copy in over_v:
        copy.wait_send()
    result_store.wait()


def backward_rows(remote, tok, halo, cot, middle, act_two, act_t, wm, wa, rows_ref, units_ref, q, k, v, ctx, lse, segk_row, segk_col):
    rows, width = tok.shape
    groups, wide = wm.shape[0], wm.shape[-1]
    narrow = wa.shape[2]
    head_width = narrow // 4
    shape = jax.ShapeDtypeStruct
    vmem = pltpu.VMEM
    dma = lambda *dims: pltpu.SemaphoreType.DMA(dims)
    in_specs = [VMEM_SPEC, HBM_SPEC] + [HBM_SPEC] * 6 + [VMEM_SPEC] * 2 + [HBM_SPEC] * 4 + [VMEM_SPEC] * 3
    piece = width // SPLIT
    if remote:
        out_shape = (
            shape((rows, width), BF16),
            shape((piece, wide), F32),
            shape((piece, narrow), F32),
            shape((16, 128), F32),
            shape((rows, width), F32),
        )
        out_specs = (HBM_SPEC, VMEM_SPEC, VMEM_SPEC, VMEM_SPEC, HBM_SPEC)
    else:
        out_shape = (
            shape((rows, width), BF16),
            shape((groups, SPLIT, piece, wide), BF16),
            shape((groups, SPLIT, piece, narrow), BF16),
            shape((SPLIT, 16, 128), BF16),
            shape((2, rows, width), BF16),
            shape((rows, width), F32),
            shape((rows, width), F32),
        )
        out_specs = (HBM_SPEC,) * 7
    scratch = [
        vmem((rows, width), BF16),
        vmem((rows, width), BF16),
        vmem((width, rows), BF16),
        vmem((width, rows), BF16),
        vmem((rows, width), F32),
        vmem((rows, width), F32),
        vmem((rows, width), F32),
        vmem((rows, width), BF16),
        vmem((2, SPLIT, piece, wide), BF16),
        vmem((2, width, narrow), BF16),
        vmem((rows, head_width), BF16),
        vmem((3 * rows, head_width), BF16),
        vmem((3 * rows, head_width), BF16),
        vmem((rows, head_width), BF16),
        vmem((SPLIT, piece, wide), BF16),
        vmem((3 * rows, width), F32),
        vmem((3 * rows, head_width), F32),
        vmem((3 * rows, head_width), F32),
        vmem((head_width, rows), F32),
        vmem((head_width, 3 * rows), BF16),
        vmem((rows, head_width), BF16),
        vmem((VEC_ROWS, width), F32),
        vmem(units_ref.shape, F32),
        vmem((groups, 1, head_width), F32),
        vmem((groups, 1, head_width), F32),
        vmem((SPLIT, 16, 128), BF16),
        dma(3),
        dma(2),
        dma(2),
        dma(4),
        dma(5),
    ]
    params = dict(vmem_limit_bytes=VMEM_LIMIT)
    if remote:
        n = len(REDUCE_PARTS)
        sizes = ((piece, wide), (piece, narrow), (16, 128))
        slots = [4 * len(land_slots(p[0], 4)) for p in REDUCE_PARTS]
        scratch += [vmem((2, SPLIT) + size, BF16) for size in sizes]
        scratch += [vmem((2, SPLIT) + size, BF16) for size in sizes]
        scratch += [vmem((2, rows, width), BF16)]
        scratch += [vmem((slots[i], p[3], sizes[p[1]][1]), BF16) for i, p in enumerate(REDUCE_PARTS)]
        scratch += [dma(3, 2), dma(3, 2), dma(n, 4, 4), dma(n, max(slots)), dma(4), dma(2)]
        params.update(collective_id=1, has_side_effects=True)

    def kernel(*refs):
        ins, outs, rest = refs[:17], refs[17 : 17 + len(out_shape)], refs[17 + len(out_shape) :]
        if remote:
            outs = (outs[0], outs[1], outs[2], outs[3], outs[4], None, None)
        else:
            outs = (outs[0], None, None, None, outs[5], (outs[1], outs[2], outs[4], outs[3]), outs[6])
        backward_kernel(remote, *ins, *outs, *rest)

    return pl.pallas_call(
        kernel,
        out_shape=out_shape,
        in_specs=in_specs,
        out_specs=out_specs,
        scratch_shapes=scratch,
        compiler_params=pltpu.CompilerParams(**params),
        name="backward_rows",
    )(tok, halo, cot, middle, act_two, act_t.reshape(SPLIT, piece, 3 * rows), wm, wa, rows_ref, units_ref, q, k, v, ctx, lse, segk_row, segk_col)


def finish_kernel(piece, out_in, grad_in, sum_m, sum_a, sum_v, out, grad, *rest):
    *results, out_s, grad_s, m_s, a_s, v_s, sem, back_sem = rest
    pairs = ((out_in, out_s), (grad_in, grad_s), (sum_a, a_s), (sum_m, m_s), (sum_v, v_s))
    loads = [pltpu.make_async_copy(source, target, sem.at[i]) for i, (source, target) in enumerate(pairs)]
    for copy in loads:
        copy.start()
    stores = [pltpu.make_async_copy(out_s, out, back_sem.at[0]), pltpu.make_async_copy(grad_s, grad, back_sem.at[1])]
    for load, store in zip(loads[:2], stores):
        load.wait()
        store.start()
    for copy in loads[2:]:
        copy.wait()
    sum_m, sum_a, sum_v = m_s, a_s, v_s
    g_q, g_k, g_v, g_o, g_in, g_back, *lines = results
    head_width, units = g_q.shape[1], g_in.shape[1]
    total = sum_a[...]
    g_q[...] = total[:, :head_width]
    g_k[...] = total[:, head_width : 2 * head_width]
    g_v[...] = total[:, 2 * head_width : 3 * head_width]
    g_o[...] = total[:, 3 * head_width :].T
    g_in[...] = sum_m[:, :units]
    g_back[...] = sum_m[:, units:]
    for i in range(SHIFTS):
        lines[i][...] = sum_v[i : i + 1, :piece]
    for row in range(lines[SHIFTS].shape[1] // 128):
        lines[SHIFTS][:, row * 128 : (row + 1) * 128] = sum_v[SHIFTS + row : SHIFTS + row + 1, :]
    for copy in stores:
        copy.wait()


def finish_rows(output, grad_tokens, sum_m, sum_a, sum_v, unit_piece):
    piece, wide = sum_m.shape
    narrow = sum_a.shape[1]
    line = lambda n: jax.ShapeDtypeStruct((1, n), F32)
    shape = lambda *dims: jax.ShapeDtypeStruct(dims, F32)
    quarter = shape(piece, narrow // 4)
    half = shape(piece, wide // 2)
    return pl.pallas_call(
        functools.partial(finish_kernel, piece),
        out_shape=(
            jax.ShapeDtypeStruct(output.shape, output.dtype),
            jax.ShapeDtypeStruct(grad_tokens.shape, grad_tokens.dtype),
            quarter,
            quarter,
            quarter,
            shape(narrow // 4, piece),
            half,
            half,
        )
        + (line(piece),) * SHIFTS
        + (line(unit_piece),),
        in_specs=[pl.BlockSpec(memory_space=pltpu.HBM)] * 5,
        out_specs=(pl.BlockSpec(memory_space=pltpu.HBM),) * 2 + (VMEM_SPEC,) * (7 + SHIFTS),
        scratch_shapes=[
            pltpu.VMEM(output.shape, output.dtype),
            pltpu.VMEM(grad_tokens.shape, F32),
            pltpu.VMEM(sum_m.shape, F32),
            pltpu.VMEM(sum_a.shape, F32),
            pltpu.VMEM(sum_v.shape, F32),
            pltpu.SemaphoreType.DMA((5,)),
            pltpu.SemaphoreType.DMA((2,)),
        ],
        compiler_params=pltpu.CompilerParams(vmem_limit_bytes=VMEM_LIMIT),
        name="finish_rows",
    )(output, grad_tokens, sum_m, sum_a, sum_v)


def per_device(by_kernel, *args):
    (
        tokens,
        cotangent,
        segment_ids,
        ln1_gain,
        ln1_bias,
        w_query,
        query_bias,
        w_key,
        w_value,
        value_bias,
        w_out,
        out_bias,
        ln2_gain,
        ln2_bias,
        w_in,
        in_bias,
        w_back,
        back_bias,
    ) = args
    rows, width = tokens.shape
    n_dp, n_tensor = lax.axis_size("dp"), lax.axis_size("tensor")
    index = lax.axis_index("tensor")
    head_width = w_query.shape[1]
    units = w_in.shape[1]
    piece = ln1_gain.shape[0]
    unit_piece = in_bias.shape[0]

    vectors = (ln1_gain, ln1_bias, query_bias, value_bias, out_bias, ln2_gain, ln2_bias, back_bias)
    if by_kernel:
        lines = [vector.reshape(1, piece) for vector in vectors]
        sources = (w_in, w_back.T, w_query, w_key, w_value, w_out, *lines, in_bias.reshape(-1, 128))
        full_mlp, full_att, halo, *saved = forward_rows(True, tokens, segment_ids, units, *sources)
    else:
        shard_mlp = jnp.concatenate([w_in, w_back.T], axis=1)
        shard_att = jnp.concatenate([w_query, w_key, w_value, w_out.T], axis=1)
        edge = jnp.full((rows,), -1, jnp.int32)
        segs = jnp.concatenate([edge, segment_ids[0], edge])
        segs = lax.dynamic_slice_in_dim(segs, index * rows, 3 * rows)[None, :]
        shard_vec = jnp.concatenate([jnp.stack(vectors).reshape(-1), in_bias])
        full_mlp, full_att, full_vec, halo = gather_by_ops((shard_mlp, shard_att, shard_vec), tokens)
        flat = full_vec[0]
        rows8 = jnp.swapaxes(flat[:, : 8 * piece].reshape(n_dp, 8, piece), 0, 1).reshape(8, SPLIT, width // SPLIT)
        rows8 = jnp.pad(jnp.swapaxes(rows8, 0, 1), ((0, 0), (0, 0), (0, 128 - width // SPLIT)))
        unit_rows = flat[:, 8 * piece :].reshape(SPLIT, -1, 128)
        full_vec = jnp.concatenate([rows8, unit_rows], axis=1)
        full_vec = jnp.pad(full_vec, ((0, 0), (0, 16 - full_vec.shape[1]), (0, 0)))
        full_mlp = full_mlp.reshape(n_tensor, SPLIT, width // SPLIT, 2 * units)
        full_att = full_att.reshape(n_tensor, SPLIT, width // SPLIT, 4 * head_width)
        saved = forward_rows(False, tokens, segs, units, halo, full_att, full_vec)
    rows_vec, units_vec, segk_row, segk_col, lse, act_t, query, keys, values, context, middle, act_two = saved
    full_att = full_att.reshape(n_tensor, width, 4 * head_width)
    results = backward_rows(
        by_kernel, tokens, halo, cotangent, middle, act_two, act_t, full_mlp, full_att, rows_vec, units_vec, query, keys, values,
        context, lse, segk_row, segk_col,
    )
    if by_kernel:
        output, sum_mlp, sum_att, sum_vec, grad_tokens = results
        output, grad_tokens, g_wq, g_wk, g_wv, g_wo, g_win, g_wback, *vec = finish_rows(
            output, grad_tokens, sum_mlp, sum_att, sum_vec, unit_piece
        )
        vec = [line.reshape(-1) for line in vec]
    else:
        output, grad_mlp, grad_att, grad_vec, halo_rows, grad_own, grad_middle = results
        split = lambda array: array.reshape(n_tensor, n_dp, width // n_dp, array.shape[-1])
        rows8 = jnp.swapaxes(grad_vec[:, :8, : width // 8], 0, 1).reshape(8, n_dp, piece)
        unit_flat = grad_vec[:, 8 : 8 + unit_piece * n_dp // SPLIT // 128].reshape(n_dp, unit_piece)
        flat = jnp.concatenate([jnp.swapaxes(rows8, 0, 1).reshape(n_dp, 8 * piece), unit_flat], axis=1)
        flat = jnp.broadcast_to(flat[None], (n_tensor,) + flat.shape)
        sum_mlp, sum_att, sum_vec, halo_back = reduce_by_ops((split(grad_mlp), split(grad_att), flat), halo_rows)
        vec = [sum_vec[i * piece : (i + 1) * piece] for i in range(8)] + [sum_vec[8 * piece :]]
        from_left = jnp.where(index > 0, halo_back[0].astype(F32), 0.0)
        from_right = jnp.where(index < n_tensor - 1, halo_back[1].astype(F32), 0.0)
        norm_one, rate_one = norm_parts(tokens.astype(F32))
        grad_tokens = grad_middle + norm_pull(grad_own + from_left + from_right, norm_one, rate_one, rows_vec[0:1])
        g_wq, g_wk, g_wv = (sum_att[:, i * head_width : (i + 1) * head_width] for i in range(3))
        g_wo = sum_att[:, 3 * head_width :].T
        g_win, g_wback = sum_mlp[:, :units], sum_mlp[:, units:]
    g_ln1_gain, g_ln1_bias, g_q, g_v, g_o, g_ln2_gain, g_ln2_bias, g_b, g_i = vec
    return (
        output,
        grad_tokens,
        g_ln1_gain,
        g_ln1_bias,
        g_wq,
        g_q,
        g_wk,
        g_wv,
        g_v,
        g_wo,
        g_o,
        g_ln2_gain,
        g_ln2_bias,
        g_win,
        g_i,
        g_wback.T,
        g_b,
    )


def solution(mesh):
    by_kernel = mesh.shape["dp"] == 8 and mesh.shape["tensor"] == 4
    rows = P(("dp", "tensor"), None)
    line, first, second = P("dp"), P("dp", "tensor"), P("tensor", "dp")
    return jax.shard_map(
        functools.partial(per_device, by_kernel),
        mesh=mesh,
        in_specs=(rows, rows, P("dp", None), line, line, first, line, first, first, line, second, line, line, line, first, line, second, line),
        out_specs=(rows, rows, line, line, first, line, first, first, line, second, line, line, line, first, line, second, line),
        check_vma=False,
    )
```

```python
import functools

import jax
import jax.numpy as jnp
from jax import lax
from jax.experimental import pallas as pl
from jax.experimental.pallas import tpu as pltpu
from jax.sharding import PartitionSpec as P

HEAD_DIM = 64
EPSILON = 1e-12
MASKED = -1000000000.0
MESH_ID = pl.DeviceIdType.MESH
F32 = jnp.float32
BF16 = jnp.bfloat16

NN = (((1,), (0,)), ((), ()))
NT = (((1,), (1,)), ((), ()))
TN = (((0,), (0,)), ((), ()))


def mxu(left, right, dims):
    return lax.dot_general(left, right, dims, preferred_element_type=F32)


def position():
    dp = lax.axis_index("dp")
    tensor = lax.axis_index("tensor")
    return dp // 2, dp % 2, tensor // 2, tensor % 2


def device(z, y, x, core):
    return (z * 2 + y, x * 2 + core)


def offsets(depth):
    found = [(dz, dy, dx) for dz in range(1 - depth, depth) for dy in range(2) for dx in range(2)]
    return sorted(found, key=lambda item: abs(item[0]) + item[1] + item[2])


def level(route, offset):
    dims = dict(zip("zyx", offset))
    last = -1
    for place, name in enumerate(route):
        if dims[name] != 0:
            last = place
    return last


def when(condition, action):
    if condition is True:
        action()
    else:
        pl.when(condition)(action)


def meet_neighbours(depth):
    z, y, x, core = position()
    dp, tensor = lax.axis_index("dp"), lax.axis_index("tensor")
    barrier = pltpu.get_barrier_semaphore()

    def signal(target):
        pl.semaphore_signal(barrier, inc=1, device_id=target, device_id_type=MESH_ID)

    signal(device(z, y, x, 1 - core))
    signal(device(z, y, 1 - x, core))
    signal(device(z, 1 - y, x, core))
    pl.when(z > 0)(lambda: signal(device(z - 1, y, x, core)))
    pl.when(z < depth - 1)(lambda: signal(device(z + 1, y, x, core)))
    middle = (tensor == 1) | (tensor == 2)
    pl.when(middle)(lambda: signal((dp, 3 - tensor)))
    as_int = lambda flag: flag.astype(jnp.int32)
    return lambda: pl.semaphore_wait(barrier, 3 + as_int(z > 0) + as_int(z < depth - 1) + as_int(middle))


def tree_sends(route, offset, depth):
    z, y, x, core = position()
    dz = offset[0]
    lev = level(route, offset)
    sends = []
    for place, name in enumerate(route):
        if name == "z":
            if place < lev:
                continue
            if place > lev or dz < 0:
                sends.append((0, device(jnp.minimum(z + 1, depth - 1), y, x, core), z < depth - 1, 0))
            if place > lev or dz > 0:
                sends.append((1, device(jnp.maximum(z - 1, 0), y, x, core), z > 0, 0))
        elif place > lev:
            if name == "y":
                sends.append((2, device(z, 1 - y, x, core), True, 2))
            else:
                sends.append((3, device(z, y, 1 - x, core), True, 1))
    return sends


def tree_parent(route, offset):
    z, y, x, core = position()
    dz, dy, dx = offset
    name = route[level(route, offset)]
    if name == "z":
        if dz < 0:
            return 0, device(z - 1, y, x, core)
        return 1, device(z + 1, y, x, core)
    if name == "y":
        return 2, device(z, 1 - y, x, core)
    return 3, device(z, y, 1 - x, core)


def exchange_halo(rows_left, rows_right, halo, halo_send, halo_recv, own_left, own_right):
    dp, tensor = lax.axis_index("dp"), lax.axis_index("tensor")
    has_left, has_right = tensor > 0, tensor < 3
    to_right = pltpu.make_async_remote_copy(
        rows_right, halo.at[0], halo_send.at[0], halo_recv.at[0], device_id=(dp, jnp.minimum(tensor + 1, 3)), device_id_type=MESH_ID
    )
    to_left = pltpu.make_async_remote_copy(
        rows_left, halo.at[1], halo_send.at[1], halo_recv.at[1], device_id=(dp, jnp.maximum(tensor - 1, 0)), device_id_type=MESH_ID
    )
    fill_left = pltpu.make_async_copy(own_left, halo.at[0], halo_send.at[2])
    fill_right = pltpu.make_async_copy(own_right, halo.at[1], halo_send.at[3])
    pl.when(has_right)(lambda: to_right.start())
    pl.when(has_left)(lambda: to_left.start())
    pl.when(~has_left)(lambda: fill_left.start())
    pl.when(~has_right)(lambda: fill_right.start())

    def finish():
        pl.when(has_right)(lambda: to_right.wait_send())
        pl.when(has_left)(lambda: to_left.wait_send())
        pl.when(has_left)(lambda: to_right.wait_recv())
        pl.when(has_right)(lambda: to_left.wait_recv())
        pl.when(~has_left)(lambda: fill_left.wait())
        pl.when(~has_right)(lambda: fill_right.wait())

    return finish


def gather_events(parts, depth, srcs, outs, send_sem, recv_sem, core_send, core_recv):
    z, y, x, core = position()
    sibling = device(z, y, x, 1 - core)
    events, backs, ends = {}, {}, []

    def piece(part, offset, owner_core):
        dz, dy, dx = offset
        _, which, begin, size = parts[part]
        oy = 1 - y if dy else y
        ox = 1 - x if dx else x
        return outs[which].at[ox * 2 + owner_core, (z + dz) * 2 + oy, pl.ds(begin, size)]

    for number, offset in enumerate(offsets(depth)):
        for part, (route, which, begin, size) in enumerate(parts):
            dz, dy, dx = offset
            mine = offset == (0, 0, 0)
            target = piece(part, offset, core)
            block = srcs[which].at[pl.ds(begin, size)] if mine else target
            zi, bi = z + dz, dy * 2 + dx
            valid = True if dz == 0 else ((z + dz >= 0) & (z + dz <= depth - 1))
            sends = []
            for way, to, ok, shift in tree_sends(route, offset, depth):
                copy = pltpu.make_async_remote_copy(
                    block, target, send_sem.at[part, way, zi, bi], recv_sem.at[part, zi, bi + shift], device_id=to, device_id_type=MESH_ID
                )
                sends.append((copy, ok))
            arrival = pltpu.make_async_remote_copy(
                block, target, send_sem.at[part, 0, 0, 0], recv_sem.at[part, zi, bi], device_id=sibling, device_id_type=MESH_ID
            )
            over = pltpu.make_async_remote_copy(
                block, target, core_send.at[part, zi, bi], core_recv.at[part, zi, bi], device_id=sibling, device_id_type=MESH_ID
            )
            other = piece(part, offset, 1 - core)
            back = pltpu.make_async_remote_copy(
                other, other, core_send.at[part, zi, bi], core_recv.at[part, zi, bi], device_id=sibling, device_id_type=MESH_ID
            )

            def arrive(sends=sends, arrival=arrival, over=over, mine=mine):
                if not mine:
                    arrival.wait_recv()
                for copy, ok in sends:
                    when(ok, lambda copy=copy: copy.start())
                over.start()

            def finish(sends=sends, over=over):
                for copy, ok in sends:
                    when(ok, lambda copy=copy: copy.wait_send())
                over.wait_send()

            events[part * 100 + number] = lambda valid=valid, arrive=arrive: when(valid, arrive)
            backs[part * 100 + number] = lambda valid=valid, back=back: when(valid, lambda: back.wait_recv())
            ends.append(lambda valid=valid, finish=finish: when(valid, finish))
    return events, backs, ends


GATHER_PARTS = (
    ("xzy", 1, 0, 48),
    ("yzx", 1, 48, 48),
    ("zyx", 0, 0, 64),
    ("xzy", 0, 64, 32),
)

GATHER_STEPS = (
    (0, 100),
    (1, 101, 3, 103, 4, 104),
    (),
    (),
    (5, 7, 110, 10, 105, 11, 2, 107, 14, 12, 111, 102, 112, 118, 18, 19, 106, 6, 21, 108, 8, 114, 9, 109, 119, 25, 200, 300, 125, 116, 13, 120, 15, 121),
    (113, 16, 17, 124),
    (115, 117),
    (122, 123, 203, 204),
    (201, 303, 304),
    (20, 126, 301, 202, 22, 23, 24),
    (127, 302),
    (),
    (205, 210, 211, 208),
    (26, 305, 311, 27),
    (207, 309),
    (306, 209, 310),
    (212,),
    (206, 307, 312, 219),
    (308, 313, 319),
    (317,),
    (213, 214, 218, 320),
    (220, 324),
    (314, 216, 217, 318, 224, 225),
    (316, 221, 325),
    (315, 321),
    (215, 322, 323, 327, 326, 227, 226, 222, 223),
)


def gather_by_ops(shards, tokens):
    full = []
    for shard in shards:
        over_dp = lax.all_gather(shard, "dp", axis=0, tiled=False)
        full.append(lax.all_gather(over_dp, "tensor", axis=0, tiled=False))
    return tuple(full) + (halo_by_ops(tokens, tokens),)


def halo_by_ops(rows_left, rows_right):
    count = lax.axis_size("tensor")
    from_left = lax.ppermute(rows_right, "tensor", [(i, i + 1) for i in range(count - 1)])
    from_right = lax.ppermute(rows_left, "tensor", [(i, i - 1) for i in range(1, count)])
    return jnp.stack([from_left, from_right])


def reduce_by_ops(grads, halo_rows):
    sums = []
    for grad in grads:
        over_tensor = lax.psum_scatter(grad, "tensor", scatter_dimension=0, tiled=False)
        sums.append(lax.psum_scatter(over_tensor, "dp", scatter_dimension=0, tiled=False).astype(F32))
    return tuple(sums) + (halo_by_ops(halo_rows[0], halo_rows[1]),)


def norm_parts(values):
    center = values - jnp.mean(values, axis=-1, keepdims=True)
    rate = lax.rsqrt(jnp.mean(center * center, axis=-1, keepdims=True) + EPSILON)
    return center * rate, rate


def norm_pull(grad, normed, rate, gain):
    scaled = grad * gain
    return rate * (
        scaled
        - jnp.mean(scaled, axis=-1, keepdims=True)
        - normed * jnp.mean(scaled * normed, axis=-1, keepdims=True)
    )


def head_mask(head):
    lane = lax.broadcasted_iota(jnp.int32, (1, 3 * HEAD_DIM), 1)
    return (lane >= head * HEAD_DIM) & (lane < (head + 1) * HEAD_DIM)


QB = 256
UNITS = 768
VMEM_LIMIT = 63 * 1024 * 1024
VEC_ROWS = 16
SPLIT = 8
SHIFTS = 8
VMEM_SPEC = pl.BlockSpec(memory_space=pltpu.VMEM)
HBM_SPEC = pl.BlockSpec(memory_space=pl.ANY)


class Ticker:
    def __init__(self, steps, table):
        self.steps, self.table, self.point = steps, table, 0

    def __call__(self):
        if self.steps:
            for number in self.table[self.point]:
                self.steps[number]()
        self.point += 1


def unpack_vectors(vec_ref, rows_ref, units_ref, n_dp):
    width, groups = rows_ref.shape[1], units_ref.shape[0]
    piece, unit_rows = width // n_dp, units_ref.shape[2] * groups // n_dp // 128
    pieces = [vec_ref[dp].astype(F32) for dp in range(n_dp)]
    rows_ref[...] = jnp.concatenate([item[:, :piece] for item in pieces], axis=1)
    lines = [item[SHIFTS + row : SHIFTS + row + 1, :] for item in pieces for row in range(unit_rows)]
    per_group = len(lines) // groups
    for group in range(groups):
        units_ref[group] = jnp.concatenate(lines[group * per_group : (group + 1) * per_group], axis=1)


def pack_vectors(rows_ref, units_ref, vec_ref, n_dp):
    width, groups = rows_ref.shape[1], units_ref.shape[0]
    piece, unit_rows = width // n_dp, units_ref.shape[2] * groups // n_dp // 128
    vec_ref[...] = jnp.zeros_like(vec_ref)
    for dp in range(n_dp):
        vec_ref[dp, 0:SHIFTS, 0:piece] = rows_ref[0:SHIFTS, dp * piece : (dp + 1) * piece].astype(BF16)
        for row in range(unit_rows):
            begin = (dp * unit_rows + row) * 128
            group, lane = begin // units_ref.shape[2], begin % units_ref.shape[2]
            vec_ref[dp, SHIFTS + row : SHIFTS + row + 1, :] = units_ref[group, :, lane : lane + 128].astype(BF16)


def attend_block(q, k, v, same):
    total = jnp.zeros(q.shape, F32)
    logs = []
    for head in range(q.shape[1] // HEAD_DIM):
        mask = head_mask(head)
        raw = mxu(jnp.where(mask, q, jnp.zeros_like(q)), k, NT)
        scores = jnp.where(same, raw, MASKED)
        top = jnp.max(scores, axis=1, keepdims=True)
        expo = jnp.exp(scores - top)
        denom = jnp.sum(expo, axis=1, keepdims=True)
        part = mxu(expo.astype(BF16), v, NN)
        total = jnp.where(mask, part / denom, total)
        logs.append(top + jnp.log(denom))
    return total.astype(BF16), logs


def forward_kernel(remote, *refs):
    if remote:
        tok, segs, w_in, w_back, w_query, w_key, w_value, w_out = refs[:8]
        lines, unit_line = refs[8:16], refs[16]
        full_m, full_a, halo_hbm = refs[17:20]
        refs = refs[20:]
    else:
        tok, segs, halo, wa, vec = refs[:5]
        refs = refs[5:]
    rows_ref, units_ref, segk, segcol, lse, *stores_hbm = refs[:12]
    act, attn, logs_ref, qshift, act_t, q, k, v, ctx, middle, act_two, store_sem = refs[12:24]
    if remote:
        halo, wa, vec, shard_m, shard_a, shard_v, segs_all = refs[24:31]
        send_sem, recv_sem, core_send, core_recv, own_sem, vec_send, vec_recv, halo_send, halo_recv = refs[31:]
    rows, width = tok.shape
    groups = wa.shape[0]
    head_width = q.shape[2]
    depth = 4
    tick = Ticker(None, None)
    order = list(range(groups))
    logs_ref[...] = jnp.zeros_like(logs_ref)
    if remote:
        z, y, x, core = position()
        dp, tensor = lax.axis_index("dp"), lax.axis_index("tensor")
        order = [x * 2 + core, x * 2 + 1 - core, (1 - x) * 2 + core, (1 - x) * 2 + 1 - core]
        peers = [lax.rem(dp + shift, SPLIT) for shift in range(1, SPLIT)]
        barrier = pltpu.get_barrier_semaphore()
        middle_pair = (tensor == 1) | (tensor == 2)

        def signal(target):
            pl.semaphore_signal(barrier, inc=1, device_id=target, device_id_type=MESH_ID)

        for peer in peers:
            signal((peer, tensor))
        signal(device(z, y, x, 1 - core))
        signal(device(z, y, 1 - x, core))
        pl.when(middle_pair)(lambda: signal((dp, 3 - tensor)))
        stacked = jnp.concatenate([line[...].astype(F32) for line in lines], axis=0)
        padding = jnp.zeros((SHIFTS, 128 - stacked.shape[1]), F32)
        tail = jnp.zeros((16 - SHIFTS - unit_line.shape[0], 128), F32)
        shard_v[...] = jnp.concatenate(
            [jnp.concatenate([stacked, padding], axis=1), unit_line[...].astype(F32), tail], axis=0
        ).astype(BF16)
        shard_a[...] = jnp.concatenate([w_query[...], w_key[...], w_value[...], w_out[...].T], axis=1)
        shard_m[:, : w_in.shape[1]] = w_in[...]
        shard_m[:, w_in.shape[1] :] = w_back[...]
        edge = jnp.full((1, rows), -1, jnp.int32)
        segs_all[...] = jnp.concatenate([edge, segs[...], edge], axis=1)
        pl.semaphore_wait(barrier, SPLIT + 1 + middle_pair.astype(jnp.int32))
        own = [
            pltpu.make_async_copy(shard_v, vec.at[dp], own_sem.at[0]),
            pltpu.make_async_copy(shard_a, wa.at[tensor, dp], own_sem.at[1]),
            pltpu.make_async_copy(shard_m, full_m.at[tensor, dp], own_sem.at[2]),
        ]
        vec_copies = [
            pltpu.make_async_remote_copy(
                shard_v, vec.at[dp], vec_send.at[i], vec_recv.at[i], device_id=(peer, tensor), device_id_type=MESH_ID
            )
            for i, peer in enumerate(peers)
        ]
        for copy in vec_copies:
            copy.start()
        for copy in own:
            copy.start()
        finish_halo = exchange_halo(tok, tok, halo, halo_send, halo_recv, tok, tok)
        events, backs, ends = gather_events(GATHER_PARTS, depth, (shard_m, shard_a), (full_m, wa), send_sem, recv_sem, core_send, core_recv)
        tick = Ticker(events, GATHER_STEPS)
        tick()
        for i in range(SPLIT - 1):
            source = lax.rem(dp + SPLIT - 1 - i, SPLIT)
            pltpu.make_async_remote_copy(
                vec.at[source], vec.at[source], vec_send.at[i], vec_recv.at[i], device_id=(dp, 3 - tensor), device_id_type=MESH_ID
            ).wait_recv()
        own[0].wait()

    def wait_backs(array, dx):
        if remote:
            for key, step in backs.items():
                part, number = key // 100, key % 100
                if GATHER_PARTS[part][1] == array and (dx is None or offsets(depth)[number][2] == dx):
                    step()

    if remote:
        segk[...] = segs_all[:, pl.ds(pl.multiple_of(tensor * rows, rows), 3 * rows)]
    else:
        segk[...] = segs[...]
    segcol[...] = jnp.broadcast_to(segk[...], (8, 3 * rows)).T
    unpack_vectors(vec, rows_ref, units_ref, SPLIT)
    shifts = rows_ref[0:SHIFTS, :]
    for group in range(groups):
        lanes = slice(group * head_width, (group + 1) * head_width)
        qshift[group] = shifts[:, lanes]
    tick()
    gain, shift = rows_ref[0:1, :], rows_ref[1:2, :]
    for part in (1, 0, 2):
        if remote and part == 0:
            finish_halo()
        source = tok if part == 1 else halo.at[part // 2]
        normed, _ = norm_parts(source[...].astype(F32))
        act[part * rows : (part + 1) * rows, :] = (normed * gain + shift).astype(BF16)
        tick()
    act_t[...] = act[...].T
    stores = [pltpu.make_async_copy(act_t, stores_hbm[0], store_sem.at[0])]
    stores[0].start()
    if remote:
        halo_copy = pltpu.make_async_copy(halo, halo_hbm, own_sem.at[0])
        halo_copy.start()
        own[1].wait()
    for s in range(groups):
        t = order[s]
        if s % 2 == 1:
            wait_backs(1, s // 2)
        if remote and s == groups - 1:
            att_copy = pltpu.make_async_copy(wa, full_a, own_sem.at[1])
            att_copy.start()
        cut = lambda i: wa[t, :, :, i * head_width : (i + 1) * head_width].reshape(width, head_width)
        own_rows = act[rows : 2 * rows, :]
        query = (mxu(own_rows, cut(0), NN) + qshift[t, 2:3, :]).astype(BF16)
        q[t] = query * jnp.asarray(HEAD_DIM**-0.5, BF16)
        k[t] = mxu(act[...], cut(1), NN).astype(BF16)
        tick()
        v[t] = (mxu(act[...], cut(2), NN) + qshift[t, 3:4, :]).astype(BF16)
        tick()
        band = QB + 2 * rows
        for block in range(rows // QB):
            here, keys = pl.ds(block * QB, QB), pl.ds(block * QB, band)
            same = segcol[pl.ds(rows + block * QB, QB), 0:1] == segk[:, keys]
            result, logs = attend_block(q[t, here, :], k[t, keys, :], v[t, keys, :], same)
            ctx[t, here, :] = result
            for head, value in enumerate(logs):
                logs_ref[here, head : head + 1] = value
            tick()
        lse[t] = logs_ref[...].T[0 : lse.shape[1], :]
        part = mxu(ctx[t], cut(3), NT)
        if s == 0:
            attn[...] = part
        else:
            attn[...] += part
        for i, source in enumerate((q, k, v, ctx)):
            stores.append(pltpu.make_async_copy(source.at[t], stores_hbm[1 + i].at[t], store_sem.at[1 + 4 * s + i]))
            stores[-1].start()
        tick()
    total = tok[...].astype(F32) + attn[...] + rows_ref[4:5, :]
    middle[...] = total
    normed, _ = norm_parts(total)
    act_two[...] = (normed * rows_ref[5:6, :] + rows_ref[6:7, :]).astype(BF16)
    for i, source in enumerate((middle, act_two)):
        stores.append(pltpu.make_async_copy(source, stores_hbm[5 + i], store_sem.at[1 + 4 * groups + i]))
        stores[-1].start()
    tick()
    for copy in stores:
        copy.wait()
    if remote:
        wait_backs(0, None)
        own[2].wait()
        for end in ends:
            end()
        for copy in vec_copies:
            copy.wait_send()
        halo_copy.wait()
        att_copy.wait()


def forward_rows(remote, tok, segs, units, *sources):
    rows, width = tok.shape
    groups, head_width = 4, width // 4
    piece = width // SPLIT
    shape = jax.ShapeDtypeStruct
    vmem = pltpu.VMEM
    dma = lambda *dims: pltpu.SemaphoreType.DMA(dims)
    saved = (
        ((width, 3 * rows), BF16),
        ((groups, rows, head_width), BF16),
        ((groups, 3 * rows, head_width), BF16),
        ((groups, 3 * rows, head_width), BF16),
        ((groups, rows, head_width), BF16),
        ((rows, width), F32),
        ((rows, width), BF16),
    )
    out_shape = (
        shape((VEC_ROWS, width), F32),
        shape((groups, 1, units), F32),
        shape((1, 3 * rows), jnp.int32),
        shape((3 * rows, 8), jnp.int32),
        shape((groups, 8, rows), F32),
    ) + tuple(shape(*item) for item in saved)
    out_specs = (VMEM_SPEC,) * 5 + (HBM_SPEC,) * 7
    scratch = [
        vmem((3 * rows, width), BF16),
        vmem((rows, width), F32),
        vmem((rows, 128), F32),
        vmem((groups, SHIFTS, head_width), F32),
    ]
    scratch += [vmem(*item) for item in saved] + [dma(3 + 4 * groups)]
    params = dict(vmem_limit_bytes=VMEM_LIMIT)
    if remote:
        n = len(GATHER_PARTS)
        wide, narrow = (piece, 2 * units), (piece, 4 * head_width)
        out_shape = (
            shape((groups, SPLIT) + wide, BF16),
            shape((groups, SPLIT) + narrow, BF16),
            shape((2, rows, width), BF16),
        ) + out_shape
        out_specs = (HBM_SPEC,) * 3 + out_specs
        scratch += [
            vmem((2, rows, width), BF16),
            vmem((groups, SPLIT) + narrow, BF16),
            vmem((SPLIT, 16, 128), BF16),
            vmem(wide, BF16),
            vmem(narrow, BF16),
            vmem((16, 128), BF16),
            vmem((1, segs.shape[1] + 2 * rows), jnp.int32),
        ]
        scratch += [dma(n, 4, 4, 4), dma(n, 4, 4), dma(n, 4, 4), dma(n, 4, 4), dma(3), dma(SPLIT - 1), dma(SPLIT - 1), dma(4), dma(2)]
        params.update(collective_id=0, has_side_effects=True)
    return pl.pallas_call(
        functools.partial(forward_kernel, remote),
        out_shape=out_shape,
        in_specs=[VMEM_SPEC] * (2 + len(sources)),
        out_specs=out_specs,
        scratch_shapes=scratch,
        compiler_params=pltpu.CompilerParams(**params),
        name="forward_rows",
    )(tok, segs, *sources)


def mlp_block(act, cot, act_t, cot_t, win, wback, bias, out, gact, gbias):
    pre = mxu(act[...], win, NN) + bias
    phi = 0.5 + 0.5 * lax.erf(pre * (0.5**0.5))
    hidden = (pre * phi).astype(BF16)
    slope = phi + pre * (jnp.exp(-0.5 * pre * pre) * 0.3989422804014327)
    grad_pre = mxu(cot[...], wback, NN) * slope
    low = grad_pre.astype(BF16)
    gbias[...] = jnp.sum(grad_pre, axis=0, keepdims=True)
    out[...] += mxu(hidden, wback, NT)
    gact[...] += mxu(low, win, NT)
    return mxu(act_t[...], low, NN).astype(BF16), mxu(cot_t[...], hidden, NN).astype(BF16)


def pull_group(q, k, v, do, ctx, lse, segq_row, segk_col, kt, dk_acc, dv_acc, dq_acc, tick):
    rows, width = q.shape
    heads = width // HEAD_DIM
    kt[...] = k[...].T
    dk_acc[...] = jnp.zeros_like(dk_acc)
    dv_acc[...] = jnp.zeros_like(dv_acc)
    dq_acc[...] = jnp.zeros_like(dq_acc)
    grad = do[...]
    product = grad.astype(F32) * ctx[...].astype(F32)
    row = lax.broadcasted_iota(jnp.int32, (8, width), 0)
    lane = lax.broadcasted_iota(jnp.int32, (8, width), 1)
    pick = jnp.where((lane >= row * HEAD_DIM) & (lane < (row + 1) * HEAD_DIM), 1.0, 0.0)
    delta_all = lax.dot_general(pick, product, NT, precision=lax.Precision.HIGHEST, preferred_element_type=F32)
    for block in range(rows // QB):
        here = pl.ds(block * QB, QB)
        span = slice(block * QB, (block + 1) * QB)
        segq = segq_row[:, here]
        query = q[here, :]
        q_stack = jnp.concatenate([jnp.where(head_mask(h), query, jnp.zeros_like(query)) for h in range(heads)], axis=0)
        do_stack = jnp.concatenate([jnp.where(head_mask(h), grad[span], jnp.zeros_like(query)) for h in range(heads)], axis=0)

        def body(tile, carry):
            keys = pl.ds(pl.multiple_of(block * QB + tile * QB, QB), QB)
            same = segk_col[keys, 0:1] == segq
            raw = mxu(k[keys, :], q_stack, NT)
            grad_weights = mxu(v[keys, :], do_stack, NT)
            dv_part = dk_part = None
            for head in range(heads):
                part = slice(head * QB, (head + 1) * QB)
                probs = jnp.exp(jnp.where(same, raw[:, part], MASKED) - lse[head : head + 1, here])
                grad_raw = (probs * (grad_weights[:, part] - delta_all[head : head + 1, span])).astype(BF16)
                low = probs.astype(BF16)
                spot = slice(head * QB, (head + 1) * QB)
                one, two = mxu(low, do_stack[spot], NN), mxu(grad_raw, q_stack[spot], NN)
                dv_part = one if head == 0 else dv_part + one
                dk_part = two if head == 0 else dk_part + two
                lanes = pl.ds(head * HEAD_DIM, HEAD_DIM)
                dq_acc[lanes, here] += mxu(kt[lanes, keys], grad_raw, NN)
            dv_acc[keys, :] += dv_part
            dk_acc[keys, :] += dk_part
            return carry

        lax.fori_loop(0, (QB + 2 * rows) // QB, body, 0, unroll=True)
        tick()


def land_slots(route, depth):
    ways = []
    for offset in offsets(depth):
        lev = level(route, offset)
        dz, dy, dx = offset
        for place, name in enumerate(route):
            if name == "z":
                if place < lev:
                    continue
                if place > lev or dz < 0:
                    ways.append((0, dy * 2 + dx))
                if place > lev or dz > 0:
                    ways.append((1, dy * 2 + dx))
            elif place > lev:
                ways.append((2 if name == "y" else 3, dy * 2 + dx))
    ways = sorted(set(ways))
    return {way: number * depth for number, way in enumerate(ways)}


def reduce_events(parts, depth, accs, cores, lands, outs, send_sem, recv_sem):
    z, y, x, core = position()
    sibling = device(z, y, x, 1 - core)
    events, ends = {}, []
    for offset in reversed(offsets(depth)):
        for part, (route, which, begin, size) in enumerate(parts):
            slots = land_slots(route, depth)
            dz, dy, dx = offset
            mine = offset == (0, 0, 0)
            zi, bi = z + dz, dy * 2 + dx
            valid = True if dz == 0 else ((z + dz >= 0) & (z + dz <= depth - 1))
            oy = 1 - y if dy else y
            ox = 1 - x if dx else x
            rows = pl.ds(begin, size)
            spot = zi * 2 + oy
            own = accs[which].at[ox, spot, rows]
            other = cores[which].at[ox, spot, rows]
            children = []
            for way, to, ok, shift in tree_sends(route, offset, depth):
                slot = slots[way, bi] + zi
                land = lands[part].at[slot]
                wait = pltpu.make_async_remote_copy(
                    land, land, send_sem.at[part, 0, 0], recv_sem.at[part, slot], device_id=sibling, device_id_type=MESH_ID
                )
                children.append((land, wait, ok))
            send = None
            if not mine:
                way, to = tree_parent(route, offset)
                slot = slots[way, bi - {0: 0, 1: 0, 2: 2, 3: 1}[way]] + zi
                send = pltpu.make_async_remote_copy(
                    own, lands[part].at[slot], send_sem.at[part, zi, bi], recv_sem.at[part, slot], device_id=to, device_id_type=MESH_ID
                )

            def work(own=own, other=other, children=children, send=send, which=which, rows=rows):
                for land, wait, ok in children:
                    when(ok, lambda wait=wait: wait.wait_recv())
                total = own[...].astype(F32) + other[...].astype(F32)
                for land, wait, ok in children:
                    term = land[...].astype(F32)
                    total = total + (term if ok is True else jnp.where(ok, term, 0.0))
                if send is None:
                    outs[which][rows] = total
                else:
                    own[...] = total.astype(BF16)
                    send.start()

            events[part * 100 + offsets(depth).index(offset)] = lambda valid=valid, work=work: when(valid, work)
            if send is not None:
                ends.append(lambda valid=valid, send=send: when(valid, lambda: send.wait_send()))
    return events, ends


REDUCE_PARTS = (
    ("zxy", 0, 0, 96),
    ("zyx", 1, 0, 96),
    ("zxy", 2, 0, 16),
)

REDUCE_STEPS = (
    (),
    (27, 26, 23, 22, 16, 15),
    (8,),
    (24, 20, 25, 21, 18, 14),
    (10, 7, 3),
    (17, 13),
    (),
    (9, 6),
    (),
    (),
    (),
    (2,),
    (),
    (19, 12, 127, 126, 124, 123),
    (122, 120, 117, 116, 115, 113),
    (109, 108, 106, 102),
    (),
    (11, 5),
    (),
    (),
    (),
    (),
    (4, 1),
    (125, 121, 118, 114, 110, 107),
    (),
    (119, 112, 227, 226, 223, 222, 216, 215, 208, 225, 221, 218, 214, 210, 207, 203, 0, 103),
    (111, 105, 224, 217, 209, 219, 220, 213, 206, 202, 212, 104, 205, 101, 211, 201, 204, 100, 200),
)


def backward_kernel(remote, *refs):
    (tok, halo, cot_hbm, mid_hbm, two_hbm, act_t_hbm, wm_hbm, wa_hbm, rows_ref, units_ref) = refs[:10]
    (q_hbm, k_hbm, v_hbm, ctx_hbm, lse, segk_row, segk_col) = refs[10:17]
    output_hbm, sum_m, sum_a, sum_v, result_hbm, rest_hbm, back_hbm = refs[17:24]
    (cot, two, cot_t, two_t, mid, out_acc, gact, low_ref, wm, wa, q, k, v, ctx, stage_m) = refs[24:39]
    (grad_one, dk_acc, dv_acc, dq_acc, kt, do_ref, sums, gunits, qsum, vsum, gvec) = refs[39:50]
    (in_sem, wm_sem, wa_sem, group_sem, out_sem) = refs[50:55]
    rows, width = tok.shape
    groups = wm_hbm.shape[0]
    head_width = q.shape[1]
    units = units_ref.shape[2]
    segq_row = segk_row.at[:, pl.ds(rows, rows)]
    narrow = wa.shape[2]
    stage_a = wm.at[1, :, :, pl.ds(0, narrow)]
    depth = 4
    tick = Ticker(None, None)
    if remote:
        count = len(REDUCE_PARTS)
        (acc_m, acc_a, acc_v, core_m, core_a, core_v, halo_land) = refs[55:62]
        lands = refs[62 : 62 + count]
        core_send, core_recv, send_sem, recv_sem, halo_send, halo_recv = refs[62 + count :]
        z, y, x, core = position()
        dp, tensor = lax.axis_index("dp"), lax.axis_index("tensor")
        sibling = device(z, y, x, 1 - core)
        order = [((1 - x) * 2 + 1 - core, 1 - x, False), ((1 - x) * 2 + core, 1 - x, True), (x * 2 + 1 - core, x, False), (x * 2 + core, x, True)]
        events, ends = reduce_events(
            REDUCE_PARTS, depth, (acc_m, acc_a, acc_v), (core_m, core_a, core_v), lands, (sum_m, sum_a, sum_v), send_sem, recv_sem
        )
        over = {}
        for which, (stage, cores) in enumerate(((stage_m, core_m), (stage_a, core_a))):
            for step, side in ((0, 1 - x), (2, x)):
                over[which, step] = pltpu.make_async_remote_copy(
                    stage, cores.at[side], core_send.at[which, step // 2], core_recv.at[which, step // 2], device_id=sibling, device_id_type=MESH_ID
                )
        wait_neighbours = meet_neighbours(depth)
        tick = Ticker(events, REDUCE_STEPS)
    else:
        order = [(t, 0, False) for t in range(groups)]
    t_of = [item[0] for item in order]

    load = lambda source, target, number: pltpu.make_async_copy(source, target, in_sem.at[number])
    inputs = [load(cot_hbm, cot, 0), load(two_hbm, two, 1), load(mid_hbm, mid, 2)]
    for copy in inputs:
        copy.start()
    wm_loads = [pltpu.make_async_copy(wm_hbm.at[t_of[s]], wm.at[s % 2], wm_sem.at[s % 2]) for s in range(groups)]
    wa_loads = [pltpu.make_async_copy(wa_hbm.at[t_of[s]], wa.at[s % 2], wa_sem.at[s % 2]) for s in range(groups)]
    group_loads = [
        [
            pltpu.make_async_copy(source.at[t_of[s]], target, group_sem.at[i])
            for i, (source, target) in enumerate(((q_hbm, q), (k_hbm, k), (v_hbm, v), (ctx_hbm, ctx)))
        ]
        for s in range(groups)
    ]
    wm_loads[0].start()
    wm_loads[1].start()
    wa_loads[0].start()
    for copy in group_loads[0]:
        copy.start()
    for copy in inputs:
        copy.wait()
    two_t[...] = two[...].T
    cot_t[...] = cot[...].T
    out_acc[...] = jnp.zeros_like(out_acc)
    gact[...] = jnp.zeros_like(gact)
    sums[...] = jnp.zeros_like(sums)

    def block_rows(value):
        return value.reshape(SPLIT, width // SPLIT, value.shape[1])

    for s in range(groups):
        t, side, mine = order[s]
        slot = s % 2
        wm_loads[s].wait()
        target = acc_m.at[side] if mine else stage_m
        if remote and s == 2:
            over[0, 0].wait_send()

        def body(block, carry):
            here = pl.ds(pl.multiple_of(block * UNITS, UNITS), UNITS)
            there = pl.ds(pl.multiple_of(units + block * UNITS, UNITS), UNITS)
            gin, gback = mlp_block(
                two, cot, two_t, cot_t, wm[slot, :, :, here].reshape(width, UNITS), wm[slot, :, :, there].reshape(width, UNITS), units_ref[t, :, here], out_acc, gact, gunits.at[t, :, here]
            )
            target[:, :, here] = block_rows(gin)
            target[:, :, there] = block_rows(gback)
            return carry

        lax.fori_loop(0, units // UNITS, body, 0)
        if remote:
            if s == 0:
                wait_neighbours()
            if not mine:
                over[0, s].start()
            else:
                over[0, s - 1].wait_recv()
        else:
            copy = pltpu.make_async_copy(stage_m, rest_hbm[0].at[t], out_sem.at[0])
            copy.start()
            copy.wait()
        if s + 2 < groups:
            wm_loads[s + 2].start()
        tick()
    act_t = wm.at[0]
    act_load = pltpu.make_async_copy(act_t_hbm, act_t, in_sem.at[2])
    act_load.start()
    upstream = cot[...].astype(F32)
    normed, rate = norm_parts(mid[...])
    two[...] = (mid[...] + out_acc[...] + rows_ref[7:8, :]).astype(BF16)
    output_store = pltpu.make_async_copy(two, output_hbm, out_sem.at[1])
    output_store.start()
    grad_two = gact[...]
    gmid = upstream + norm_pull(grad_two, normed, rate, rows_ref[5:6, :])
    mid[...] = gmid
    low_ref[...] = gmid.astype(BF16)
    sums[4:5, :] = jnp.sum(gmid, axis=0, keepdims=True)
    sums[5:6, :] = jnp.sum(grad_two * normed, axis=0, keepdims=True)
    sums[6:7, :] = jnp.sum(grad_two, axis=0, keepdims=True)
    sums[7:8, :] = jnp.sum(upstream, axis=0, keepdims=True)
    low_t = two_t
    low_t[...] = low_ref[...].T
    halo_loads = [
        pltpu.make_async_copy(halo.at[0], cot, in_sem.at[0]),
        pltpu.make_async_copy(halo.at[1], wa.at[groups % 2, pl.ds(0, rows)], in_sem.at[1]),
    ]
    halo_loads[0].start()
    tick()
    act_load.wait()
    for s in range(groups):
        t, side, mine = order[s]
        wa_loads[s].wait()
        for copy in group_loads[s]:
            copy.wait()
        if s + 1 < groups:
            wa_loads[s + 1].start()
        else:
            halo_loads[1].start()
        weights = wa[s % 2]
        target = acc_a.at[side] if mine else stage_a
        if remote and s == 2:
            over[1, 0].wait_send()
        first, second, third = head_width, 2 * head_width, 3 * head_width
        do_ref[...] = mxu(low_ref[...], weights[:, third:], NN).astype(BF16)
        target[:, :, third:] = block_rows(mxu(low_t[...], ctx[...], NN).astype(BF16))
        tick()
        pull_group(q, k, v, do_ref, ctx, lse.at[t], segq_row, segk_col, kt, dk_acc, dv_acc, dq_acc, lambda: tick())
        if s + 1 < groups:
            for copy in group_loads[s + 1]:
                copy.start()
        dq = (dq_acc[...] * HEAD_DIM**-0.5).T.astype(BF16)
        dk = dk_acc[...].astype(BF16)
        dv = dv_acc[...].astype(BF16)
        qsum[t] = jnp.sum(dq.astype(F32), axis=0, keepdims=True)
        vsum[t] = jnp.sum(dv_acc[...], axis=0, keepdims=True)
        target[:, :, :first] = block_rows(mxu(act_t[:, :, rows : 2 * rows].reshape(width, rows), dq, NN).astype(BF16))
        target[:, :, first:second] = block_rows(mxu(act_t[...].reshape(width, 3 * rows), dk, NN).astype(BF16))
        target[:, :, second:third] = block_rows(mxu(act_t[...].reshape(width, 3 * rows), dv, NN).astype(BF16))
        if remote:
            if not mine:
                over[1, s].start()
            else:
                over[1, s - 1].wait_recv()
        tick()
        both = jnp.concatenate([dk, dv], axis=1)
        lanes = weights[:, first:third]
        for part in range(3):
            here = slice(part * rows, (part + 1) * rows)
            value = mxu(both[here], lanes, NT)
            if part == 1:
                value = value + mxu(dq, weights[:, :first], NT)
            if s == 0:
                grad_one[here, :] = value
            else:
                grad_one[here, :] += value
        if not remote:
            copy = pltpu.make_async_copy(stage_a, rest_hbm[1].at[t], out_sem.at[0])
            copy.start()
            copy.wait()
        tick()
    output_store.wait()
    low_ref[...] = grad_one[:rows, :].astype(BF16)
    two[...] = grad_one[2 * rows :, :].astype(BF16)
    if remote:
        finish_halo = exchange_halo(low_ref, two, halo_land, halo_send, halo_recv, low_ref, two)
    gain_sum = jnp.zeros((1, width), F32)
    for copy in halo_loads:
        copy.wait()
    for part, source in enumerate((cot, tok, wa.at[groups % 2, pl.ds(0, rows)])):
        normed, rate = norm_parts(source[...].astype(F32))
        gain_sum = gain_sum + jnp.sum(grad_one[part * rows : (part + 1) * rows, :] * normed, axis=0, keepdims=True)
    sums[0:1, :] = gain_sum
    sums[1:2, :] = jnp.sum(grad_one[...], axis=0, keepdims=True)
    for t in range(groups):
        sums[2:3, t * head_width : (t + 1) * head_width] = qsum[t]
        sums[3:4, t * head_width : (t + 1) * head_width] = vsum[t]
    pack_vectors(sums, gunits, gvec, SPLIT)
    if not remote:
        copies = [
            pltpu.make_async_copy(low_ref, rest_hbm[2].at[0], out_sem.at[0]),
            pltpu.make_async_copy(two, rest_hbm[2].at[1], out_sem.at[1]),
            pltpu.make_async_copy(grad_one.at[pl.ds(rows, rows)], result_hbm, out_sem.at[2]),
            pltpu.make_async_copy(mid, back_hbm, out_sem.at[3]),
            pltpu.make_async_copy(gvec, rest_hbm[3], out_sem.at[4]),
        ]
        for copy in copies:
            copy.start()
        for copy in copies:
            copy.wait()
        return
    acc_v[0] = gvec[...]
    acc_v[1] = gvec[...]
    over_v = [
        pltpu.make_async_remote_copy(
            gvec, core_v.at[side], core_send.at[2, side], core_recv.at[2, side], device_id=sibling, device_id_type=MESH_ID
        )
        for side in range(2)
    ]
    for copy in over_v:
        copy.start()
    for copy in over_v:
        copy.wait_recv()
    tick()
    finish_halo()
    from_left = jnp.where(tensor > 0, halo_land[0].astype(F32), 0.0)
    from_right = jnp.where(tensor < 3, halo_land[1].astype(F32), 0.0)
    normed, rate = norm_parts(tok[...].astype(F32))
    total = grad_one[rows : 2 * rows, :] + from_left + from_right
    out_acc[...] = mid[...] + norm_pull(total, normed, rate, rows_ref[0:1, :])
    result_store = pltpu.make_async_copy(out_acc, result_hbm, out_sem.at[2])
    result_store.start()
    tick()
    for end in ends:
        end()
    over[0, 2].wait_send()
    over[1, 2].wait_send()
    for copy in over_v:
        copy.wait_send()
    result_store.wait()


def backward_rows(remote, tok, halo, cot, middle, act_two, act_t, wm, wa, rows_ref, units_ref, q, k, v, ctx, lse, segk_row, segk_col):
    rows, width = tok.shape
    groups, wide = wm.shape[0], wm.shape[-1]
    narrow = wa.shape[2]
    head_width = narrow // 4
    shape = jax.ShapeDtypeStruct
    vmem = pltpu.VMEM
    dma = lambda *dims: pltpu.SemaphoreType.DMA(dims)
    in_specs = [VMEM_SPEC, HBM_SPEC] + [HBM_SPEC] * 6 + [VMEM_SPEC] * 2 + [HBM_SPEC] * 4 + [VMEM_SPEC] * 3
    piece = width // SPLIT
    if remote:
        out_shape = (
            shape((rows, width), BF16),
            shape((piece, wide), F32),
            shape((piece, narrow), F32),
            shape((16, 128), F32),
            shape((rows, width), F32),
        )
        out_specs = (HBM_SPEC, VMEM_SPEC, VMEM_SPEC, VMEM_SPEC, HBM_SPEC)
    else:
        out_shape = (
            shape((rows, width), BF16),
            shape((groups, SPLIT, piece, wide), BF16),
            shape((groups, SPLIT, piece, narrow), BF16),
            shape((SPLIT, 16, 128), BF16),
            shape((2, rows, width), BF16),
            shape((rows, width), F32),
            shape((rows, width), F32),
        )
        out_specs = (HBM_SPEC,) * 7
    scratch = [
        vmem((rows, width), BF16),
        vmem((rows, width), BF16),
        vmem((width, rows), BF16),
        vmem((width, rows), BF16),
        vmem((rows, width), F32),
        vmem((rows, width), F32),
        vmem((rows, width), F32),
        vmem((rows, width), BF16),
        vmem((2, SPLIT, piece, wide), BF16),
        vmem((2, width, narrow), BF16),
        vmem((rows, head_width), BF16),
        vmem((3 * rows, head_width), BF16),
        vmem((3 * rows, head_width), BF16),
        vmem((rows, head_width), BF16),
        vmem((SPLIT, piece, wide), BF16),
        vmem((3 * rows, width), F32),
        vmem((3 * rows, head_width), F32),
        vmem((3 * rows, head_width), F32),
        vmem((head_width, rows), F32),
        vmem((head_width, 3 * rows), BF16),
        vmem((rows, head_width), BF16),
        vmem((VEC_ROWS, width), F32),
        vmem(units_ref.shape, F32),
        vmem((groups, 1, head_width), F32),
        vmem((groups, 1, head_width), F32),
        vmem((SPLIT, 16, 128), BF16),
        dma(3),
        dma(2),
        dma(2),
        dma(4),
        dma(5),
    ]
    params = dict(vmem_limit_bytes=VMEM_LIMIT)
    if remote:
        n = len(REDUCE_PARTS)
        sizes = ((piece, wide), (piece, narrow), (16, 128))
        slots = [4 * len(land_slots(p[0], 4)) for p in REDUCE_PARTS]
        scratch += [vmem((2, SPLIT) + size, BF16) for size in sizes]
        scratch += [vmem((2, SPLIT) + size, BF16) for size in sizes]
        scratch += [vmem((2, rows, width), BF16)]
        scratch += [vmem((slots[i], p[3], sizes[p[1]][1]), BF16) for i, p in enumerate(REDUCE_PARTS)]
        scratch += [dma(3, 2), dma(3, 2), dma(n, 4, 4), dma(n, max(slots)), dma(4), dma(2)]
        params.update(collective_id=1, has_side_effects=True)

    def kernel(*refs):
        ins, outs, rest = refs[:17], refs[17 : 17 + len(out_shape)], refs[17 + len(out_shape) :]
        if remote:
            outs = (outs[0], outs[1], outs[2], outs[3], outs[4], None, None)
        else:
            outs = (outs[0], None, None, None, outs[5], (outs[1], outs[2], outs[4], outs[3]), outs[6])
        backward_kernel(remote, *ins, *outs, *rest)

    return pl.pallas_call(
        kernel,
        out_shape=out_shape,
        in_specs=in_specs,
        out_specs=out_specs,
        scratch_shapes=scratch,
        compiler_params=pltpu.CompilerParams(**params),
        name="backward_rows",
    )(tok, halo, cot, middle, act_two, act_t.reshape(SPLIT, piece, 3 * rows), wm, wa, rows_ref, units_ref, q, k, v, ctx, lse, segk_row, segk_col)


def finish_kernel(piece, out_in, grad_in, sum_m, sum_a, sum_v, out, grad, *rest):
    *results, out_s, grad_s, m_s, a_s, v_s, sem, back_sem = rest
    pairs = ((out_in, out_s), (grad_in, grad_s), (sum_a, a_s), (sum_m, m_s), (sum_v, v_s))
    loads = [pltpu.make_async_copy(source, target, sem.at[i]) for i, (source, target) in enumerate(pairs)]
    for copy in loads:
        copy.start()
    stores = [pltpu.make_async_copy(out_s, out, back_sem.at[0]), pltpu.make_async_copy(grad_s, grad, back_sem.at[1])]
    for load, store in zip(loads[:2], stores):
        load.wait()
        store.start()
    for copy in loads[2:]:
        copy.wait()
    sum_m, sum_a, sum_v = m_s, a_s, v_s
    g_q, g_k, g_v, g_o, g_in, g_back, *lines = results
    head_width, units = g_q.shape[1], g_in.shape[1]
    total = sum_a[...]
    g_q[...] = total[:, :head_width]
    g_k[...] = total[:, head_width : 2 * head_width]
    g_v[...] = total[:, 2 * head_width : 3 * head_width]
    g_o[...] = total[:, 3 * head_width :].T
    g_in[...] = sum_m[:, :units]
    g_back[...] = sum_m[:, units:]
    for i in range(SHIFTS):
        lines[i][...] = sum_v[i : i + 1, :piece]
    for row in range(lines[SHIFTS].shape[1] // 128):
        lines[SHIFTS][:, row * 128 : (row + 1) * 128] = sum_v[SHIFTS + row : SHIFTS + row + 1, :]
    for copy in stores:
        copy.wait()


def finish_rows(output, grad_tokens, sum_m, sum_a, sum_v, unit_piece):
    piece, wide = sum_m.shape
    narrow = sum_a.shape[1]
    line = lambda n: jax.ShapeDtypeStruct((1, n), F32)
    shape = lambda *dims: jax.ShapeDtypeStruct(dims, F32)
    quarter = shape(piece, narrow // 4)
    half = shape(piece, wide // 2)
    return pl.pallas_call(
        functools.partial(finish_kernel, piece),
        out_shape=(
            jax.ShapeDtypeStruct(output.shape, output.dtype),
            jax.ShapeDtypeStruct(grad_tokens.shape, grad_tokens.dtype),
            quarter,
            quarter,
            quarter,
            shape(narrow // 4, piece),
            half,
            half,
        )
        + (line(piece),) * SHIFTS
        + (line(unit_piece),),
        in_specs=[pl.BlockSpec(memory_space=pltpu.HBM)] * 5,
        out_specs=(pl.BlockSpec(memory_space=pltpu.HBM),) * 2 + (VMEM_SPEC,) * (7 + SHIFTS),
        scratch_shapes=[
            pltpu.VMEM(output.shape, output.dtype),
            pltpu.VMEM(grad_tokens.shape, F32),
            pltpu.VMEM(sum_m.shape, F32),
            pltpu.VMEM(sum_a.shape, F32),
            pltpu.VMEM(sum_v.shape, F32),
            pltpu.SemaphoreType.DMA((5,)),
            pltpu.SemaphoreType.DMA((2,)),
        ],
        compiler_params=pltpu.CompilerParams(vmem_limit_bytes=VMEM_LIMIT),
        name="finish_rows",
    )(output, grad_tokens, sum_m, sum_a, sum_v)


def per_device(by_kernel, *args):
    (
        tokens,
        cotangent,
        segment_ids,
        ln1_gain,
        ln1_bias,
        w_query,
        query_bias,
        w_key,
        w_value,
        value_bias,
        w_out,
        out_bias,
        ln2_gain,
        ln2_bias,
        w_in,
        in_bias,
        w_back,
        back_bias,
    ) = args
    rows, width = tokens.shape
    n_dp, n_tensor = lax.axis_size("dp"), lax.axis_size("tensor")
    index = lax.axis_index("tensor")
    head_width = w_query.shape[1]
    units = w_in.shape[1]
    piece = ln1_gain.shape[0]
    unit_piece = in_bias.shape[0]

    vectors = (ln1_gain, ln1_bias, query_bias, value_bias, out_bias, ln2_gain, ln2_bias, back_bias)
    if by_kernel:
        lines = [vector.reshape(1, piece) for vector in vectors]
        sources = (w_in, w_back.T, w_query, w_key, w_value, w_out, *lines, in_bias.reshape(-1, 128))
        full_mlp, full_att, halo, *saved = forward_rows(True, tokens, segment_ids, units, *sources)
    else:
        shard_mlp = jnp.concatenate([w_in, w_back.T], axis=1)
        shard_att = jnp.concatenate([w_query, w_key, w_value, w_out.T], axis=1)
        edge = jnp.full((rows,), -1, jnp.int32)
        segs = jnp.concatenate([edge, segment_ids[0], edge])
        segs = lax.dynamic_slice_in_dim(segs, index * rows, 3 * rows)[None, :]
        shard_vec = jnp.concatenate([jnp.stack(vectors).reshape(-1), in_bias])
        full_mlp, full_att, full_vec, halo = gather_by_ops((shard_mlp, shard_att, shard_vec), tokens)
        flat = full_vec[0]
        rows8 = jnp.swapaxes(flat[:, : 8 * piece].reshape(n_dp, 8, piece), 0, 1).reshape(8, SPLIT, width // SPLIT)
        rows8 = jnp.pad(jnp.swapaxes(rows8, 0, 1), ((0, 0), (0, 0), (0, 128 - width // SPLIT)))
        unit_rows = flat[:, 8 * piece :].reshape(SPLIT, -1, 128)
        full_vec = jnp.concatenate([rows8, unit_rows], axis=1)
        full_vec = jnp.pad(full_vec, ((0, 0), (0, 16 - full_vec.shape[1]), (0, 0)))
        full_mlp = full_mlp.reshape(n_tensor, SPLIT, width // SPLIT, 2 * units)
        full_att = full_att.reshape(n_tensor, SPLIT, width // SPLIT, 4 * head_width)
        saved = forward_rows(False, tokens, segs, units, halo, full_att, full_vec)
    rows_vec, units_vec, segk_row, segk_col, lse, act_t, query, keys, values, context, middle, act_two = saved
    full_att = full_att.reshape(n_tensor, width, 4 * head_width)
    results = backward_rows(
        by_kernel, tokens, halo, cotangent, middle, act_two, act_t, full_mlp, full_att, rows_vec, units_vec, query, keys, values,
        context, lse, segk_row, segk_col,
    )
    if by_kernel:
        output, sum_mlp, sum_att, sum_vec, grad_tokens = results
        output, grad_tokens, g_wq, g_wk, g_wv, g_wo, g_win, g_wback, *vec = finish_rows(
            output, grad_tokens, sum_mlp, sum_att, sum_vec, unit_piece
        )
        vec = [line.reshape(-1) for line in vec]
    else:
        output, grad_mlp, grad_att, grad_vec, halo_rows, grad_own, grad_middle = results
        split = lambda array: array.reshape(n_tensor, n_dp, width // n_dp, array.shape[-1])
        rows8 = jnp.swapaxes(grad_vec[:, :8, : width // 8], 0, 1).reshape(8, n_dp, piece)
        unit_flat = grad_vec[:, 8 : 8 + unit_piece * n_dp // SPLIT // 128].reshape(n_dp, unit_piece)
        flat = jnp.concatenate([jnp.swapaxes(rows8, 0, 1).reshape(n_dp, 8 * piece), unit_flat], axis=1)
        flat = jnp.broadcast_to(flat[None], (n_tensor,) + flat.shape)
        sum_mlp, sum_att, sum_vec, halo_back = reduce_by_ops((split(grad_mlp), split(grad_att), flat), halo_rows)
        vec = [sum_vec[i * piece : (i + 1) * piece] for i in range(8)] + [sum_vec[8 * piece :]]
        from_left = jnp.where(index > 0, halo_back[0].astype(F32), 0.0)
        from_right = jnp.where(index < n_tensor - 1, halo_back[1].astype(F32), 0.0)
        norm_one, rate_one = norm_parts(tokens.astype(F32))
        grad_tokens = grad_middle + norm_pull(grad_own + from_left + from_right, norm_one, rate_one, rows_vec[0:1])
        g_wq, g_wk, g_wv = (sum_att[:, i * head_width : (i + 1) * head_width] for i in range(3))
        g_wo = sum_att[:, 3 * head_width :].T
        g_win, g_wback = sum_mlp[:, :units], sum_mlp[:, units:]
    g_ln1_gain, g_ln1_bias, g_q, g_v, g_o, g_ln2_gain, g_ln2_bias, g_b, g_i = vec
    return (
        output,
        grad_tokens,
        g_ln1_gain,
        g_ln1_bias,
        g_wq,
        g_q,
        g_wk,
        g_wv,
        g_v,
        g_wo,
        g_o,
        g_ln2_gain,
        g_ln2_bias,
        g_win,
        g_i,
        g_wback.T,
        g_b,
    )


def solution(mesh):
    by_kernel = mesh.shape["dp"] == 8 and mesh.shape["tensor"] == 4
    rows = P(("dp", "tensor"), None)
    line, first, second = P("dp"), P("dp", "tensor"), P("tensor", "dp")
    return jax.shard_map(
        functools.partial(per_device, by_kernel),
        mesh=mesh,
        in_specs=(rows, rows, P("dp", None), line, line, first, line, first, first, line, second, line, line, line, first, line, second, line),
        out_specs=(rows, rows, line, line, first, line, first, first, line, second, line, line, line, first, line, second, line),
        check_vma=False,
    )
```

```python
import functools

import jax
import jax.numpy as jnp
from jax import lax
from jax.experimental import pallas as pl
from jax.experimental.pallas import tpu as pltpu
from jax.sharding import PartitionSpec as P

HEAD_DIM = 64
EPSILON = 1e-12
MASKED = -1000000000.0
MESH_ID = pl.DeviceIdType.MESH
F32 = jnp.float32
BF16 = jnp.bfloat16

NN = (((1,), (0,)), ((), ()))
NT = (((1,), (1,)), ((), ()))
TN = (((0,), (0,)), ((), ()))


def mxu(left, right, dims):
    return lax.dot_general(left, right, dims, preferred_element_type=F32)


def position():
    dp = lax.axis_index("dp")
    tensor = lax.axis_index("tensor")
    return dp // 2, dp % 2, tensor // 2, tensor % 2


def device(z, y, x, core):
    return (z * 2 + y, x * 2 + core)


def offsets(depth):
    found = [(dz, dy, dx) for dz in range(1 - depth, depth) for dy in range(2) for dx in range(2)]
    return sorted(found, key=lambda item: abs(item[0]) + item[1] + item[2])


def level(route, offset):
    dims = dict(zip("zyx", offset))
    last = -1
    for place, name in enumerate(route):
        if dims[name] != 0:
            last = place
    return last


def when(condition, action):
    if condition is True:
        action()
    else:
        pl.when(condition)(action)


def meet_neighbours(depth):
    z, y, x, core = position()
    dp, tensor = lax.axis_index("dp"), lax.axis_index("tensor")
    barrier = pltpu.get_barrier_semaphore()

    def signal(target):
        pl.semaphore_signal(barrier, inc=1, device_id=target, device_id_type=MESH_ID)

    signal(device(z, y, x, 1 - core))
    signal(device(z, y, 1 - x, core))
    signal(device(z, 1 - y, x, core))
    pl.when(z > 0)(lambda: signal(device(z - 1, y, x, core)))
    pl.when(z < depth - 1)(lambda: signal(device(z + 1, y, x, core)))
    middle = (tensor == 1) | (tensor == 2)
    pl.when(middle)(lambda: signal((dp, 3 - tensor)))
    as_int = lambda flag: flag.astype(jnp.int32)
    return lambda: pl.semaphore_wait(barrier, 3 + as_int(z > 0) + as_int(z < depth - 1) + as_int(middle))


def tree_sends(route, offset, depth):
    z, y, x, core = position()
    dz = offset[0]
    lev = level(route, offset)
    sends = []
    for place, name in enumerate(route):
        if name == "z":
            if place < lev:
                continue
            if place > lev or dz < 0:
                sends.append((0, device(jnp.minimum(z + 1, depth - 1), y, x, core), z < depth - 1, 0))
            if place > lev or dz > 0:
                sends.append((1, device(jnp.maximum(z - 1, 0), y, x, core), z > 0, 0))
        elif place > lev:
            if name == "y":
                sends.append((2, device(z, 1 - y, x, core), True, 2))
            else:
                sends.append((3, device(z, y, 1 - x, core), True, 1))
    return sends


def tree_parent(route, offset):
    z, y, x, core = position()
    dz, dy, dx = offset
    name = route[level(route, offset)]
    if name == "z":
        if dz < 0:
            return 0, device(z - 1, y, x, core)
        return 1, device(z + 1, y, x, core)
    if name == "y":
        return 2, device(z, 1 - y, x, core)
    return 3, device(z, y, 1 - x, core)


def exchange_halo(rows_left, rows_right, halo, halo_send, halo_recv, own_left, own_right):
    dp, tensor = lax.axis_index("dp"), lax.axis_index("tensor")
    has_left, has_right = tensor > 0, tensor < 3
    to_right = pltpu.make_async_remote_copy(
        rows_right, halo.at[0], halo_send.at[0], halo_recv.at[0], device_id=(dp, jnp.minimum(tensor + 1, 3)), device_id_type=MESH_ID
    )
    to_left = pltpu.make_async_remote_copy(
        rows_left, halo.at[1], halo_send.at[1], halo_recv.at[1], device_id=(dp, jnp.maximum(tensor - 1, 0)), device_id_type=MESH_ID
    )
    fill_left = pltpu.make_async_copy(own_left, halo.at[0], halo_send.at[2])
    fill_right = pltpu.make_async_copy(own_right, halo.at[1], halo_send.at[3])
    pl.when(has_right)(lambda: to_right.start())
    pl.when(has_left)(lambda: to_left.start())
    pl.when(~has_left)(lambda: fill_left.start())
    pl.when(~has_right)(lambda: fill_right.start())

    def finish():
        pl.when(has_right)(lambda: to_right.wait_send())
        pl.when(has_left)(lambda: to_left.wait_send())
        pl.when(has_left)(lambda: to_right.wait_recv())
        pl.when(has_right)(lambda: to_left.wait_recv())
        pl.when(~has_left)(lambda: fill_left.wait())
        pl.when(~has_right)(lambda: fill_right.wait())

    return finish


def gather_events(parts, depth, srcs, outs, send_sem, recv_sem, core_send, core_recv):
    z, y, x, core = position()
    sibling = device(z, y, x, 1 - core)
    events, backs, ends = {}, {}, []

    def piece(part, offset, owner_core):
        dz, dy, dx = offset
        _, which, begin, size = parts[part]
        oy = 1 - y if dy else y
        ox = 1 - x if dx else x
        return outs[which].at[ox * 2 + owner_core, (z + dz) * 2 + oy, pl.ds(begin, size)]

    for number, offset in enumerate(offsets(depth)):
        for part, (route, which, begin, size) in enumerate(parts):
            dz, dy, dx = offset
            mine = offset == (0, 0, 0)
            target = piece(part, offset, core)
            block = srcs[which].at[pl.ds(begin, size)] if mine else target
            zi, bi = z + dz, dy * 2 + dx
            valid = True if dz == 0 else ((z + dz >= 0) & (z + dz <= depth - 1))
            sends = []
            for way, to, ok, shift in tree_sends(route, offset, depth):
                copy = pltpu.make_async_remote_copy(
                    block, target, send_sem.at[part, way, zi, bi], recv_sem.at[part, zi, bi + shift], device_id=to, device_id_type=MESH_ID
                )
                sends.append((copy, ok))
            arrival = pltpu.make_async_remote_copy(
                block, target, send_sem.at[part, 0, 0, 0], recv_sem.at[part, zi, bi], device_id=sibling, device_id_type=MESH_ID
            )
            over = pltpu.make_async_remote_copy(
                block, target, core_send.at[part, zi, bi], core_recv.at[part, zi, bi], device_id=sibling, device_id_type=MESH_ID
            )
            other = piece(part, offset, 1 - core)
            back = pltpu.make_async_remote_copy(
                other, other, core_send.at[part, zi, bi], core_recv.at[part, zi, bi], device_id=sibling, device_id_type=MESH_ID
            )

            def arrive(sends=sends, arrival=arrival, over=over, mine=mine):
                if not mine:
                    arrival.wait_recv()
                for copy, ok in sends:
                    when(ok, lambda copy=copy: copy.start())
                over.start()

            def finish(sends=sends, over=over):
                for copy, ok in sends:
                    when(ok, lambda copy=copy: copy.wait_send())
                over.wait_send()

            events[part * 100 + number] = lambda valid=valid, arrive=arrive: when(valid, arrive)
            backs[part * 100 + number] = lambda valid=valid, back=back: when(valid, lambda: back.wait_recv())
            ends.append(lambda valid=valid, finish=finish: when(valid, finish))
    return events, backs, ends


GATHER_PARTS = (
    ("xzy", 1, 0, 48),
    ("yzx", 1, 48, 48),
    ("zyx", 0, 0, 64),
    ("xzy", 0, 64, 32),
)

GATHER_STEPS = (
    (0, 100),
    (1, 101, 3, 103, 4, 104),
    (),
    (),
    (5, 7, 110, 10, 105, 11, 2, 107, 14, 12, 111, 102, 112, 118, 18, 19, 106, 6, 21, 108, 8, 114, 9, 109, 119, 25, 200, 300, 125, 116, 13, 120, 15, 121),
    (113, 16, 17, 124),
    (115, 117),
    (122, 123, 203, 204),
    (201, 303, 304),
    (20, 126, 301, 202, 22, 23, 24),
    (127, 302),
    (),
    (205, 210, 211, 208),
    (26, 305, 311, 27),
    (207, 309),
    (306, 209, 310),
    (212,),
    (206, 307, 312, 219),
    (308, 313, 319),
    (317,),
    (213, 214, 218, 320),
    (220, 324),
    (314, 216, 217, 318, 224, 225),
    (316, 221, 325),
    (315, 321),
    (215, 322, 323, 327, 326, 227, 226, 222, 223),
)


def gather_by_ops(shards, tokens):
    full = []
    for shard in shards:
        over_dp = lax.all_gather(shard, "dp", axis=0, tiled=False)
        full.append(lax.all_gather(over_dp, "tensor", axis=0, tiled=False))
    return tuple(full) + (halo_by_ops(tokens, tokens),)


def halo_by_ops(rows_left, rows_right):
    count = lax.axis_size("tensor")
    from_left = lax.ppermute(rows_right, "tensor", [(i, i + 1) for i in range(count - 1)])
    from_right = lax.ppermute(rows_left, "tensor", [(i, i - 1) for i in range(1, count)])
    return jnp.stack([from_left, from_right])


def reduce_by_ops(grads, halo_rows):
    sums = []
    for grad in grads:
        over_tensor = lax.psum_scatter(grad, "tensor", scatter_dimension=0, tiled=False)
        sums.append(lax.psum_scatter(over_tensor, "dp", scatter_dimension=0, tiled=False).astype(F32))
    return tuple(sums) + (halo_by_ops(halo_rows[0], halo_rows[1]),)


def norm_parts(values):
    center = values - jnp.mean(values, axis=-1, keepdims=True)
    rate = lax.rsqrt(jnp.mean(center * center, axis=-1, keepdims=True) + EPSILON)
    return center * rate, rate


def norm_pull(grad, normed, rate, gain):
    scaled = grad * gain
    return rate * (
        scaled
        - jnp.mean(scaled, axis=-1, keepdims=True)
        - normed * jnp.mean(scaled * normed, axis=-1, keepdims=True)
    )


def head_mask(head):
    lane = lax.broadcasted_iota(jnp.int32, (1, 3 * HEAD_DIM), 1)
    return (lane >= head * HEAD_DIM) & (lane < (head + 1) * HEAD_DIM)


QB = 256
UNITS = 768
VMEM_LIMIT = 63 * 1024 * 1024
VEC_ROWS = 16
SPLIT = 8
SHIFTS = 8
VMEM_SPEC = pl.BlockSpec(memory_space=pltpu.VMEM)
HBM_SPEC = pl.BlockSpec(memory_space=pl.ANY)


class Ticker:
    def __init__(self, steps, table):
        self.steps, self.table, self.point = steps, table, 0

    def __call__(self):
        if self.steps:
            for number in self.table[self.point]:
                self.steps[number]()
        self.point += 1


def unpack_vectors(vec_ref, rows_ref, units_ref, n_dp):
    width, groups = rows_ref.shape[1], units_ref.shape[0]
    piece, unit_rows = width // n_dp, units_ref.shape[2] * groups // n_dp // 128
    pieces = [vec_ref[dp].astype(F32) for dp in range(n_dp)]
    rows_ref[...] = jnp.concatenate([item[:, :piece] for item in pieces], axis=1)
    lines = [item[SHIFTS + row : SHIFTS + row + 1, :] for item in pieces for row in range(unit_rows)]
    per_group = len(lines) // groups
    for group in range(groups):
        units_ref[group] = jnp.concatenate(lines[group * per_group : (group + 1) * per_group], axis=1)


def pack_vectors(rows_ref, units_ref, vec_ref, n_dp):
    width, groups = rows_ref.shape[1], units_ref.shape[0]
    piece, unit_rows = width // n_dp, units_ref.shape[2] * groups // n_dp // 128
    vec_ref[...] = jnp.zeros_like(vec_ref)
    for dp in range(n_dp):
        vec_ref[dp, 0:SHIFTS, 0:piece] = rows_ref[0:SHIFTS, dp * piece : (dp + 1) * piece].astype(BF16)
        for row in range(unit_rows):
            begin = (dp * unit_rows + row) * 128
            group, lane = begin // units_ref.shape[2], begin % units_ref.shape[2]
            vec_ref[dp, SHIFTS + row : SHIFTS + row + 1, :] = units_ref[group, :, lane : lane + 128].astype(BF16)


def attend_block(q, k, v, same):
    total = jnp.zeros(q.shape, F32)
    logs = []
    for head in range(q.shape[1] // HEAD_DIM):
        mask = head_mask(head)
        raw = mxu(jnp.where(mask, q, jnp.zeros_like(q)), k, NT)
        scores = jnp.where(same, raw, MASKED)
        top = jnp.max(scores, axis=1, keepdims=True)
        expo = jnp.exp(scores - top)
        denom = jnp.sum(expo, axis=1, keepdims=True)
        part = mxu(expo.astype(BF16), v, NN)
        total = jnp.where(mask, part / denom, total)
        logs.append(top + jnp.log(denom))
    return total.astype(BF16), logs


def forward_kernel(remote, *refs):
    if remote:
        tok, segs, w_in, w_back, w_query, w_key, w_value, w_out = refs[:8]
        lines, unit_line = refs[8:16], refs[16]
        full_m, full_a, halo_hbm = refs[17:20]
        refs = refs[20:]
    else:
        tok, segs, halo, wa, vec = refs[:5]
        refs = refs[5:]
    rows_ref, units_ref, segk, segcol, lse, *stores_hbm = refs[:12]
    act, attn, logs_ref, qshift, act_t, q, k, v, ctx, middle, act_two, store_sem = refs[12:24]
    if remote:
        halo, wa, vec, shard_m, shard_a, shard_v, segs_all = refs[24:31]
        send_sem, recv_sem, core_send, core_recv, own_sem, vec_send, vec_recv, halo_send, halo_recv = refs[31:]
    rows, width = tok.shape
    groups = wa.shape[0]
    head_width = q.shape[2]
    depth = 4
    tick = Ticker(None, None)
    order = list(range(groups))
    logs_ref[...] = jnp.zeros_like(logs_ref)
    if remote:
        z, y, x, core = position()
        dp, tensor = lax.axis_index("dp"), lax.axis_index("tensor")
        order = [x * 2 + core, x * 2 + 1 - core, (1 - x) * 2 + core, (1 - x) * 2 + 1 - core]
        peers = [lax.rem(dp + shift, SPLIT) for shift in range(1, SPLIT)]
        barrier = pltpu.get_barrier_semaphore()
        middle_pair = (tensor == 1) | (tensor == 2)

        def signal(target):
            pl.semaphore_signal(barrier, inc=1, device_id=target, device_id_type=MESH_ID)

        for peer in peers:
            signal((peer, tensor))
        signal(device(z, y, x, 1 - core))
        signal(device(z, y, 1 - x, core))
        pl.when(middle_pair)(lambda: signal((dp, 3 - tensor)))
        stacked = jnp.concatenate([line[...].astype(F32) for line in lines], axis=0)
        padding = jnp.zeros((SHIFTS, 128 - stacked.shape[1]), F32)
        tail = jnp.zeros((16 - SHIFTS - unit_line.shape[0], 128), F32)
        shard_v[...] = jnp.concatenate(
            [jnp.concatenate([stacked, padding], axis=1), unit_line[...].astype(F32), tail], axis=0
        ).astype(BF16)
        shard_a[...] = jnp.concatenate([w_query[...], w_key[...], w_value[...], w_out[...].T], axis=1)
        shard_m[:, : w_in.shape[1]] = w_in[...]
        shard_m[:, w_in.shape[1] :] = w_back[...]
        edge = jnp.full((1, rows), -1, jnp.int32)
        segs_all[...] = jnp.concatenate([edge, segs[...], edge], axis=1)
        pl.semaphore_wait(barrier, SPLIT + 1 + middle_pair.astype(jnp.int32))
        own = [
            pltpu.make_async_copy(shard_v, vec.at[dp], own_sem.at[0]),
            pltpu.make_async_copy(shard_a, wa.at[tensor, dp], own_sem.at[1]),
            pltpu.make_async_copy(shard_m, full_m.at[tensor, dp], own_sem.at[2]),
        ]
        vec_copies = [
            pltpu.make_async_remote_copy(
                shard_v, vec.at[dp], vec_send.at[i], vec_recv.at[i], device_id=(peer, tensor), device_id_type=MESH_ID
            )
            for i, peer in enumerate(peers)
        ]
        for copy in vec_copies:
            copy.start()
        for copy in own:
            copy.start()
        finish_halo = exchange_halo(tok, tok, halo, halo_send, halo_recv, tok, tok)
        events, backs, ends = gather_events(GATHER_PARTS, depth, (shard_m, shard_a), (full_m, wa), send_sem, recv_sem, core_send, core_recv)
        tick = Ticker(events, GATHER_STEPS)
        tick()
        for i in range(SPLIT - 1):
            source = lax.rem(dp + SPLIT - 1 - i, SPLIT)
            pltpu.make_async_remote_copy(
                vec.at[source], vec.at[source], vec_send.at[i], vec_recv.at[i], device_id=(dp, 3 - tensor), device_id_type=MESH_ID
            ).wait_recv()
        own[0].wait()

    def wait_backs(array, dx):
        if remote:
            for key, step in backs.items():
                part, number = key // 100, key % 100
                if GATHER_PARTS[part][1] == array and (dx is None or offsets(depth)[number][2] == dx):
                    step()

    if remote:
        segk[...] = segs_all[:, pl.ds(pl.multiple_of(tensor * rows, rows), 3 * rows)]
    else:
        segk[...] = segs[...]
    segcol[...] = jnp.broadcast_to(segk[...], (8, 3 * rows)).T
    unpack_vectors(vec, rows_ref, units_ref, SPLIT)
    shifts = rows_ref[0:SHIFTS, :]
    for group in range(groups):
        lanes = slice(group * head_width, (group + 1) * head_width)
        qshift[group] = shifts[:, lanes]
    tick()
    gain, shift = rows_ref[0:1, :], rows_ref[1:2, :]
    for part in (1, 0, 2):
        if remote and part == 0:
            finish_halo()
        source = tok if part == 1 else halo.at[part // 2]
        normed, _ = norm_parts(source[...].astype(F32))
        act[part * rows : (part + 1) * rows, :] = (normed * gain + shift).astype(BF16)
        tick()
    act_t[...] = act[...].T
    stores = [pltpu.make_async_copy(act_t, stores_hbm[0], store_sem.at[0])]
    stores[0].start()
    if remote:
        halo_copy = pltpu.make_async_copy(halo, halo_hbm, own_sem.at[0])
        halo_copy.start()
        own[1].wait()
    for s in range(groups):
        t = order[s]
        if s % 2 == 1:
            wait_backs(1, s // 2)
        if remote and s == groups - 1:
            att_copy = pltpu.make_async_copy(wa, full_a, own_sem.at[1])
            att_copy.start()
        cut = lambda i: wa[t, :, :, i * head_width : (i + 1) * head_width].reshape(width, head_width)
        own_rows = act[rows : 2 * rows, :]
        query = (mxu(own_rows, cut(0), NN) + qshift[t, 2:3, :]).astype(BF16)
        q[t] = query * jnp.asarray(HEAD_DIM**-0.5, BF16)
        k[t] = mxu(act[...], cut(1), NN).astype(BF16)
        tick()
        v[t] = (mxu(act[...], cut(2), NN) + qshift[t, 3:4, :]).astype(BF16)
        tick()
        band = QB + 2 * rows
        for block in range(rows // QB):
            here, keys = pl.ds(block * QB, QB), pl.ds(block * QB, band)
            same = segcol[pl.ds(rows + block * QB, QB), 0:1] == segk[:, keys]
            result, logs = attend_block(q[t, here, :], k[t, keys, :], v[t, keys, :], same)
            ctx[t, here, :] = result
            for head, value in enumerate(logs):
                logs_ref[here, head : head + 1] = value
            tick()
        lse[t] = logs_ref[...].T[0 : lse.shape[1], :]
        part = mxu(ctx[t], cut(3), NT)
        if s == 0:
            attn[...] = part
        else:
            attn[...] += part
        for i, source in enumerate((q, k, v, ctx)):
            stores.append(pltpu.make_async_copy(source.at[t], stores_hbm[1 + i].at[t], store_sem.at[1 + 4 * s + i]))
            stores[-1].start()
        tick()
    total = tok[...].astype(F32) + attn[...] + rows_ref[4:5, :]
    middle[...] = total
    normed, _ = norm_parts(total)
    act_two[...] = (normed * rows_ref[5:6, :] + rows_ref[6:7, :]).astype(BF16)
    for i, source in enumerate((middle, act_two)):
        stores.append(pltpu.make_async_copy(source, stores_hbm[5 + i], store_sem.at[1 + 4 * groups + i]))
        stores[-1].start()
    tick()
    for copy in stores:
        copy.wait()
    if remote:
        wait_backs(0, None)
        own[2].wait()
        for end in ends:
            end()
        for copy in vec_copies:
            copy.wait_send()
        halo_copy.wait()
        att_copy.wait()


def forward_rows(remote, tok, segs, units, *sources):
    rows, width = tok.shape
    groups, head_width = 4, width // 4
    piece = width // SPLIT
    shape = jax.ShapeDtypeStruct
    vmem = pltpu.VMEM
    dma = lambda *dims: pltpu.SemaphoreType.DMA(dims)
    saved = (
        ((width, 3 * rows), BF16),
        ((groups, rows, head_width), BF16),
        ((groups, 3 * rows, head_width), BF16),
        ((groups, 3 * rows, head_width), BF16),
        ((groups, rows, head_width), BF16),
        ((rows, width), F32),
        ((rows, width), BF16),
    )
    out_shape = (
        shape((VEC_ROWS, width), F32),
        shape((groups, 1, units), F32),
        shape((1, 3 * rows), jnp.int32),
        shape((3 * rows, 8), jnp.int32),
        shape((groups, 8, rows), F32),
    ) + tuple(shape(*item) for item in saved)
    out_specs = (VMEM_SPEC,) * 5 + (HBM_SPEC,) * 7
    scratch = [
        vmem((3 * rows, width), BF16),
        vmem((rows, width), F32),
        vmem((rows, 128), F32),
        vmem((groups, SHIFTS, head_width), F32),
    ]
    scratch += [vmem(*item) for item in saved] + [dma(3 + 4 * groups)]
    params = dict(vmem_limit_bytes=VMEM_LIMIT)
    if remote:
        n = len(GATHER_PARTS)
        wide, narrow = (piece, 2 * units), (piece, 4 * head_width)
        out_shape = (
            shape((groups, SPLIT) + wide, BF16),
            shape((groups, SPLIT) + narrow, BF16),
            shape((2, rows, width), BF16),
        ) + out_shape
        out_specs = (HBM_SPEC,) * 3 + out_specs
        scratch += [
            vmem((2, rows, width), BF16),
            vmem((groups, SPLIT) + narrow, BF16),
            vmem((SPLIT, 16, 128), BF16),
            vmem(wide, BF16),
            vmem(narrow, BF16),
            vmem((16, 128), BF16),
            vmem((1, segs.shape[1] + 2 * rows), jnp.int32),
        ]
        scratch += [dma(n, 4, 4, 4), dma(n, 4, 4), dma(n, 4, 4), dma(n, 4, 4), dma(3), dma(SPLIT - 1), dma(SPLIT - 1), dma(4), dma(2)]
        params.update(collective_id=0, has_side_effects=True)
    return pl.pallas_call(
        functools.partial(forward_kernel, remote),
        out_shape=out_shape,
        in_specs=[VMEM_SPEC] * (2 + len(sources)),
        out_specs=out_specs,
        scratch_shapes=scratch,
        compiler_params=pltpu.CompilerParams(**params),
        name="forward_rows",
    )(tok, segs, *sources)


def mlp_block(act, cot, act_t, cot_t, win, wback, bias, out, gact, gbias):
    pre = mxu(act[...], win, NN) + bias
    phi = 0.5 + 0.5 * lax.erf(pre * (0.5**0.5))
    hidden = (pre * phi).astype(BF16)
    slope = phi + pre * (jnp.exp(-0.5 * pre * pre) * 0.3989422804014327)
    grad_pre = mxu(cot[...], wback, NN) * slope
    low = grad_pre.astype(BF16)
    gbias[...] = jnp.sum(grad_pre, axis=0, keepdims=True)
    out[...] += mxu(hidden, wback, NT)
    gact[...] += mxu(low, win, NT)
    return mxu(act_t[...], low, NN).astype(BF16), mxu(cot_t[...], hidden, NN).astype(BF16)


def pull_group(q, k, v, do, ctx, lse, segq_row, segk_col, kt, dk_acc, dv_acc, dq_acc, tick):
    rows, width = q.shape
    heads = width // HEAD_DIM
    kt[...] = k[...].T
    dk_acc[...] = jnp.zeros_like(dk_acc)
    dv_acc[...] = jnp.zeros_like(dv_acc)
    dq_acc[...] = jnp.zeros_like(dq_acc)
    grad = do[...]
    product = grad.astype(F32) * ctx[...].astype(F32)
    row = lax.broadcasted_iota(jnp.int32, (8, width), 0)
    lane = lax.broadcasted_iota(jnp.int32, (8, width), 1)
    pick = jnp.where((lane >= row * HEAD_DIM) & (lane < (row + 1) * HEAD_DIM), 1.0, 0.0)
    delta_all = lax.dot_general(pick, product, NT, precision=lax.Precision.HIGHEST, preferred_element_type=F32)
    for block in range(rows // QB):
        here = pl.ds(block * QB, QB)
        span = slice(block * QB, (block + 1) * QB)
        segq = segq_row[:, here]
        query = q[here, :]
        q_stack = jnp.concatenate([jnp.where(head_mask(h), query, jnp.zeros_like(query)) for h in range(heads)], axis=0)
        do_stack = jnp.concatenate([jnp.where(head_mask(h), grad[span], jnp.zeros_like(query)) for h in range(heads)], axis=0)

        def body(tile, carry):
            keys = pl.ds(pl.multiple_of(block * QB + tile * QB, QB), QB)
            same = segk_col[keys, 0:1] == segq
            raw = mxu(k[keys, :], q_stack, NT)
            grad_weights = mxu(v[keys, :], do_stack, NT)
            dv_part = dk_part = None
            for head in range(heads):
                part = slice(head * QB, (head + 1) * QB)
                probs = jnp.exp(jnp.where(same, raw[:, part], MASKED) - lse[head : head + 1, here])
                grad_raw = (probs * (grad_weights[:, part] - delta_all[head : head + 1, span])).astype(BF16)
                low = probs.astype(BF16)
                spot = slice(head * QB, (head + 1) * QB)
                one, two = mxu(low, do_stack[spot], NN), mxu(grad_raw, q_stack[spot], NN)
                dv_part = one if head == 0 else dv_part + one
                dk_part = two if head == 0 else dk_part + two
                lanes = pl.ds(head * HEAD_DIM, HEAD_DIM)
                dq_acc[lanes, here] += mxu(kt[lanes, keys], grad_raw, NN)
            dv_acc[keys, :] += dv_part
            dk_acc[keys, :] += dk_part
            return carry

        lax.fori_loop(0, (QB + 2 * rows) // QB, body, 0, unroll=True)
        tick()


def land_slots(route, depth):
    ways = []
    for offset in offsets(depth):
        lev = level(route, offset)
        dz, dy, dx = offset
        for place, name in enumerate(route):
            if name == "z":
                if place < lev:
                    continue
                if place > lev or dz < 0:
                    ways.append((0, dy * 2 + dx))
                if place > lev or dz > 0:
                    ways.append((1, dy * 2 + dx))
            elif place > lev:
                ways.append((2 if name == "y" else 3, dy * 2 + dx))
    ways = sorted(set(ways))
    return {way: number * depth for number, way in enumerate(ways)}


def reduce_events(parts, depth, accs, cores, lands, outs, send_sem, recv_sem):
    z, y, x, core = position()
    sibling = device(z, y, x, 1 - core)
    events, ends = {}, []
    for offset in reversed(offsets(depth)):
        for part, (route, which, begin, size) in enumerate(parts):
            slots = land_slots(route, depth)
            dz, dy, dx = offset
            mine = offset == (0, 0, 0)
            zi, bi = z + dz, dy * 2 + dx
            valid = True if dz == 0 else ((z + dz >= 0) & (z + dz <= depth - 1))
            oy = 1 - y if dy else y
            ox = 1 - x if dx else x
            rows = pl.ds(begin, size)
            spot = zi * 2 + oy
            own = accs[which].at[ox, spot, rows]
            other = cores[which].at[ox, spot, rows]
            children = []
            for way, to, ok, shift in tree_sends(route, offset, depth):
                slot = slots[way, bi] + zi
                land = lands[part].at[slot]
                wait = pltpu.make_async_remote_copy(
                    land, land, send_sem.at[part, 0, 0], recv_sem.at[part, slot], device_id=sibling, device_id_type=MESH_ID
                )
                children.append((land, wait, ok))
            send = None
            if not mine:
                way, to = tree_parent(route, offset)
                slot = slots[way, bi - {0: 0, 1: 0, 2: 2, 3: 1}[way]] + zi
                send = pltpu.make_async_remote_copy(
                    own, lands[part].at[slot], send_sem.at[part, zi, bi], recv_sem.at[part, slot], device_id=to, device_id_type=MESH_ID
                )

            def work(own=own, other=other, children=children, send=send, which=which, rows=rows):
                for land, wait, ok in children:
                    when(ok, lambda wait=wait: wait.wait_recv())
                total = own[...].astype(F32) + other[...].astype(F32)
                for land, wait, ok in children:
                    term = land[...].astype(F32)
                    total = total + (term if ok is True else jnp.where(ok, term, 0.0))
                if send is None:
                    outs[which][rows] = total
                else:
                    own[...] = total.astype(BF16)
                    send.start()

            events[part * 100 + offsets(depth).index(offset)] = lambda valid=valid, work=work: when(valid, work)
            if send is not None:
                ends.append(lambda valid=valid, send=send: when(valid, lambda: send.wait_send()))
    return events, ends


REDUCE_PARTS = (
    ("zxy", 0, 0, 96),
    ("zyx", 1, 0, 96),
    ("zxy", 2, 0, 16),
)

REDUCE_STEPS = (
    (),
    (27, 26, 23, 22, 16, 15),
    (8,),
    (24, 20, 25, 21, 18, 14),
    (10, 7, 3),
    (17, 13),
    (),
    (9, 6),
    (),
    (),
    (),
    (2,),
    (),
    (19, 12, 127, 126, 124, 123),
    (122, 120, 117, 116, 115, 113),
    (109, 108, 106, 102),
    (),
    (11, 5),
    (),
    (),
    (),
    (),
    (4, 1),
    (125, 121, 118, 114, 110, 107),
    (),
    (119, 112, 227, 226, 223, 222, 216, 215, 208, 225, 221, 218, 214, 210, 207, 203, 0, 103),
    (111, 105, 224, 217, 209, 219, 220, 213, 206, 202, 212, 104, 205, 101, 211, 201, 204, 100, 200),
)


def backward_kernel(remote, *refs):
    (tok, halo, cot_hbm, mid_hbm, two_hbm, act_t_hbm, wm_hbm, wa_hbm, rows_ref, units_ref) = refs[:10]
    (q_hbm, k_hbm, v_hbm, ctx_hbm, lse, segk_row, segk_col) = refs[10:17]
    output_hbm, sum_m, sum_a, sum_v, result_hbm, rest_hbm, back_hbm = refs[17:24]
    (cot, two, cot_t, two_t, mid, out_acc, gact, low_ref, wm, wa, q, k, v, ctx, stage_m) = refs[24:39]
    (grad_one, dk_acc, dv_acc, dq_acc, kt, do_ref, sums, gunits, qsum, vsum, gvec) = refs[39:50]
    (in_sem, wm_sem, wa_sem, group_sem, out_sem) = refs[50:55]
    rows, width = tok.shape
    groups = wm_hbm.shape[0]
    head_width = q.shape[1]
    units = units_ref.shape[2]
    segq_row = segk_row.at[:, pl.ds(rows, rows)]
    narrow = wa.shape[2]
    stage_a = wm.at[1, :, :, pl.ds(0, narrow)]
    depth = 4
    tick = Ticker(None, None)
    if remote:
        count = len(REDUCE_PARTS)
        (acc_m, acc_a, acc_v, core_m, core_a, core_v, halo_land) = refs[55:62]
        lands = refs[62 : 62 + count]
        core_send, core_recv, send_sem, recv_sem, halo_send, halo_recv = refs[62 + count :]
        z, y, x, core = position()
        dp, tensor = lax.axis_index("dp"), lax.axis_index("tensor")
        sibling = device(z, y, x, 1 - core)
        order = [((1 - x) * 2 + 1 - core, 1 - x, False), ((1 - x) * 2 + core, 1 - x, True), (x * 2 + 1 - core, x, False), (x * 2 + core, x, True)]
        events, ends = reduce_events(
            REDUCE_PARTS, depth, (acc_m, acc_a, acc_v), (core_m, core_a, core_v), lands, (sum_m, sum_a, sum_v), send_sem, recv_sem
        )
        over = {}
        for which, (stage, cores) in enumerate(((stage_m, core_m), (stage_a, core_a))):
            for step, side in ((0, 1 - x), (2, x)):
                over[which, step] = pltpu.make_async_remote_copy(
                    stage, cores.at[side], core_send.at[which, step // 2], core_recv.at[which, step // 2], device_id=sibling, device_id_type=MESH_ID
                )
        wait_neighbours = meet_neighbours(depth)
        tick = Ticker(events, REDUCE_STEPS)
    else:
        order = [(t, 0, False) for t in range(groups)]
    t_of = [item[0] for item in order]

    load = lambda source, target, number: pltpu.make_async_copy(source, target, in_sem.at[number])
    inputs = [load(cot_hbm, cot, 0), load(two_hbm, two, 1), load(mid_hbm, mid, 2)]
    for copy in inputs:
        copy.start()
    wm_loads = [pltpu.make_async_copy(wm_hbm.at[t_of[s]], wm.at[s % 2], wm_sem.at[s % 2]) for s in range(groups)]
    wa_loads = [pltpu.make_async_copy(wa_hbm.at[t_of[s]], wa.at[s % 2], wa_sem.at[s % 2]) for s in range(groups)]
    group_loads = [
        [
            pltpu.make_async_copy(source.at[t_of[s]], target, group_sem.at[i])
            for i, (source, target) in enumerate(((q_hbm, q), (k_hbm, k), (v_hbm, v), (ctx_hbm, ctx)))
        ]
        for s in range(groups)
    ]
    wm_loads[0].start()
    wm_loads[1].start()
    wa_loads[0].start()
    for copy in group_loads[0]:
        copy.start()
    inputs[1].wait()
    two_t[...] = two[...].T
    inputs[0].wait()
    cot_t[...] = cot[...].T
    out_acc[...] = jnp.zeros_like(out_acc)
    gact[...] = jnp.zeros_like(gact)
    sums[...] = jnp.zeros_like(sums)

    def block_rows(value):
        return value.reshape(SPLIT, width // SPLIT, value.shape[1])

    for s in range(groups):
        t, side, mine = order[s]
        slot = s % 2
        wm_loads[s].wait()
        target = acc_m.at[side] if mine else stage_m
        if remote and s == 2:
            over[0, 0].wait_send()

        def body(block, carry):
            here = pl.ds(pl.multiple_of(block * UNITS, UNITS), UNITS)
            there = pl.ds(pl.multiple_of(units + block * UNITS, UNITS), UNITS)
            gin, gback = mlp_block(
                two, cot, two_t, cot_t, wm[slot, :, :, here].reshape(width, UNITS), wm[slot, :, :, there].reshape(width, UNITS), units_ref[t, :, here], out_acc, gact, gunits.at[t, :, here]
            )
            target[:, :, here] = block_rows(gin)
            target[:, :, there] = block_rows(gback)
            return carry

        lax.fori_loop(0, units // UNITS, body, 0)
        if remote:
            if s == 0:
                wait_neighbours()
            if not mine:
                over[0, s].start()
            else:
                over[0, s - 1].wait_recv()
        else:
            copy = pltpu.make_async_copy(stage_m, rest_hbm[0].at[t], out_sem.at[0])
            copy.start()
            copy.wait()
        if s + 2 < groups:
            wm_loads[s + 2].start()
        tick()
    act_t = wm.at[0]
    act_load = pltpu.make_async_copy(act_t_hbm, act_t, wm_sem.at[0])
    act_load.start()
    inputs[2].wait()
    upstream = cot[...].astype(F32)
    normed, rate = norm_parts(mid[...])
    two[...] = (mid[...] + out_acc[...] + rows_ref[7:8, :]).astype(BF16)
    output_store = pltpu.make_async_copy(two, output_hbm, out_sem.at[1])
    output_store.start()
    grad_two = gact[...]
    gmid = upstream + norm_pull(grad_two, normed, rate, rows_ref[5:6, :])
    mid[...] = gmid
    low_ref[...] = gmid.astype(BF16)
    sums[4:5, :] = jnp.sum(gmid, axis=0, keepdims=True)
    sums[5:6, :] = jnp.sum(grad_two * normed, axis=0, keepdims=True)
    sums[6:7, :] = jnp.sum(grad_two, axis=0, keepdims=True)
    sums[7:8, :] = jnp.sum(upstream, axis=0, keepdims=True)
    low_t = two_t
    low_t[...] = low_ref[...].T
    halo_loads = [
        pltpu.make_async_copy(halo.at[0], cot, in_sem.at[0]),
        pltpu.make_async_copy(halo.at[1], wa.at[groups % 2, pl.ds(0, rows)], in_sem.at[1]),
    ]
    halo_loads[0].start()
    tick()
    act_load.wait()
    for s in range(groups):
        t, side, mine = order[s]
        wa_loads[s].wait()
        for copy in group_loads[s]:
            copy.wait()
        if s + 1 < groups:
            wa_loads[s + 1].start()
        else:
            halo_loads[1].start()
        weights = wa[s % 2]
        target = acc_a.at[side] if mine else stage_a
        if remote and s == 2:
            over[1, 0].wait_send()
        first, second, third = head_width, 2 * head_width, 3 * head_width
        do_ref[...] = mxu(low_ref[...], weights[:, third:], NN).astype(BF16)
        target[:, :, third:] = block_rows(mxu(low_t[...], ctx[...], NN).astype(BF16))
        tick()
        pull_group(q, k, v, do_ref, ctx, lse.at[t], segq_row, segk_col, kt, dk_acc, dv_acc, dq_acc, lambda: tick())
        if s + 1 < groups:
            for copy in group_loads[s + 1]:
                copy.start()
        dq = (dq_acc[...] * HEAD_DIM**-0.5).T.astype(BF16)
        dk = dk_acc[...].astype(BF16)
        dv = dv_acc[...].astype(BF16)
        qsum[t] = jnp.sum(dq.astype(F32), axis=0, keepdims=True)
        vsum[t] = jnp.sum(dv_acc[...], axis=0, keepdims=True)
        target[:, :, :first] = block_rows(mxu(act_t[:, :, rows : 2 * rows].reshape(width, rows), dq, NN).astype(BF16))
        both = jnp.concatenate([dk, dv], axis=1)
        target[:, :, first:third] = block_rows(mxu(act_t[...].reshape(width, 3 * rows), both, NN).astype(BF16))
        if remote:
            if not mine:
                over[1, s].start()
            else:
                over[1, s - 1].wait_recv()
        tick()
        lanes = weights[:, first:third]
        for part in range(3):
            here = slice(part * rows, (part + 1) * rows)
            value = mxu(both[here], lanes, NT)
            if part == 1:
                value = value + mxu(dq, weights[:, :first], NT)
            if s == 0:
                grad_one[here, :] = value
            else:
                grad_one[here, :] += value
        if not remote:
            copy = pltpu.make_async_copy(stage_a, rest_hbm[1].at[t], out_sem.at[0])
            copy.start()
            copy.wait()
        tick()
    output_store.wait()
    low_ref[...] = grad_one[:rows, :].astype(BF16)
    two[...] = grad_one[2 * rows :, :].astype(BF16)
    if remote:
        finish_halo = exchange_halo(low_ref, two, halo_land, halo_send, halo_recv, low_ref, two)
    gain_sum = jnp.zeros((1, width), F32)
    for copy in halo_loads:
        copy.wait()
    for part, source in enumerate((cot, tok, wa.at[groups % 2, pl.ds(0, rows)])):
        normed, rate = norm_parts(source[...].astype(F32))
        gain_sum = gain_sum + jnp.sum(grad_one[part * rows : (part + 1) * rows, :] * normed, axis=0, keepdims=True)
    sums[0:1, :] = gain_sum
    sums[1:2, :] = jnp.sum(grad_one[...], axis=0, keepdims=True)
    for t in range(groups):
        sums[2:3, t * head_width : (t + 1) * head_width] = qsum[t]
        sums[3:4, t * head_width : (t + 1) * head_width] = vsum[t]
    pack_vectors(sums, gunits, gvec, SPLIT)
    if not remote:
        copies = [
            pltpu.make_async_copy(low_ref, rest_hbm[2].at[0], out_sem.at[0]),
            pltpu.make_async_copy(two, rest_hbm[2].at[1], out_sem.at[1]),
            pltpu.make_async_copy(grad_one.at[pl.ds(rows, rows)], result_hbm, out_sem.at[2]),
            pltpu.make_async_copy(mid, back_hbm, out_sem.at[3]),
            pltpu.make_async_copy(gvec, rest_hbm[3], out_sem.at[4]),
        ]
        for copy in copies:
            copy.start()
        for copy in copies:
            copy.wait()
        return
    acc_v[0] = gvec[...]
    acc_v[1] = gvec[...]
    over_v = [
        pltpu.make_async_remote_copy(
            gvec, core_v.at[side], core_send.at[2, side], core_recv.at[2, side], device_id=sibling, device_id_type=MESH_ID
        )
        for side in range(2)
    ]
    for copy in over_v:
        copy.start()
    for copy in over_v:
        copy.wait_recv()
    tick()
    finish_halo()
    from_left = jnp.where(tensor > 0, halo_land[0].astype(F32), 0.0)
    from_right = jnp.where(tensor < 3, halo_land[1].astype(F32), 0.0)
    normed, rate = norm_parts(tok[...].astype(F32))
    total = grad_one[rows : 2 * rows, :] + from_left + from_right
    out_acc[...] = mid[...] + norm_pull(total, normed, rate, rows_ref[0:1, :])
    result_store = pltpu.make_async_copy(out_acc, result_hbm, out_sem.at[2])
    result_store.start()
    tick()
    for end in ends:
        end()
    over[0, 2].wait_send()
    over[1, 2].wait_send()
    for copy in over_v:
        copy.wait_send()
    result_store.wait()


def backward_rows(remote, tok, halo, cot, middle, act_two, act_t, wm, wa, rows_ref, units_ref, q, k, v, ctx, lse, segk_row, segk_col):
    rows, width = tok.shape
    groups, wide = wm.shape[0], wm.shape[-1]
    narrow = wa.shape[2]
    head_width = narrow // 4
    shape = jax.ShapeDtypeStruct
    vmem = pltpu.VMEM
    dma = lambda *dims: pltpu.SemaphoreType.DMA(dims)
    in_specs = [VMEM_SPEC, HBM_SPEC] + [HBM_SPEC] * 6 + [VMEM_SPEC] * 2 + [HBM_SPEC] * 4 + [VMEM_SPEC] * 3
    piece = width // SPLIT
    if remote:
        out_shape = (
            shape((rows, width), BF16),
            shape((piece, wide), F32),
            shape((piece, narrow), F32),
            shape((16, 128), F32),
            shape((rows, width), F32),
        )
        out_specs = (HBM_SPEC, VMEM_SPEC, VMEM_SPEC, VMEM_SPEC, HBM_SPEC)
    else:
        out_shape = (
            shape((rows, width), BF16),
            shape((groups, SPLIT, piece, wide), BF16),
            shape((groups, SPLIT, piece, narrow), BF16),
            shape((SPLIT, 16, 128), BF16),
            shape((2, rows, width), BF16),
            shape((rows, width), F32),
            shape((rows, width), F32),
        )
        out_specs = (HBM_SPEC,) * 7
    scratch = [
        vmem((rows, width), BF16),
        vmem((rows, width), BF16),
        vmem((width, rows), BF16),
        vmem((width, rows), BF16),
        vmem((rows, width), F32),
        vmem((rows, width), F32),
        vmem((rows, width), F32),
        vmem((rows, width), BF16),
        vmem((2, SPLIT, piece, wide), BF16),
        vmem((2, width, narrow), BF16),
        vmem((rows, head_width), BF16),
        vmem((3 * rows, head_width), BF16),
        vmem((3 * rows, head_width), BF16),
        vmem((rows, head_width), BF16),
        vmem((SPLIT, piece, wide), BF16),
        vmem((3 * rows, width), F32),
        vmem((3 * rows, head_width), F32),
        vmem((3 * rows, head_width), F32),
        vmem((head_width, rows), F32),
        vmem((head_width, 3 * rows), BF16),
        vmem((rows, head_width), BF16),
        vmem((VEC_ROWS, width), F32),
        vmem(units_ref.shape, F32),
        vmem((groups, 1, head_width), F32),
        vmem((groups, 1, head_width), F32),
        vmem((SPLIT, 16, 128), BF16),
        dma(3),
        dma(2),
        dma(2),
        dma(4),
        dma(5),
    ]
    params = dict(vmem_limit_bytes=VMEM_LIMIT)
    if remote:
        n = len(REDUCE_PARTS)
        sizes = ((piece, wide), (piece, narrow), (16, 128))
        slots = [4 * len(land_slots(p[0], 4)) for p in REDUCE_PARTS]
        scratch += [vmem((2, SPLIT) + size, BF16) for size in sizes]
        scratch += [vmem((2, SPLIT) + size, BF16) for size in sizes]
        scratch += [vmem((2, rows, width), BF16)]
        scratch += [vmem((slots[i], p[3], sizes[p[1]][1]), BF16) for i, p in enumerate(REDUCE_PARTS)]
        scratch += [dma(3, 2), dma(3, 2), dma(n, 4, 4), dma(n, max(slots)), dma(4), dma(2)]
        params.update(collective_id=1, has_side_effects=True)

    def kernel(*refs):
        ins, outs, rest = refs[:17], refs[17 : 17 + len(out_shape)], refs[17 + len(out_shape) :]
        if remote:
            outs = (outs[0], outs[1], outs[2], outs[3], outs[4], None, None)
        else:
            outs = (outs[0], None, None, None, outs[5], (outs[1], outs[2], outs[4], outs[3]), outs[6])
        backward_kernel(remote, *ins, *outs, *rest)

    return pl.pallas_call(
        kernel,
        out_shape=out_shape,
        in_specs=in_specs,
        out_specs=out_specs,
        scratch_shapes=scratch,
        compiler_params=pltpu.CompilerParams(**params),
        name="backward_rows",
    )(tok, halo, cot, middle, act_two, act_t.reshape(SPLIT, piece, 3 * rows), wm, wa, rows_ref, units_ref, q, k, v, ctx, lse, segk_row, segk_col)


def finish_kernel(piece, out_in, grad_in, sum_m, sum_a, sum_v, out, grad, *rest):
    *results, out_s, grad_s, m_s, a_s, v_s, sem, back_sem = rest
    pairs = ((out_in, out_s), (grad_in, grad_s), (sum_a, a_s), (sum_m, m_s), (sum_v, v_s))
    loads = [pltpu.make_async_copy(source, target, sem.at[i]) for i, (source, target) in enumerate(pairs)]
    for copy in loads:
        copy.start()
    stores = [pltpu.make_async_copy(out_s, out, back_sem.at[0]), pltpu.make_async_copy(grad_s, grad, back_sem.at[1])]
    for load, store in zip(loads[:2], stores):
        load.wait()
        store.start()
    for copy in loads[2:]:
        copy.wait()
    sum_m, sum_a, sum_v = m_s, a_s, v_s
    g_q, g_k, g_v, g_o, g_in, g_back, *lines = results
    head_width, units = g_q.shape[1], g_in.shape[1]
    total = sum_a[...]
    g_q[...] = total[:, :head_width]
    g_k[...] = total[:, head_width : 2 * head_width]
    g_v[...] = total[:, 2 * head_width : 3 * head_width]
    g_o[...] = total[:, 3 * head_width :].T
    g_in[...] = sum_m[:, :units]
    g_back[...] = sum_m[:, units:]
    for i in range(SHIFTS):
        lines[i][...] = sum_v[i : i + 1, :piece]
    for row in range(lines[SHIFTS].shape[0] // 128):
        lines[SHIFTS][row * 128 : (row + 1) * 128] = sum_v[SHIFTS + row, :]
    for copy in stores:
        copy.wait()


def finish_rows(output, grad_tokens, sum_m, sum_a, sum_v, unit_piece):
    piece, wide = sum_m.shape
    narrow = sum_a.shape[1]
    line = lambda n: jax.ShapeDtypeStruct((1, n), F32)
    shape = lambda *dims: jax.ShapeDtypeStruct(dims, F32)
    quarter = shape(piece, narrow // 4)
    half = shape(piece, wide // 2)
    return pl.pallas_call(
        functools.partial(finish_kernel, piece),
        out_shape=(
            jax.ShapeDtypeStruct(output.shape, output.dtype),
            jax.ShapeDtypeStruct(grad_tokens.shape, grad_tokens.dtype),
            quarter,
            quarter,
            quarter,
            shape(narrow // 4, piece),
            half,
            half,
        )
        + (line(piece),) * SHIFTS
        + (shape(unit_piece),),
        in_specs=[pl.BlockSpec(memory_space=pltpu.HBM)] * 5,
        out_specs=(pl.BlockSpec(memory_space=pltpu.HBM),) * 2 + (VMEM_SPEC,) * (7 + SHIFTS),
        scratch_shapes=[
            pltpu.VMEM(output.shape, output.dtype),
            pltpu.VMEM(grad_tokens.shape, F32),
            pltpu.VMEM(sum_m.shape, F32),
            pltpu.VMEM(sum_a.shape, F32),
            pltpu.VMEM(sum_v.shape, F32),
            pltpu.SemaphoreType.DMA((5,)),
            pltpu.SemaphoreType.DMA((2,)),
        ],
        compiler_params=pltpu.CompilerParams(vmem_limit_bytes=VMEM_LIMIT),
        name="finish_rows",
    )(output, grad_tokens, sum_m, sum_a, sum_v)


def per_device(by_kernel, *args):
    (
        tokens,
        cotangent,
        segment_ids,
        ln1_gain,
        ln1_bias,
        w_query,
        query_bias,
        w_key,
        w_value,
        value_bias,
        w_out,
        out_bias,
        ln2_gain,
        ln2_bias,
        w_in,
        in_bias,
        w_back,
        back_bias,
    ) = args
    rows, width = tokens.shape
    n_dp, n_tensor = lax.axis_size("dp"), lax.axis_size("tensor")
    index = lax.axis_index("tensor")
    head_width = w_query.shape[1]
    units = w_in.shape[1]
    piece = ln1_gain.shape[0]
    unit_piece = in_bias.shape[0]

    vectors = (ln1_gain, ln1_bias, query_bias, value_bias, out_bias, ln2_gain, ln2_bias, back_bias)
    if by_kernel:
        lines = [vector.reshape(1, piece) for vector in vectors]
        sources = (w_in, w_back.T, w_query, w_key, w_value, w_out, *lines, in_bias.reshape(-1, 128))
        full_mlp, full_att, halo, *saved = forward_rows(True, tokens, segment_ids, units, *sources)
    else:
        shard_mlp = jnp.concatenate([w_in, w_back.T], axis=1)
        shard_att = jnp.concatenate([w_query, w_key, w_value, w_out.T], axis=1)
        edge = jnp.full((rows,), -1, jnp.int32)
        segs = jnp.concatenate([edge, segment_ids[0], edge])
        segs = lax.dynamic_slice_in_dim(segs, index * rows, 3 * rows)[None, :]
        shard_vec = jnp.concatenate([jnp.stack(vectors).reshape(-1), in_bias])
        full_mlp, full_att, full_vec, halo = gather_by_ops((shard_mlp, shard_att, shard_vec), tokens)
        flat = full_vec[0]
        rows8 = jnp.swapaxes(flat[:, : 8 * piece].reshape(n_dp, 8, piece), 0, 1).reshape(8, SPLIT, width // SPLIT)
        rows8 = jnp.pad(jnp.swapaxes(rows8, 0, 1), ((0, 0), (0, 0), (0, 128 - width // SPLIT)))
        unit_rows = flat[:, 8 * piece :].reshape(SPLIT, -1, 128)
        full_vec = jnp.concatenate([rows8, unit_rows], axis=1)
        full_vec = jnp.pad(full_vec, ((0, 0), (0, 16 - full_vec.shape[1]), (0, 0)))
        full_mlp = full_mlp.reshape(n_tensor, SPLIT, width // SPLIT, 2 * units)
        full_att = full_att.reshape(n_tensor, SPLIT, width // SPLIT, 4 * head_width)
        saved = forward_rows(False, tokens, segs, units, halo, full_att, full_vec)
    rows_vec, units_vec, segk_row, segk_col, lse, act_t, query, keys, values, context, middle, act_two = saved
    full_att = full_att.reshape(n_tensor, width, 4 * head_width)
    results = backward_rows(
        by_kernel, tokens, halo, cotangent, middle, act_two, act_t, full_mlp, full_att, rows_vec, units_vec, query, keys, values,
        context, lse, segk_row, segk_col,
    )
    if by_kernel:
        output, sum_mlp, sum_att, sum_vec, grad_tokens = results
        output, grad_tokens, g_wq, g_wk, g_wv, g_wo, g_win, g_wback, *vec = finish_rows(
            output, grad_tokens, sum_mlp, sum_att, sum_vec, unit_piece
        )
        vec = [line.reshape(-1) for line in vec]
    else:
        output, grad_mlp, grad_att, grad_vec, halo_rows, grad_own, grad_middle = results
        split = lambda array: array.reshape(n_tensor, n_dp, width // n_dp, array.shape[-1])
        rows8 = jnp.swapaxes(grad_vec[:, :8, : width // 8], 0, 1).reshape(8, n_dp, piece)
        unit_flat = grad_vec[:, 8 : 8 + unit_piece * n_dp // SPLIT // 128].reshape(n_dp, unit_piece)
        flat = jnp.concatenate([jnp.swapaxes(rows8, 0, 1).reshape(n_dp, 8 * piece), unit_flat], axis=1)
        flat = jnp.broadcast_to(flat[None], (n_tensor,) + flat.shape)
        sum_mlp, sum_att, sum_vec, halo_back = reduce_by_ops((split(grad_mlp), split(grad_att), flat), halo_rows)
        vec = [sum_vec[i * piece : (i + 1) * piece] for i in range(8)] + [sum_vec[8 * piece :]]
        from_left = jnp.where(index > 0, halo_back[0].astype(F32), 0.0)
        from_right = jnp.where(index < n_tensor - 1, halo_back[1].astype(F32), 0.0)
        norm_one, rate_one = norm_parts(tokens.astype(F32))
        grad_tokens = grad_middle + norm_pull(grad_own + from_left + from_right, norm_one, rate_one, rows_vec[0:1])
        g_wq, g_wk, g_wv = (sum_att[:, i * head_width : (i + 1) * head_width] for i in range(3))
        g_wo = sum_att[:, 3 * head_width :].T
        g_win, g_wback = sum_mlp[:, :units], sum_mlp[:, units:]
    g_ln1_gain, g_ln1_bias, g_q, g_v, g_o, g_ln2_gain, g_ln2_bias, g_b, g_i = vec
    return (
        output,
        grad_tokens,
        g_ln1_gain,
        g_ln1_bias,
        g_wq,
        g_q,
        g_wk,
        g_wv,
        g_v,
        g_wo,
        g_o,
        g_ln2_gain,
        g_ln2_bias,
        g_win,
        g_i,
        g_wback.T,
        g_b,
    )


def solution(mesh):
    by_kernel = mesh.shape["dp"] == 8 and mesh.shape["tensor"] == 4
    rows = P(("dp", "tensor"), None)
    line, first, second = P("dp"), P("dp", "tensor"), P("tensor", "dp")
    return jax.shard_map(
        functools.partial(per_device, by_kernel),
        mesh=mesh,
        in_specs=(rows, rows, P("dp", None), line, line, first, line, first, first, line, second, line, line, line, first, line, second, line),
        out_specs=(rows, rows, line, line, first, line, first, first, line, second, line, line, line, first, line, second, line),
        check_vma=False,
    )
```

```python
import functools

import jax
import jax.numpy as jnp
from jax import lax
from jax.experimental import pallas as pl
from jax.experimental.pallas import tpu as pltpu
from jax.sharding import PartitionSpec as P

HEAD_DIM = 64
EPSILON = 1e-12
MASKED = -1000000000.0
MESH_ID = pl.DeviceIdType.MESH
F32 = jnp.float32
BF16 = jnp.bfloat16

NN = (((1,), (0,)), ((), ()))
NT = (((1,), (1,)), ((), ()))
TN = (((0,), (0,)), ((), ()))


def mxu(left, right, dims):
    return lax.dot_general(left, right, dims, preferred_element_type=F32)


def position():
    dp = lax.axis_index("dp")
    tensor = lax.axis_index("tensor")
    return dp // 2, dp % 2, tensor // 2, tensor % 2


def device(z, y, x, core):
    return (z * 2 + y, x * 2 + core)


def offsets(depth):
    found = [(dz, dy, dx) for dz in range(1 - depth, depth) for dy in range(2) for dx in range(2)]
    return sorted(found, key=lambda item: abs(item[0]) + item[1] + item[2])


def level(route, offset):
    dims = dict(zip("zyx", offset))
    last = -1
    for place, name in enumerate(route):
        if dims[name] != 0:
            last = place
    return last


def when(condition, action):
    if condition is True:
        action()
    else:
        pl.when(condition)(action)


def meet_neighbours(depth):
    z, y, x, core = position()
    dp, tensor = lax.axis_index("dp"), lax.axis_index("tensor")
    barrier = pltpu.get_barrier_semaphore()

    def signal(target):
        pl.semaphore_signal(barrier, inc=1, device_id=target, device_id_type=MESH_ID)

    signal(device(z, y, x, 1 - core))
    signal(device(z, y, 1 - x, core))
    signal(device(z, 1 - y, x, core))
    pl.when(z > 0)(lambda: signal(device(z - 1, y, x, core)))
    pl.when(z < depth - 1)(lambda: signal(device(z + 1, y, x, core)))
    middle = (tensor == 1) | (tensor == 2)
    pl.when(middle)(lambda: signal((dp, 3 - tensor)))
    as_int = lambda flag: flag.astype(jnp.int32)
    return lambda: pl.semaphore_wait(barrier, 3 + as_int(z > 0) + as_int(z < depth - 1) + as_int(middle))


def tree_sends(route, offset, depth):
    z, y, x, core = position()
    dz = offset[0]
    lev = level(route, offset)
    sends = []
    for place, name in enumerate(route):
        if name == "z":
            if place < lev:
                continue
            if place > lev or dz < 0:
                sends.append((0, device(jnp.minimum(z + 1, depth - 1), y, x, core), z < depth - 1, 0))
            if place > lev or dz > 0:
                sends.append((1, device(jnp.maximum(z - 1, 0), y, x, core), z > 0, 0))
        elif place > lev:
            if name == "y":
                sends.append((2, device(z, 1 - y, x, core), True, 2))
            else:
                sends.append((3, device(z, y, 1 - x, core), True, 1))
    return sends


def tree_parent(route, offset):
    z, y, x, core = position()
    dz, dy, dx = offset
    name = route[level(route, offset)]
    if name == "z":
        if dz < 0:
            return 0, device(z - 1, y, x, core)
        return 1, device(z + 1, y, x, core)
    if name == "y":
        return 2, device(z, 1 - y, x, core)
    return 3, device(z, y, 1 - x, core)


def exchange_halo(rows_left, rows_right, halo, halo_send, halo_recv, own_left, own_right):
    dp, tensor = lax.axis_index("dp"), lax.axis_index("tensor")
    has_left, has_right = tensor > 0, tensor < 3
    to_right = pltpu.make_async_remote_copy(
        rows_right, halo.at[0], halo_send.at[0], halo_recv.at[0], device_id=(dp, jnp.minimum(tensor + 1, 3)), device_id_type=MESH_ID
    )
    to_left = pltpu.make_async_remote_copy(
        rows_left, halo.at[1], halo_send.at[1], halo_recv.at[1], device_id=(dp, jnp.maximum(tensor - 1, 0)), device_id_type=MESH_ID
    )
    fill_left = pltpu.make_async_copy(own_left, halo.at[0], halo_send.at[2])
    fill_right = pltpu.make_async_copy(own_right, halo.at[1], halo_send.at[3])
    pl.when(has_right)(lambda: to_right.start())
    pl.when(has_left)(lambda: to_left.start())
    pl.when(~has_left)(lambda: fill_left.start())
    pl.when(~has_right)(lambda: fill_right.start())

    def finish():
        pl.when(has_right)(lambda: to_right.wait_send())
        pl.when(has_left)(lambda: to_left.wait_send())
        pl.when(has_left)(lambda: to_right.wait_recv())
        pl.when(has_right)(lambda: to_left.wait_recv())
        pl.when(~has_left)(lambda: fill_left.wait())
        pl.when(~has_right)(lambda: fill_right.wait())

    return finish


def gather_events(parts, depth, srcs, outs, send_sem, recv_sem, core_send, core_recv):
    z, y, x, core = position()
    sibling = device(z, y, x, 1 - core)
    events, backs, ends = {}, {}, []

    def piece(part, offset, owner_core):
        dz, dy, dx = offset
        _, which, begin, size = parts[part]
        oy = 1 - y if dy else y
        ox = 1 - x if dx else x
        return outs[which].at[ox * 2 + owner_core, (z + dz) * 2 + oy, pl.ds(begin, size)]

    for number, offset in enumerate(offsets(depth)):
        for part, (route, which, begin, size) in enumerate(parts):
            dz, dy, dx = offset
            mine = offset == (0, 0, 0)
            target = piece(part, offset, core)
            block = srcs[which].at[pl.ds(begin, size)] if mine else target
            zi, bi = z + dz, dy * 2 + dx
            valid = True if dz == 0 else ((z + dz >= 0) & (z + dz <= depth - 1))
            sends = []
            for way, to, ok, shift in tree_sends(route, offset, depth):
                copy = pltpu.make_async_remote_copy(
                    block, target, send_sem.at[part, way, zi, bi], recv_sem.at[part, zi, bi + shift], device_id=to, device_id_type=MESH_ID
                )
                sends.append((copy, ok))
            arrival = pltpu.make_async_remote_copy(
                block, target, send_sem.at[part, 0, 0, 0], recv_sem.at[part, zi, bi], device_id=sibling, device_id_type=MESH_ID
            )
            over = pltpu.make_async_remote_copy(
                block, target, core_send.at[part, zi, bi], core_recv.at[part, zi, bi], device_id=sibling, device_id_type=MESH_ID
            )
            other = piece(part, offset, 1 - core)
            back = pltpu.make_async_remote_copy(
                other, other, core_send.at[part, zi, bi], core_recv.at[part, zi, bi], device_id=sibling, device_id_type=MESH_ID
            )

            def arrive(sends=sends, arrival=arrival, over=over, mine=mine):
                if not mine:
                    arrival.wait_recv()
                for copy, ok in sends:
                    when(ok, lambda copy=copy: copy.start())
                over.start()

            def finish(sends=sends, over=over):
                for copy, ok in sends:
                    when(ok, lambda copy=copy: copy.wait_send())
                over.wait_send()

            events[part * 100 + number] = lambda valid=valid, arrive=arrive: when(valid, arrive)
            backs[part * 100 + number] = lambda valid=valid, back=back: when(valid, lambda: back.wait_recv())
            ends.append(lambda valid=valid, finish=finish: when(valid, finish))
    return events, backs, ends


GATHER_PARTS = (
    ("xzy", 1, 0, 48),
    ("yzx", 1, 48, 48),
    ("zyx", 0, 0, 64),
    ("xzy", 0, 64, 32),
)

GATHER_STEPS = (
    (0, 100),
    (1, 101, 3, 103, 4, 104),
    (),
    (),
    (5, 7, 110, 10, 105, 11, 2, 107, 14, 12, 111, 102, 112, 118, 18, 19, 106, 6, 21, 108, 8, 114, 9, 109, 119, 25, 200, 300, 125, 116, 13, 120, 15, 121),
    (113, 16, 17, 124),
    (115, 117),
    (122, 123, 203, 204),
    (201, 303, 304),
    (20, 126, 301, 202, 22, 23, 24),
    (127, 302),
    (),
    (205, 210, 211, 208),
    (26, 305, 311, 27),
    (207, 309),
    (306, 209, 310),
    (212,),
    (206, 307, 312, 219),
    (308, 313, 319),
    (317,),
    (213, 214, 218, 320),
    (220, 324),
    (314, 216, 217, 318, 224, 225),
    (316, 221, 325),
    (315, 321),
    (215, 322, 323, 327, 326, 227, 226, 222, 223),
)


def gather_by_ops(shards, tokens):
    full = []
    for shard in shards:
        over_dp = lax.all_gather(shard, "dp", axis=0, tiled=False)
        full.append(lax.all_gather(over_dp, "tensor", axis=0, tiled=False))
    return tuple(full) + (halo_by_ops(tokens, tokens),)


def halo_by_ops(rows_left, rows_right):
    count = lax.axis_size("tensor")
    from_left = lax.ppermute(rows_right, "tensor", [(i, i + 1) for i in range(count - 1)])
    from_right = lax.ppermute(rows_left, "tensor", [(i, i - 1) for i in range(1, count)])
    return jnp.stack([from_left, from_right])


def reduce_by_ops(grads, halo_rows):
    sums = []
    for grad in grads:
        over_tensor = lax.psum_scatter(grad, "tensor", scatter_dimension=0, tiled=False)
        sums.append(lax.psum_scatter(over_tensor, "dp", scatter_dimension=0, tiled=False).astype(F32))
    return tuple(sums) + (halo_by_ops(halo_rows[0], halo_rows[1]),)


def norm_parts(values):
    center = values - jnp.mean(values, axis=-1, keepdims=True)
    rate = lax.rsqrt(jnp.mean(center * center, axis=-1, keepdims=True) + EPSILON)
    return center * rate, rate


def norm_pull(grad, normed, rate, gain):
    scaled = grad * gain
    return rate * (
        scaled
        - jnp.mean(scaled, axis=-1, keepdims=True)
        - normed * jnp.mean(scaled * normed, axis=-1, keepdims=True)
    )


def head_mask(head):
    lane = lax.broadcasted_iota(jnp.int32, (1, 3 * HEAD_DIM), 1)
    return (lane >= head * HEAD_DIM) & (lane < (head + 1) * HEAD_DIM)


QB = 256
UNITS = 768
VMEM_LIMIT = 63 * 1024 * 1024
VEC_ROWS = 16
SPLIT = 8
SHIFTS = 8
VMEM_SPEC = pl.BlockSpec(memory_space=pltpu.VMEM)
HBM_SPEC = pl.BlockSpec(memory_space=pl.ANY)


class Ticker:
    def __init__(self, steps, table):
        self.steps, self.table, self.point = steps, table, 0

    def __call__(self):
        if self.steps:
            for number in self.table[self.point]:
                self.steps[number]()
        self.point += 1


def unpack_vectors(vec_ref, rows_ref, units_ref, n_dp):
    width, groups = rows_ref.shape[1], units_ref.shape[0]
    piece, unit_rows = width // n_dp, units_ref.shape[2] * groups // n_dp // 128
    pieces = [vec_ref[dp].astype(F32) for dp in range(n_dp)]
    rows_ref[...] = jnp.concatenate([item[:, :piece] for item in pieces], axis=1)
    lines = [item[SHIFTS + row : SHIFTS + row + 1, :] for item in pieces for row in range(unit_rows)]
    per_group = len(lines) // groups
    for group in range(groups):
        units_ref[group] = jnp.concatenate(lines[group * per_group : (group + 1) * per_group], axis=1)


def pack_vectors(rows_ref, units_ref, vec_ref, n_dp):
    width, groups = rows_ref.shape[1], units_ref.shape[0]
    piece, unit_rows = width // n_dp, units_ref.shape[2] * groups // n_dp // 128
    vec_ref[...] = jnp.zeros_like(vec_ref)
    for dp in range(n_dp):
        vec_ref[dp, 0:SHIFTS, 0:piece] = rows_ref[0:SHIFTS, dp * piece : (dp + 1) * piece].astype(BF16)
        for row in range(unit_rows):
            begin = (dp * unit_rows + row) * 128
            group, lane = begin // units_ref.shape[2], begin % units_ref.shape[2]
            vec_ref[dp, SHIFTS + row : SHIFTS + row + 1, :] = units_ref[group, :, lane : lane + 128].astype(BF16)


def attend_block(q, k, v, same):
    total = jnp.zeros(q.shape, F32)
    logs = []
    for head in range(q.shape[1] // HEAD_DIM):
        mask = head_mask(head)
        raw = mxu(jnp.where(mask, q, jnp.zeros_like(q)), k, NT)
        scores = jnp.where(same, raw, MASKED)
        top = jnp.max(scores, axis=1, keepdims=True)
        expo = jnp.exp(scores - top)
        denom = jnp.sum(expo, axis=1, keepdims=True)
        part = mxu(expo.astype(BF16), v, NN)
        total = jnp.where(mask, part / denom, total)
        logs.append(top + jnp.log(denom))
    return total.astype(BF16), logs


def forward_kernel(remote, *refs):
    if remote:
        tok, segs, w_in, w_back, w_query, w_key, w_value, w_out = refs[:8]
        lines, unit_line = refs[8:16], refs[16]
        full_m, full_a, halo_hbm = refs[17:20]
        refs = refs[20:]
    else:
        tok, segs, halo, wa, vec = refs[:5]
        refs = refs[5:]
    rows_ref, units_ref, segk, segcol, lse, *stores_hbm = refs[:12]
    act, attn, logs_ref, qshift, act_t, q, k, v, ctx, middle, act_two, store_sem = refs[12:24]
    if remote:
        halo, wa, vec, shard_m, shard_a, shard_v, segs_all = refs[24:31]
        send_sem, recv_sem, core_send, core_recv, own_sem, vec_send, vec_recv, halo_send, halo_recv = refs[31:]
    rows, width = tok.shape
    groups = wa.shape[0]
    head_width = q.shape[2]
    depth = 4
    tick = Ticker(None, None)
    order = list(range(groups))
    logs_ref[...] = jnp.zeros_like(logs_ref)
    if remote:
        z, y, x, core = position()
        dp, tensor = lax.axis_index("dp"), lax.axis_index("tensor")
        order = [x * 2 + core, x * 2 + 1 - core, (1 - x) * 2 + core, (1 - x) * 2 + 1 - core]
        peers = [lax.rem(dp + shift, SPLIT) for shift in range(1, SPLIT)]
        barrier = pltpu.get_barrier_semaphore()
        middle_pair = (tensor == 1) | (tensor == 2)

        def signal(target):
            pl.semaphore_signal(barrier, inc=1, device_id=target, device_id_type=MESH_ID)

        for peer in peers:
            signal((peer, tensor))
        signal(device(z, y, x, 1 - core))
        signal(device(z, y, 1 - x, core))
        pl.when(middle_pair)(lambda: signal((dp, 3 - tensor)))
        stacked = jnp.concatenate([line[...].astype(F32) for line in lines], axis=0)
        padding = jnp.zeros((SHIFTS, 128 - stacked.shape[1]), F32)
        tail = jnp.zeros((16 - SHIFTS - unit_line.shape[0], 128), F32)
        shard_v[...] = jnp.concatenate(
            [jnp.concatenate([stacked, padding], axis=1), unit_line[...].astype(F32), tail], axis=0
        ).astype(BF16)
        shard_a[...] = jnp.concatenate([w_query[...], w_key[...], w_value[...], w_out[...].T], axis=1)
        shard_m[:, : w_in.shape[1]] = w_in[...]
        shard_m[:, w_in.shape[1] :] = w_back[...]
        edge = jnp.full((1, rows), -1, jnp.int32)
        segs_all[...] = jnp.concatenate([edge, segs[...], edge], axis=1)
        pl.semaphore_wait(barrier, SPLIT + 1 + middle_pair.astype(jnp.int32))
        own = [
            pltpu.make_async_copy(shard_v, vec.at[dp], own_sem.at[0]),
            pltpu.make_async_copy(shard_a, wa.at[tensor, dp], own_sem.at[1]),
            pltpu.make_async_copy(shard_m, full_m.at[tensor, dp], own_sem.at[2]),
        ]
        vec_copies = [
            pltpu.make_async_remote_copy(
                shard_v, vec.at[dp], vec_send.at[i], vec_recv.at[i], device_id=(peer, tensor), device_id_type=MESH_ID
            )
            for i, peer in enumerate(peers)
        ]
        for copy in vec_copies:
            copy.start()
        for copy in own:
            copy.start()
        finish_halo = exchange_halo(tok, tok, halo, halo_send, halo_recv, tok, tok)
        events, backs, ends = gather_events(GATHER_PARTS, depth, (shard_m, shard_a), (full_m, wa), send_sem, recv_sem, core_send, core_recv)
        tick = Ticker(events, GATHER_STEPS)
        tick()
        for i in range(SPLIT - 1):
            source = lax.rem(dp + SPLIT - 1 - i, SPLIT)
            pltpu.make_async_remote_copy(
                vec.at[source], vec.at[source], vec_send.at[i], vec_recv.at[i], device_id=(dp, 3 - tensor), device_id_type=MESH_ID
            ).wait_recv()
        own[0].wait()

    def wait_backs(array, dx):
        if remote:
            for key, step in backs.items():
                part, number = key // 100, key % 100
                if GATHER_PARTS[part][1] == array and (dx is None or offsets(depth)[number][2] == dx):
                    step()

    if remote:
        segk[...] = segs_all[:, pl.ds(pl.multiple_of(tensor * rows, rows), 3 * rows)]
    else:
        segk[...] = segs[...]
    segcol[...] = jnp.broadcast_to(segk[...], (8, 3 * rows)).T
    unpack_vectors(vec, rows_ref, units_ref, SPLIT)
    shifts = rows_ref[0:SHIFTS, :]
    for group in range(groups):
        lanes = slice(group * head_width, (group + 1) * head_width)
        qshift[group] = shifts[:, lanes]
    tick()
    gain, shift = rows_ref[0:1, :], rows_ref[1:2, :]
    for part in (1, 0, 2):
        if remote and part == 0:
            finish_halo()
        source = tok if part == 1 else halo.at[part // 2]
        normed, _ = norm_parts(source[...].astype(F32))
        act[part * rows : (part + 1) * rows, :] = (normed * gain + shift).astype(BF16)
        tick()
    act_t[...] = act[...].T
    stores = [pltpu.make_async_copy(act_t, stores_hbm[0], store_sem.at[0])]
    stores[0].start()
    if remote:
        halo_copy = pltpu.make_async_copy(halo, halo_hbm, own_sem.at[0])
        halo_copy.start()
        own[1].wait()
    for s in range(groups):
        t = order[s]
        if s % 2 == 1:
            wait_backs(1, s // 2)
        if remote and s == groups - 1:
            att_copy = pltpu.make_async_copy(wa, full_a, own_sem.at[1])
            att_copy.start()
        cut = lambda i: wa[t, :, :, i * head_width : (i + 1) * head_width].reshape(width, head_width)
        own_rows = act[rows : 2 * rows, :]
        query = (mxu(own_rows, cut(0), NN) + qshift[t, 2:3, :]).astype(BF16)
        q[t] = query * jnp.asarray(HEAD_DIM**-0.5, BF16)
        k[t] = mxu(act[...], cut(1), NN).astype(BF16)
        tick()
        v[t] = (mxu(act[...], cut(2), NN) + qshift[t, 3:4, :]).astype(BF16)
        tick()
        band = QB + 2 * rows
        for block in range(rows // QB):
            here, keys = pl.ds(block * QB, QB), pl.ds(block * QB, band)
            same = segcol[pl.ds(rows + block * QB, QB), 0:1] == segk[:, keys]
            result, logs = attend_block(q[t, here, :], k[t, keys, :], v[t, keys, :], same)
            ctx[t, here, :] = result
            for head, value in enumerate(logs):
                logs_ref[here, head : head + 1] = value
            tick()
        lse[t] = logs_ref[...].T[0 : lse.shape[1], :]
        part = mxu(ctx[t], cut(3), NT)
        if s == 0:
            attn[...] = part
        else:
            attn[...] += part
        for i, source in enumerate((q, k, v, ctx)):
            stores.append(pltpu.make_async_copy(source.at[t], stores_hbm[1 + i].at[t], store_sem.at[1 + 4 * s + i]))
            stores[-1].start()
        tick()
    total = tok[...].astype(F32) + attn[...] + rows_ref[4:5, :]
    middle[...] = total
    normed, _ = norm_parts(total)
    act_two[...] = (normed * rows_ref[5:6, :] + rows_ref[6:7, :]).astype(BF16)
    for i, source in enumerate((middle, act_two)):
        stores.append(pltpu.make_async_copy(source, stores_hbm[5 + i], store_sem.at[1 + 4 * groups + i]))
        stores[-1].start()
    tick()
    for copy in stores:
        copy.wait()
    if remote:
        wait_backs(0, None)
        own[2].wait()
        for end in ends:
            end()
        for copy in vec_copies:
            copy.wait_send()
        halo_copy.wait()
        att_copy.wait()


def forward_rows(remote, tok, segs, units, *sources):
    rows, width = tok.shape
    groups, head_width = 4, width // 4
    piece = width // SPLIT
    shape = jax.ShapeDtypeStruct
    vmem = pltpu.VMEM
    dma = lambda *dims: pltpu.SemaphoreType.DMA(dims)
    saved = (
        ((width, 3 * rows), BF16),
        ((groups, rows, head_width), BF16),
        ((groups, 3 * rows, head_width), BF16),
        ((groups, 3 * rows, head_width), BF16),
        ((groups, rows, head_width), BF16),
        ((rows, width), F32),
        ((rows, width), BF16),
    )
    out_shape = (
        shape((VEC_ROWS, width), F32),
        shape((groups, 1, units), F32),
        shape((1, 3 * rows), jnp.int32),
        shape((3 * rows, 8), jnp.int32),
        shape((groups, 8, rows), F32),
    ) + tuple(shape(*item) for item in saved)
    out_specs = (VMEM_SPEC,) * 5 + (HBM_SPEC,) * 7
    scratch = [
        vmem((3 * rows, width), BF16),
        vmem((rows, width), F32),
        vmem((rows, 128), F32),
        vmem((groups, SHIFTS, head_width), F32),
    ]
    scratch += [vmem(*item) for item in saved] + [dma(3 + 4 * groups)]
    params = dict(vmem_limit_bytes=VMEM_LIMIT)
    if remote:
        n = len(GATHER_PARTS)
        wide, narrow = (piece, 2 * units), (piece, 4 * head_width)
        out_shape = (
            shape((groups, SPLIT) + wide, BF16),
            shape((groups, SPLIT) + narrow, BF16),
            shape((2, rows, width), BF16),
        ) + out_shape
        out_specs = (HBM_SPEC,) * 3 + out_specs
        scratch += [
            vmem((2, rows, width), BF16),
            vmem((groups, SPLIT) + narrow, BF16),
            vmem((SPLIT, 16, 128), BF16),
            vmem(wide, BF16),
            vmem(narrow, BF16),
            vmem((16, 128), BF16),
            vmem((1, segs.shape[1] + 2 * rows), jnp.int32),
        ]
        scratch += [dma(n, 4, 4, 4), dma(n, 4, 4), dma(n, 4, 4), dma(n, 4, 4), dma(3), dma(SPLIT - 1), dma(SPLIT - 1), dma(4), dma(2)]
        params.update(collective_id=0, has_side_effects=True)
    return pl.pallas_call(
        functools.partial(forward_kernel, remote),
        out_shape=out_shape,
        in_specs=[VMEM_SPEC] * (2 + len(sources)),
        out_specs=out_specs,
        scratch_shapes=scratch,
        compiler_params=pltpu.CompilerParams(**params),
        name="forward_rows",
    )(tok, segs, *sources)


def mlp_block(act, cot, act_t, cot_t, win, wback, bias, out, gact, gbias):
    pre = mxu(act[...], win, NN) + bias
    phi = 0.5 + 0.5 * lax.erf(pre * (0.5**0.5))
    hidden = (pre * phi).astype(BF16)
    slope = phi + pre * (jnp.exp(-0.5 * pre * pre) * 0.3989422804014327)
    grad_pre = mxu(cot[...], wback, NN) * slope
    low = grad_pre.astype(BF16)
    gbias[...] = jnp.sum(grad_pre, axis=0, keepdims=True)
    out[...] += mxu(hidden, wback, NT)
    gact[...] += mxu(low, win, NT)
    return mxu(act_t[...], low, NN).astype(BF16), mxu(cot_t[...], hidden, NN).astype(BF16)


def pull_group(q, k, v, do, ctx, lse, segq_row, segk_col, kt, dk_acc, dv_acc, dq_acc, tick):
    rows, width = q.shape
    heads = width // HEAD_DIM
    kt[...] = k[...].T
    dk_acc[...] = jnp.zeros_like(dk_acc)
    dv_acc[...] = jnp.zeros_like(dv_acc)
    dq_acc[...] = jnp.zeros_like(dq_acc)
    grad = do[...]
    product = grad.astype(F32) * ctx[...].astype(F32)
    row = lax.broadcasted_iota(jnp.int32, (8, width), 0)
    lane = lax.broadcasted_iota(jnp.int32, (8, width), 1)
    pick = jnp.where((lane >= row * HEAD_DIM) & (lane < (row + 1) * HEAD_DIM), 1.0, 0.0)
    delta_all = lax.dot_general(pick, product, NT, precision=lax.Precision.HIGHEST, preferred_element_type=F32)
    for block in range(rows // QB):
        here = pl.ds(block * QB, QB)
        span = slice(block * QB, (block + 1) * QB)
        segq = segq_row[:, here]
        query = q[here, :]
        q_stack = jnp.concatenate([jnp.where(head_mask(h), query, jnp.zeros_like(query)) for h in range(heads)], axis=0)
        do_stack = jnp.concatenate([jnp.where(head_mask(h), grad[span], jnp.zeros_like(query)) for h in range(heads)], axis=0)

        def body(tile, carry):
            keys = pl.ds(pl.multiple_of(block * QB + tile * QB, QB), QB)
            same = segk_col[keys, 0:1] == segq
            raw = mxu(k[keys, :], q_stack, NT)
            grad_weights = mxu(v[keys, :], do_stack, NT)
            dv_part = dk_part = None
            for head in range(heads):
                part = slice(head * QB, (head + 1) * QB)
                probs = jnp.exp(jnp.where(same, raw[:, part], MASKED) - lse[head : head + 1, here])
                grad_raw = (probs * (grad_weights[:, part] - delta_all[head : head + 1, span])).astype(BF16)
                low = probs.astype(BF16)
                spot = slice(head * QB, (head + 1) * QB)
                one, two = mxu(low, do_stack[spot], NN), mxu(grad_raw, q_stack[spot], NN)
                dv_part = one if head == 0 else dv_part + one
                dk_part = two if head == 0 else dk_part + two
                lanes = pl.ds(head * HEAD_DIM, HEAD_DIM)
                dq_acc[lanes, here] += mxu(kt[lanes, keys], grad_raw, NN)
            dv_acc[keys, :] += dv_part
            dk_acc[keys, :] += dk_part
            return carry

        lax.fori_loop(0, (QB + 2 * rows) // QB, body, 0, unroll=True)
        tick()


def land_slots(route, depth):
    ways = []
    for offset in offsets(depth):
        lev = level(route, offset)
        dz, dy, dx = offset
        for place, name in enumerate(route):
            if name == "z":
                if place < lev:
                    continue
                if place > lev or dz < 0:
                    ways.append((0, dy * 2 + dx))
                if place > lev or dz > 0:
                    ways.append((1, dy * 2 + dx))
            elif place > lev:
                ways.append((2 if name == "y" else 3, dy * 2 + dx))
    ways = sorted(set(ways))
    return {way: number * depth for number, way in enumerate(ways)}


def reduce_events(parts, depth, accs, cores, lands, outs, send_sem, recv_sem):
    z, y, x, core = position()
    sibling = device(z, y, x, 1 - core)
    events, ends = {}, []
    for offset in reversed(offsets(depth)):
        for part, (route, which, begin, size) in enumerate(parts):
            slots = land_slots(route, depth)
            dz, dy, dx = offset
            mine = offset == (0, 0, 0)
            zi, bi = z + dz, dy * 2 + dx
            valid = True if dz == 0 else ((z + dz >= 0) & (z + dz <= depth - 1))
            oy = 1 - y if dy else y
            ox = 1 - x if dx else x
            rows = pl.ds(begin, size)
            spot = zi * 2 + oy
            own = accs[which].at[ox, spot, rows]
            other = cores[which].at[ox, spot, rows]
            children = []
            for way, to, ok, shift in tree_sends(route, offset, depth):
                slot = slots[way, bi] + zi
                land = lands[part].at[slot]
                wait = pltpu.make_async_remote_copy(
                    land, land, send_sem.at[part, 0, 0], recv_sem.at[part, slot], device_id=sibling, device_id_type=MESH_ID
                )
                children.append((land, wait, ok))
            send = None
            if not mine:
                way, to = tree_parent(route, offset)
                slot = slots[way, bi - {0: 0, 1: 0, 2: 2, 3: 1}[way]] + zi
                send = pltpu.make_async_remote_copy(
                    own, lands[part].at[slot], send_sem.at[part, zi, bi], recv_sem.at[part, slot], device_id=to, device_id_type=MESH_ID
                )

            def work(own=own, other=other, children=children, send=send, which=which, rows=rows):
                for land, wait, ok in children:
                    when(ok, lambda wait=wait: wait.wait_recv())
                total = own[...].astype(F32) + other[...].astype(F32)
                for land, wait, ok in children:
                    term = land[...].astype(F32)
                    total = total + (term if ok is True else jnp.where(ok, term, 0.0))
                if send is None:
                    outs[which][rows] = total
                else:
                    own[...] = total.astype(BF16)
                    send.start()

            events[part * 100 + offsets(depth).index(offset)] = lambda valid=valid, work=work: when(valid, work)
            if send is not None:
                ends.append(lambda valid=valid, send=send: when(valid, lambda: send.wait_send()))
    return events, ends


REDUCE_PARTS = (
    ("zxy", 0, 0, 96),
    ("zyx", 1, 0, 96),
    ("zxy", 2, 0, 16),
)

REDUCE_STEPS = (
    (),
    (27, 26, 23, 22, 16, 15),
    (8,),
    (24, 20, 25, 21, 18, 14),
    (10, 7, 3),
    (17, 13),
    (),
    (9, 6),
    (),
    (),
    (),
    (2,),
    (),
    (19, 12, 127, 126, 124, 123),
    (122, 120, 117, 116, 115, 113),
    (109, 108, 106, 102),
    (),
    (11, 5),
    (),
    (),
    (),
    (),
    (4, 1),
    (125, 121, 118, 114, 110, 107),
    (),
    (119, 112, 227, 226, 223, 222, 216, 215, 208, 225, 221, 218, 214, 210, 207, 203, 0, 103),
    (111, 105, 224, 217, 209, 219, 220, 213, 206, 202, 212, 104, 205, 101, 211, 201, 204, 100, 200),
)


def backward_kernel(remote, *refs):
    (tok, halo, cot_hbm, mid_hbm, two_hbm, act_t_hbm, wm_hbm, wa_hbm, rows_ref, units_ref) = refs[:10]
    (q_hbm, k_hbm, v_hbm, ctx_hbm, lse, segk_row, segk_col) = refs[10:17]
    output_hbm, sum_m, sum_a, sum_v, result_hbm, rest_hbm, back_hbm = refs[17:24]
    (cot, two, cot_t, two_t, mid, out_acc, gact, low_ref, wm, wa, q, k, v, ctx, stage_m) = refs[24:39]
    (grad_one, dk_acc, dv_acc, dq_acc, kt, do_ref, sums, gunits, qsum, vsum, gvec) = refs[39:50]
    (in_sem, wm_sem, wa_sem, group_sem, out_sem) = refs[50:55]
    rows, width = tok.shape
    groups = wm_hbm.shape[0]
    head_width = q.shape[1]
    units = units_ref.shape[2]
    segq_row = segk_row.at[:, pl.ds(rows, rows)]
    narrow = wa.shape[2]
    stage_a = wm.at[1, :, :, pl.ds(0, narrow)]
    depth = 4
    tick = Ticker(None, None)
    if remote:
        count = len(REDUCE_PARTS)
        (acc_m, acc_a, acc_v, core_m, core_a, core_v, halo_land) = refs[55:62]
        lands = refs[62 : 62 + count]
        core_send, core_recv, send_sem, recv_sem, halo_send, halo_recv = refs[62 + count :]
        z, y, x, core = position()
        dp, tensor = lax.axis_index("dp"), lax.axis_index("tensor")
        sibling = device(z, y, x, 1 - core)
        order = [((1 - x) * 2 + 1 - core, 1 - x, False), ((1 - x) * 2 + core, 1 - x, True), (x * 2 + 1 - core, x, False), (x * 2 + core, x, True)]
        events, ends = reduce_events(
            REDUCE_PARTS, depth, (acc_m, acc_a, acc_v), (core_m, core_a, core_v), lands, (sum_m, sum_a, sum_v), send_sem, recv_sem
        )
        over = {}
        for which, (stage, cores) in enumerate(((stage_m, core_m), (stage_a, core_a))):
            for step, side in ((0, 1 - x), (2, x)):
                over[which, step] = pltpu.make_async_remote_copy(
                    stage, cores.at[side], core_send.at[which, step // 2], core_recv.at[which, step // 2], device_id=sibling, device_id_type=MESH_ID
                )
        wait_neighbours = meet_neighbours(depth)
        tick = Ticker(events, REDUCE_STEPS)
    else:
        order = [(t, 0, False) for t in range(groups)]
    t_of = [item[0] for item in order]

    load = lambda source, target, number: pltpu.make_async_copy(source, target, in_sem.at[number])
    inputs = [load(cot_hbm, cot, 0), load(two_hbm, two, 1), load(mid_hbm, mid, 2)]
    for copy in inputs:
        copy.start()
    wm_loads = [pltpu.make_async_copy(wm_hbm.at[t_of[s]], wm.at[s % 2], wm_sem.at[s % 2]) for s in range(groups)]
    wa_loads = [pltpu.make_async_copy(wa_hbm.at[t_of[s]], wa.at[s % 2], wa_sem.at[s % 2]) for s in range(groups)]
    group_loads = [
        [
            pltpu.make_async_copy(source.at[t_of[s]], target, group_sem.at[i])
            for i, (source, target) in enumerate(((q_hbm, q), (k_hbm, k), (v_hbm, v), (ctx_hbm, ctx)))
        ]
        for s in range(groups)
    ]
    wm_loads[0].start()
    wm_loads[1].start()
    wa_loads[0].start()
    for copy in group_loads[0]:
        copy.start()
    inputs[1].wait()
    two_t[...] = two[...].T
    inputs[0].wait()
    cot_t[...] = cot[...].T
    out_acc[...] = jnp.zeros_like(out_acc)
    gact[...] = jnp.zeros_like(gact)
    sums[...] = jnp.zeros_like(sums)

    def block_rows(value):
        return value.reshape(SPLIT, width // SPLIT, value.shape[1])

    for s in range(groups):
        t, side, mine = order[s]
        slot = s % 2
        wm_loads[s].wait()
        target = acc_m.at[side] if mine else stage_m
        if remote and s == 2:
            over[0, 0].wait_send()

        def body(block, carry):
            here = pl.ds(pl.multiple_of(block * UNITS, UNITS), UNITS)
            there = pl.ds(pl.multiple_of(units + block * UNITS, UNITS), UNITS)
            gin, gback = mlp_block(
                two, cot, two_t, cot_t, wm[slot, :, :, here].reshape(width, UNITS), wm[slot, :, :, there].reshape(width, UNITS), units_ref[t, :, here], out_acc, gact, gunits.at[t, :, here]
            )
            target[:, :, here] = block_rows(gin)
            target[:, :, there] = block_rows(gback)
            return carry

        lax.fori_loop(0, units // UNITS, body, 0)
        if remote:
            if s == 0:
                wait_neighbours()
            if not mine:
                over[0, s].start()
            else:
                over[0, s - 1].wait_recv()
        else:
            copy = pltpu.make_async_copy(stage_m, rest_hbm[0].at[t], out_sem.at[0])
            copy.start()
            copy.wait()
        if s + 2 < groups:
            wm_loads[s + 2].start()
        tick()
    act_t = wm.at[0]
    act_load = pltpu.make_async_copy(act_t_hbm, act_t, wm_sem.at[0])
    act_load.start()
    inputs[2].wait()
    upstream = cot[...].astype(F32)
    normed, rate = norm_parts(mid[...])
    two[...] = (mid[...] + out_acc[...] + rows_ref[7:8, :]).astype(BF16)
    output_store = pltpu.make_async_copy(two, output_hbm, out_sem.at[1])
    output_store.start()
    grad_two = gact[...]
    gmid = upstream + norm_pull(grad_two, normed, rate, rows_ref[5:6, :])
    mid[...] = gmid
    low_ref[...] = gmid.astype(BF16)
    sums[4:5, :] = jnp.sum(gmid, axis=0, keepdims=True)
    sums[5:6, :] = jnp.sum(grad_two * normed, axis=0, keepdims=True)
    sums[6:7, :] = jnp.sum(grad_two, axis=0, keepdims=True)
    sums[7:8, :] = jnp.sum(upstream, axis=0, keepdims=True)
    low_t = two_t
    low_t[...] = low_ref[...].T
    halo_loads = [
        pltpu.make_async_copy(halo.at[0], cot, in_sem.at[0]),
        pltpu.make_async_copy(halo.at[1], wa.at[groups % 2, pl.ds(0, rows)], in_sem.at[1]),
    ]
    halo_loads[0].start()
    tick()
    act_load.wait()
    for s in range(groups):
        t, side, mine = order[s]
        wa_loads[s].wait()
        for copy in group_loads[s]:
            copy.wait()
        if s + 1 < groups:
            wa_loads[s + 1].start()
        else:
            halo_loads[1].start()
        weights = wa[s % 2]
        target = acc_a.at[side] if mine else stage_a
        if remote and s == 2:
            over[1, 0].wait_send()
        first, second, third = head_width, 2 * head_width, 3 * head_width
        do_ref[...] = mxu(low_ref[...], weights[:, third:], NN).astype(BF16)
        target[:, :, third:] = block_rows(mxu(low_t[...], ctx[...], NN).astype(BF16))
        tick()
        pull_group(q, k, v, do_ref, ctx, lse.at[t], segq_row, segk_col, kt, dk_acc, dv_acc, dq_acc, lambda: tick())
        if s + 1 < groups:
            for copy in group_loads[s + 1]:
                copy.start()
        dq = (dq_acc[...] * HEAD_DIM**-0.5).T.astype(BF16)
        dk = dk_acc[...].astype(BF16)
        dv = dv_acc[...].astype(BF16)
        qsum[t] = jnp.sum(dq.astype(F32), axis=0, keepdims=True)
        vsum[t] = jnp.sum(dv_acc[...], axis=0, keepdims=True)
        target[:, :, :first] = block_rows(mxu(act_t[:, :, rows : 2 * rows].reshape(width, rows), dq, NN).astype(BF16))
        both = jnp.concatenate([dk, dv], axis=1)
        target[:, :, first:third] = block_rows(mxu(act_t[...].reshape(width, 3 * rows), both, NN).astype(BF16))
        if remote:
            if not mine:
                over[1, s].start()
            else:
                over[1, s - 1].wait_recv()
        tick()
        lanes = weights[:, first:third]
        for part in range(3):
            here = slice(part * rows, (part + 1) * rows)
            value = mxu(both[here], lanes, NT)
            if part == 1:
                value = value + mxu(dq, weights[:, :first], NT)
            if s == 0:
                grad_one[here, :] = value
            else:
                grad_one[here, :] += value
        if not remote:
            copy = pltpu.make_async_copy(stage_a, rest_hbm[1].at[t], out_sem.at[0])
            copy.start()
            copy.wait()
        tick()
    output_store.wait()
    low_ref[...] = grad_one[:rows, :].astype(BF16)
    two[...] = grad_one[2 * rows :, :].astype(BF16)
    if remote:
        finish_halo = exchange_halo(low_ref, two, halo_land, halo_send, halo_recv, low_ref, two)
    gain_sum = jnp.zeros((1, width), F32)
    for copy in halo_loads:
        copy.wait()
    for part, source in enumerate((cot, tok, wa.at[groups % 2, pl.ds(0, rows)])):
        normed, rate = norm_parts(source[...].astype(F32))
        gain_sum = gain_sum + jnp.sum(grad_one[part * rows : (part + 1) * rows, :] * normed, axis=0, keepdims=True)
    sums[0:1, :] = gain_sum
    sums[1:2, :] = jnp.sum(grad_one[...], axis=0, keepdims=True)
    for t in range(groups):
        sums[2:3, t * head_width : (t + 1) * head_width] = qsum[t]
        sums[3:4, t * head_width : (t + 1) * head_width] = vsum[t]
    pack_vectors(sums, gunits, gvec, SPLIT)
    if not remote:
        copies = [
            pltpu.make_async_copy(low_ref, rest_hbm[2].at[0], out_sem.at[0]),
            pltpu.make_async_copy(two, rest_hbm[2].at[1], out_sem.at[1]),
            pltpu.make_async_copy(grad_one.at[pl.ds(rows, rows)], result_hbm, out_sem.at[2]),
            pltpu.make_async_copy(mid, back_hbm, out_sem.at[3]),
            pltpu.make_async_copy(gvec, rest_hbm[3], out_sem.at[4]),
        ]
        for copy in copies:
            copy.start()
        for copy in copies:
            copy.wait()
        return
    acc_v[0] = gvec[...]
    acc_v[1] = gvec[...]
    over_v = [
        pltpu.make_async_remote_copy(
            gvec, core_v.at[side], core_send.at[2, side], core_recv.at[2, side], device_id=sibling, device_id_type=MESH_ID
        )
        for side in range(2)
    ]
    for copy in over_v:
        copy.start()
    for copy in over_v:
        copy.wait_recv()
    tick()
    finish_halo()
    from_left = jnp.where(tensor > 0, halo_land[0].astype(F32), 0.0)
    from_right = jnp.where(tensor < 3, halo_land[1].astype(F32), 0.0)
    normed, rate = norm_parts(tok[...].astype(F32))
    total = grad_one[rows : 2 * rows, :] + from_left + from_right
    out_acc[...] = mid[...] + norm_pull(total, normed, rate, rows_ref[0:1, :])
    result_store = pltpu.make_async_copy(out_acc, result_hbm, out_sem.at[2])
    result_store.start()
    tick()
    for end in ends:
        end()
    over[0, 2].wait_send()
    over[1, 2].wait_send()
    for copy in over_v:
        copy.wait_send()
    result_store.wait()


def backward_rows(remote, tok, halo, cot, middle, act_two, act_t, wm, wa, rows_ref, units_ref, q, k, v, ctx, lse, segk_row, segk_col):
    rows, width = tok.shape
    groups, wide = wm.shape[0], wm.shape[-1]
    narrow = wa.shape[2]
    head_width = narrow // 4
    shape = jax.ShapeDtypeStruct
    vmem = pltpu.VMEM
    dma = lambda *dims: pltpu.SemaphoreType.DMA(dims)
    in_specs = [VMEM_SPEC, HBM_SPEC] + [HBM_SPEC] * 6 + [VMEM_SPEC] * 2 + [HBM_SPEC] * 4 + [VMEM_SPEC] * 3
    piece = width // SPLIT
    if remote:
        out_shape = (
            shape((rows, width), BF16),
            shape((piece, wide), F32),
            shape((piece, narrow), F32),
            shape((16, 128), F32),
            shape((rows, width), F32),
        )
        out_specs = (HBM_SPEC, VMEM_SPEC, VMEM_SPEC, VMEM_SPEC, HBM_SPEC)
    else:
        out_shape = (
            shape((rows, width), BF16),
            shape((groups, SPLIT, piece, wide), BF16),
            shape((groups, SPLIT, piece, narrow), BF16),
            shape((SPLIT, 16, 128), BF16),
            shape((2, rows, width), BF16),
            shape((rows, width), F32),
            shape((rows, width), F32),
        )
        out_specs = (HBM_SPEC,) * 7
    scratch = [
        vmem((rows, width), BF16),
        vmem((rows, width), BF16),
        vmem((width, rows), BF16),
        vmem((width, rows), BF16),
        vmem((rows, width), F32),
        vmem((rows, width), F32),
        vmem((rows, width), F32),
        vmem((rows, width), BF16),
        vmem((2, SPLIT, piece, wide), BF16),
        vmem((2, width, narrow), BF16),
        vmem((rows, head_width), BF16),
        vmem((3 * rows, head_width), BF16),
        vmem((3 * rows, head_width), BF16),
        vmem((rows, head_width), BF16),
        vmem((SPLIT, piece, wide), BF16),
        vmem((3 * rows, width), F32),
        vmem((3 * rows, head_width), F32),
        vmem((3 * rows, head_width), F32),
        vmem((head_width, rows), F32),
        vmem((head_width, 3 * rows), BF16),
        vmem((rows, head_width), BF16),
        vmem((VEC_ROWS, width), F32),
        vmem(units_ref.shape, F32),
        vmem((groups, 1, head_width), F32),
        vmem((groups, 1, head_width), F32),
        vmem((SPLIT, 16, 128), BF16),
        dma(3),
        dma(2),
        dma(2),
        dma(4),
        dma(5),
    ]
    params = dict(vmem_limit_bytes=VMEM_LIMIT)
    if remote:
        n = len(REDUCE_PARTS)
        sizes = ((piece, wide), (piece, narrow), (16, 128))
        slots = [4 * len(land_slots(p[0], 4)) for p in REDUCE_PARTS]
        scratch += [vmem((2, SPLIT) + size, BF16) for size in sizes]
        scratch += [vmem((2, SPLIT) + size, BF16) for size in sizes]
        scratch += [vmem((2, rows, width), BF16)]
        scratch += [vmem((slots[i], p[3], sizes[p[1]][1]), BF16) for i, p in enumerate(REDUCE_PARTS)]
        scratch += [dma(3, 2), dma(3, 2), dma(n, 4, 4), dma(n, max(slots)), dma(4), dma(2)]
        params.update(collective_id=1, has_side_effects=True)

    def kernel(*refs):
        ins, outs, rest = refs[:17], refs[17 : 17 + len(out_shape)], refs[17 + len(out_shape) :]
        if remote:
            outs = (outs[0], outs[1], outs[2], outs[3], outs[4], None, None)
        else:
            outs = (outs[0], None, None, None, outs[5], (outs[1], outs[2], outs[4], outs[3]), outs[6])
        backward_kernel(remote, *ins, *outs, *rest)

    return pl.pallas_call(
        kernel,
        out_shape=out_shape,
        in_specs=in_specs,
        out_specs=out_specs,
        scratch_shapes=scratch,
        compiler_params=pltpu.CompilerParams(**params),
        name="backward_rows",
    )(tok, halo, cot, middle, act_two, act_t.reshape(SPLIT, piece, 3 * rows), wm, wa, rows_ref, units_ref, q, k, v, ctx, lse, segk_row, segk_col)


CHUNKS = 4


def finish_kernel(piece, out_in, grad_in, sum_m, sum_a, sum_v, out, grad, *rest):
    *results, out_s, grad_s, m_s, a_s, v_s, sem, back_sem = rest
    small = [pltpu.make_async_copy(source, target, sem.at[i]) for i, (source, target) in enumerate(((sum_m, m_s), (sum_a, a_s), (sum_v, v_s)))]
    rows = out.shape[0] // CHUNKS
    loads, stores = [], []
    for i in range(CHUNKS):
        here = pl.ds(i * rows, rows)
        for j, (source, held, target) in enumerate(((grad_in, grad_s, grad), (out_in, out_s, out))):
            loads.append(pltpu.make_async_copy(source.at[here], held.at[here], sem.at[3 + 2 * i + j]))
            stores.append(pltpu.make_async_copy(held.at[here], target.at[here], back_sem.at[2 * i + j]))
    for copy in small + loads:
        copy.start()
    for copy in small:
        copy.wait()
    for load, store in zip(loads, stores):
        load.wait()
        store.start()
    sum_m, sum_a, sum_v = m_s, a_s, v_s
    g_q, g_k, g_v, g_o, g_in, g_back, *lines = results
    head_width, units = g_q.shape[1], g_in.shape[1]
    total = sum_a[...]
    g_q[...] = total[:, :head_width]
    g_k[...] = total[:, head_width : 2 * head_width]
    g_v[...] = total[:, 2 * head_width : 3 * head_width]
    g_o[...] = total[:, 3 * head_width :].T
    g_in[...] = sum_m[:, :units]
    g_back[...] = sum_m[:, units:]
    for i in range(SHIFTS):
        lines[i][...] = sum_v[i : i + 1, :piece]
    for row in range(lines[SHIFTS].shape[0] // 128):
        lines[SHIFTS][row * 128 : (row + 1) * 128] = sum_v[SHIFTS + row, :]
    for copy in stores:
        copy.wait()


def finish_rows(output, grad_tokens, sum_m, sum_a, sum_v, unit_piece):
    piece, wide = sum_m.shape
    narrow = sum_a.shape[1]
    line = lambda n: jax.ShapeDtypeStruct((1, n), F32)
    shape = lambda *dims: jax.ShapeDtypeStruct(dims, F32)
    quarter = shape(piece, narrow // 4)
    half = shape(piece, wide // 2)
    return pl.pallas_call(
        functools.partial(finish_kernel, piece),
        out_shape=(
            jax.ShapeDtypeStruct(output.shape, output.dtype),
            jax.ShapeDtypeStruct(grad_tokens.shape, grad_tokens.dtype),
            quarter,
            quarter,
            quarter,
            shape(narrow // 4, piece),
            half,
            half,
        )
        + (line(piece),) * SHIFTS
        + (shape(unit_piece),),
        in_specs=[pl.BlockSpec(memory_space=pltpu.HBM)] * 5,
        out_specs=(pl.BlockSpec(memory_space=pltpu.HBM),) * 2 + (VMEM_SPEC,) * (7 + SHIFTS),
        scratch_shapes=[
            pltpu.VMEM(output.shape, output.dtype),
            pltpu.VMEM(grad_tokens.shape, F32),
            pltpu.VMEM(sum_m.shape, F32),
            pltpu.VMEM(sum_a.shape, F32),
            pltpu.VMEM(sum_v.shape, F32),
            pltpu.SemaphoreType.DMA((3 + 2 * CHUNKS,)),
            pltpu.SemaphoreType.DMA((2 * CHUNKS,)),
        ],
        compiler_params=pltpu.CompilerParams(vmem_limit_bytes=VMEM_LIMIT),
        name="finish_rows",
    )(output, grad_tokens, sum_m, sum_a, sum_v)


def per_device(by_kernel, *args):
    (
        tokens,
        cotangent,
        segment_ids,
        ln1_gain,
        ln1_bias,
        w_query,
        query_bias,
        w_key,
        w_value,
        value_bias,
        w_out,
        out_bias,
        ln2_gain,
        ln2_bias,
        w_in,
        in_bias,
        w_back,
        back_bias,
    ) = args
    rows, width = tokens.shape
    n_dp, n_tensor = lax.axis_size("dp"), lax.axis_size("tensor")
    index = lax.axis_index("tensor")
    head_width = w_query.shape[1]
    units = w_in.shape[1]
    piece = ln1_gain.shape[0]
    unit_piece = in_bias.shape[0]

    vectors = (ln1_gain, ln1_bias, query_bias, value_bias, out_bias, ln2_gain, ln2_bias, back_bias)
    if by_kernel:
        lines = [vector.reshape(1, piece) for vector in vectors]
        sources = (w_in, w_back.T, w_query, w_key, w_value, w_out, *lines, in_bias.reshape(-1, 128))
        full_mlp, full_att, halo, *saved = forward_rows(True, tokens, segment_ids, units, *sources)
    else:
        shard_mlp = jnp.concatenate([w_in, w_back.T], axis=1)
        shard_att = jnp.concatenate([w_query, w_key, w_value, w_out.T], axis=1)
        edge = jnp.full((rows,), -1, jnp.int32)
        segs = jnp.concatenate([edge, segment_ids[0], edge])
        segs = lax.dynamic_slice_in_dim(segs, index * rows, 3 * rows)[None, :]
        shard_vec = jnp.concatenate([jnp.stack(vectors).reshape(-1), in_bias])
        full_mlp, full_att, full_vec, halo = gather_by_ops((shard_mlp, shard_att, shard_vec), tokens)
        flat = full_vec[0]
        rows8 = jnp.swapaxes(flat[:, : 8 * piece].reshape(n_dp, 8, piece), 0, 1).reshape(8, SPLIT, width // SPLIT)
        rows8 = jnp.pad(jnp.swapaxes(rows8, 0, 1), ((0, 0), (0, 0), (0, 128 - width // SPLIT)))
        unit_rows = flat[:, 8 * piece :].reshape(SPLIT, -1, 128)
        full_vec = jnp.concatenate([rows8, unit_rows], axis=1)
        full_vec = jnp.pad(full_vec, ((0, 0), (0, 16 - full_vec.shape[1]), (0, 0)))
        full_mlp = full_mlp.reshape(n_tensor, SPLIT, width // SPLIT, 2 * units)
        full_att = full_att.reshape(n_tensor, SPLIT, width // SPLIT, 4 * head_width)
        saved = forward_rows(False, tokens, segs, units, halo, full_att, full_vec)
    rows_vec, units_vec, segk_row, segk_col, lse, act_t, query, keys, values, context, middle, act_two = saved
    full_att = full_att.reshape(n_tensor, width, 4 * head_width)
    results = backward_rows(
        by_kernel, tokens, halo, cotangent, middle, act_two, act_t, full_mlp, full_att, rows_vec, units_vec, query, keys, values,
        context, lse, segk_row, segk_col,
    )
    if by_kernel:
        output, sum_mlp, sum_att, sum_vec, grad_tokens = results
        output, grad_tokens, g_wq, g_wk, g_wv, g_wo, g_win, g_wback, *vec = finish_rows(
            output, grad_tokens, sum_mlp, sum_att, sum_vec, unit_piece
        )
        vec = [line.reshape(-1) for line in vec]
    else:
        output, grad_mlp, grad_att, grad_vec, halo_rows, grad_own, grad_middle = results
        split = lambda array: array.reshape(n_tensor, n_dp, width // n_dp, array.shape[-1])
        rows8 = jnp.swapaxes(grad_vec[:, :8, : width // 8], 0, 1).reshape(8, n_dp, piece)
        unit_flat = grad_vec[:, 8 : 8 + unit_piece * n_dp // SPLIT // 128].reshape(n_dp, unit_piece)
        flat = jnp.concatenate([jnp.swapaxes(rows8, 0, 1).reshape(n_dp, 8 * piece), unit_flat], axis=1)
        flat = jnp.broadcast_to(flat[None], (n_tensor,) + flat.shape)
        sum_mlp, sum_att, sum_vec, halo_back = reduce_by_ops((split(grad_mlp), split(grad_att), flat), halo_rows)
        vec = [sum_vec[i * piece : (i + 1) * piece] for i in range(8)] + [sum_vec[8 * piece :]]
        from_left = jnp.where(index > 0, halo_back[0].astype(F32), 0.0)
        from_right = jnp.where(index < n_tensor - 1, halo_back[1].astype(F32), 0.0)
        norm_one, rate_one = norm_parts(tokens.astype(F32))
        grad_tokens = grad_middle + norm_pull(grad_own + from_left + from_right, norm_one, rate_one, rows_vec[0:1])
        g_wq, g_wk, g_wv = (sum_att[:, i * head_width : (i + 1) * head_width] for i in range(3))
        g_wo = sum_att[:, 3 * head_width :].T
        g_win, g_wback = sum_mlp[:, :units], sum_mlp[:, units:]
    g_ln1_gain, g_ln1_bias, g_q, g_v, g_o, g_ln2_gain, g_ln2_bias, g_b, g_i = vec
    return (
        output,
        grad_tokens,
        g_ln1_gain,
        g_ln1_bias,
        g_wq,
        g_q,
        g_wk,
        g_wv,
        g_v,
        g_wo,
        g_o,
        g_ln2_gain,
        g_ln2_bias,
        g_win,
        g_i,
        g_wback.T,
        g_b,
    )


def solution(mesh):
    by_kernel = mesh.shape["dp"] == 8 and mesh.shape["tensor"] == 4
    rows = P(("dp", "tensor"), None)
    line, first, second = P("dp"), P("dp", "tensor"), P("tensor", "dp")
    return jax.shard_map(
        functools.partial(per_device, by_kernel),
        mesh=mesh,
        in_specs=(rows, rows, P("dp", None), line, line, first, line, first, first, line, second, line, line, line, first, line, second, line),
        out_specs=(rows, rows, line, line, first, line, first, first, line, second, line, line, line, first, line, second, line),
        check_vma=False,
    )
```
